32 devices in a mesh: fsdp: 16 (over z, x, core), ctx: 2 (over y).
Axes of the slice: x: 2, y: 2, z: 4, core: 2. Of those that a mesh axis runs over, the one named last changes fastest.
Arguments:
- tokens: bfloat16 [16, 1024, 768], P('fsdp', 'ctx'), may hold values from -6 to 6
- cotangent: bfloat16 [16, 1024, 768], P('fsdp', 'ctx'), may hold values from -6 to 6
- kept_blocks: int32 [16, 12, 8], P('fsdp'), may hold values from 0 to 7, as said below
- picture_starts: int32 [16, 2], P('fsdp'), may hold values from 0 to 768, as said below
- qkv_weight: bfloat16 [2, 768, 2304], P(None, 'fsdp', 'ctx'), may hold values from -0.21875 to 0.21875
- score_weight: bfloat16 [2, 768, 12], P(None, 'fsdp'), may hold values from -0.21875 to 0.21875
- out_weight: bfloat16 [2, 768, 768], P(None, 'fsdp', 'ctx'), may hold values from -1.5 to 1.5
- up_weight: bfloat16 [2, 768, 3072], P(None, 'fsdp', 'ctx'), may hold values from -0.21875 to 0.21875
- down_weight: bfloat16 [2, 3072, 768], P(None, 'fsdp', 'ctx'), may hold values from -0.109375 to 0.109375
- norm_gain: bfloat16 [2, 2, 768], P(None, None, 'fsdp'), may hold values from 0.5 to 1.5
- norm_bias: bfloat16 [2, 2, 768], P(None, None, 'fsdp'), may hold values from -4 to 4
Outputs:
- block_output: float32 [16, 1024, 768], P('fsdp', 'ctx')
- token_grad: float32 [16, 1024, 768], P('fsdp', 'ctx')
- qkv_grad: float32 [2, 768, 2304], P(None, 'fsdp', 'ctx')
- score_grad: float32 [2, 768, 12], P(None, 'fsdp')
- out_grad: float32 [2, 768, 768], P(None, 'fsdp', 'ctx')
- up_grad: float32 [2, 768, 3072], P(None, 'fsdp', 'ctx')
- down_grad: float32 [2, 3072, 768], P(None, 'fsdp', 'ctx')
- gain_grad: float32 [2, 2, 768], P(None, None, 'fsdp')
- bias_grad: float32 [2, 2, 768], P(None, None, 'fsdp')
The draws below stay inside these ranges and needn't reach their ends.
Inputs may be any that keep to these rules, and one draw needn't show every extreme that they name: `kept_blocks`: the key block of 128 keys kept by a query block is never later than that query block. `picture_starts`: each start is a multiple of 128; a piece of 256 tokens lies inside its sequence; pieces may intersect.
All inputs are finite; a program needn't handle non-finite values.
Results may differ from the reference program's by a relative error of at most 0.018.
Values may be sent and summed in bfloat16 or wider, within the bound.
No kernel may reach another device: no remote copies, remote signals or barrier semaphores. Data moves between devices by JAX's collectives and lax.ppermute only.
A program may use at most 256 MiB of HBM per device.

```python
import math
import jax
import jax.numpy as jnp
from jax import lax

D = 768
FF = 3072
HEADS = 12
HEAD_DIM = 64
LAYERS = 2
SEQ_LEN = 1024
BLK = 128
WINDOW = 64
PIC_LEN = 256
PICS = 2
SEQS = 16


def draw_kept_blocks(key, part):
    limit = jnp.arange(SEQ_LEN // BLK, dtype=jnp.int32) + 1
    return jax.random.randint(key, (SEQS, HEADS, SEQ_LEN // BLK), 0, limit[None, None, :], dtype=jnp.int32)


def draw_picture_starts(key, part):
    slots = jax.random.randint(key, (SEQS, PICS), 0, (SEQ_LEN - PIC_LEN) // BLK + 1, dtype=jnp.int32)
    return slots * BLK


def level_of(rng, extent, shards, least, high):
    def one(dim, blocks):
        steps = jax.random.uniform(jax.random.fold_in(jax.random.fold_in(rng, 6), dim), (blocks,), jnp.float32, least / len(shards), high / len(shards))
        return jnp.repeat(jnp.exp(steps), extent[dim] // blocks).reshape((-1,) + (1,) * (len(extent) - dim - 1))

    level = one(*shards[0])
    for cut in shards[1:]:
        level = level * one(*cut)
    return level


def centred(key, extent, deviation, most, cuts=(), held_as=jnp.bfloat16):
    values = jax.random.normal(key, extent, jnp.float32) * deviation
    if len(cuts) > 0:
        values = level_of(key, extent, cuts, -0.22, 0.18) * values
    return jnp.clip(values, min=-most, max=most).astype(held_as)


def setup_inputs(seed: int = 0) -> dict:
    arg_keys = jax.random.split(jax.random.key(seed), 12)
    tokens = centred(arg_keys[0], (SEQS, SEQ_LEN, D), 1.0, 6.0, ((0, 16), (1, 2)))
    cotangent = centred(arg_keys[1], (SEQS, SEQ_LEN, D), 1.0, 6.0, ((0, 16), (1, 2)))
    kept_blocks = draw_kept_blocks(jax.random.fold_in(arg_keys[11], 71), 0)
    picture_starts = draw_picture_starts(jax.random.fold_in(arg_keys[11], 71), 0)
    qkv_weight = centred(arg_keys[4], (LAYERS, D, 3 * D), D ** -0.5, 0.21875, ((1, 16), (2, 2)))
    score_weight = centred(arg_keys[5], (LAYERS, D, HEADS), D ** -0.5, 0.21875, ((1, 16),))
    out_weight = centred(arg_keys[6], (LAYERS, D, D), (D // 48) ** -0.5, 1.5, ((1, 16), (2, 2)))
    up_weight = centred(arg_keys[7], (LAYERS, D, FF), D ** -0.5, 0.21875, ((1, 16), (2, 2)))
    down_weight = centred(arg_keys[8], (LAYERS, FF, D), FF ** -0.5, 0.109375, ((1, 16), (2, 2)))
    norm_gain = jnp.clip(1.0 + 0.1 * jax.random.normal(arg_keys[9], (LAYERS, 2, D), jnp.float32), 0.5, 1.5).astype(jnp.bfloat16)
    norm_bias = centred(arg_keys[10], (LAYERS, 2, D), 0.3, 4.0, ((2, 16),))
    return dict(tokens=tokens, cotangent=cotangent, kept_blocks=kept_blocks, picture_starts=picture_starts, qkv_weight=qkv_weight, score_weight=score_weight, out_weight=out_weight, up_weight=up_weight, down_weight=down_weight, norm_gain=norm_gain, norm_bias=norm_bias)


@jax.custom_vjp
def low(v):
    return lax.optimization_barrier(v.astype(jnp.bfloat16)).astype(jnp.float32)

@jax.custom_vjp
def low_back(v):
    return v

def low_keep(v):
    return (low(v), None)

def low_pass(kept, grad):
    return (grad,)

def back_keep(v):
    return (v, None)

def back_low(kept, grad):
    return (low(grad),)
low.defvjp(low_keep, low_pass)
low_back.defvjp(back_keep, back_low)
highest = lax.Precision.HIGHEST

def both_ways(value):
    return low(low_back(value))

def normalize(residual, gain, bias):
    mean_value = lax.optimization_barrier(jnp.mean(residual, axis=-1, keepdims=True))
    centered = residual - mean_value
    variance = lax.optimization_barrier(jnp.mean(centered * centered, axis=-1, keepdims=True))
    return centered * lax.rsqrt(variance + 1e-05) * gain + bias

def gelu_tanh(value):
    return jax.nn.gelu(value, approximate=True)

def log_sigmoid(value):
    return -(jnp.maximum(-value, 0.0) + jnp.log1p(jnp.exp(-jnp.abs(value))))

def head_attend(items, base, causal, key_block):
    queries, keys, values, scores, kept = items
    logits = jnp.einsum('gqd,gkd->gqk', queries, keys, precision=highest) * HEAD_DIM ** (-0.5)
    logits = low_back(logits + log_sigmoid(scores)[:, None, :])
    allowed = base | causal[None] & (key_block[None, None, :] == kept[:, :, None])
    logits = jnp.where(allowed, logits, -1e+30)
    largest = lax.optimization_barrier(jnp.max(logits, axis=-1, keepdims=True))
    weights = jnp.exp(logits - largest)
    probs = low(weights / lax.optimization_barrier(jnp.sum(weights, axis=-1, keepdims=True)))
    return jnp.einsum('gqk,gkd->gqd', probs, values, precision=highest)

def layer_forward(residual, params, kept, starts):
    qkv_w, score_w, out_w, up_w, down_w, gain, bias = params
    group = residual.shape[0]
    hidden = low(normalize(residual, gain[0], bias[0]))
    qkv = both_ways(jnp.matmul(hidden, qkv_w, precision=highest))
    scores = both_ways(jnp.matmul(hidden, score_w, precision=highest))

    def split_heads(tensor):
        return jnp.moveaxis(tensor.reshape(group, SEQ_LEN, HEADS, HEAD_DIM), 2, 0)
    queries = split_heads(qkv[..., :D])
    keys = split_heads(qkv[..., D:2 * D])
    values = split_heads(qkv[..., 2 * D:])
    positions = jnp.arange(SEQ_LEN, dtype=jnp.int32)
    causal = positions[None, :] <= positions[:, None]
    local = causal & (positions[:, None] - positions[None, :] < WINDOW)
    inside = (positions[None, None, :] >= starts[:, :, None]) & (positions[None, None, :] < starts[:, :, None] + PIC_LEN)
    picture = jnp.any(inside[:, :, :, None] & inside[:, :, None, :], axis=1)
    base = local[None] | picture
    kept_rows = jnp.moveaxis(jnp.repeat(kept, BLK, axis=2), 1, 0)
    key_block = positions // BLK
    heads = lax.map(jax.checkpoint(lambda items: head_attend(items, base, causal, key_block)), (queries, keys, values, jnp.moveaxis(scores, 2, 0), kept_rows))
    mixed = both_ways(jnp.moveaxis(heads, 0, 2).reshape(group, SEQ_LEN, D))
    after_attn = residual + low_back(jnp.matmul(mixed, out_w, precision=highest))
    hidden2 = low(normalize(after_attn, gain[1], bias[1]))
    up_part = low_back(jnp.matmul(hidden2, up_w, precision=highest))
    active = low(gelu_tanh(up_part))
    return after_attn + low_back(jnp.matmul(active, down_w, precision=highest))

def reference(tokens, cotangent, kept_blocks, picture_starts, qkv_weight, score_weight, out_weight, up_weight, down_weight, norm_gain, norm_bias):
    group = math.gcd(SEQS, 4)
    count = SEQS // group

    def regroup(array):
        return array.reshape((count, group) + array.shape[1:])
    params = tuple((w.astype(jnp.float32) for w in (qkv_weight, score_weight, out_weight, up_weight, down_weight, norm_gain, norm_bias)))
    kept = regroup(kept_blocks)
    starts = regroup(picture_starts)

    def forward(residual, weights):

        def run(items):
            part_residual, part_kept, part_starts = items
            for layer_index in range(LAYERS):
                part_residual = layer_forward(part_residual, tuple((w[layer_index] for w in weights)), part_kept, part_starts)
            return part_residual
        return lax.map(jax.checkpoint(run), (residual, kept, starts))
    result, pullback = jax.vjp(forward, regroup(tokens.astype(jnp.float32)), params)
    token_grad, weight_grads = pullback(regroup(cotangent.astype(jnp.float32)))
    shape = (SEQS, SEQ_LEN, D)
    return (result.reshape(shape), token_grad.reshape(shape), weight_grads[0], weight_grads[1], weight_grads[2], weight_grads[3], weight_grads[4], weight_grads[5], weight_grads[6])
```

```python
import math
from functools import partial

import jax
import jax.numpy as jnp
from jax import lax
from jax.experimental import pallas as pl
from jax.experimental.pallas import tpu as pltpu
from jax.sharding import PartitionSpec as P

HEADS = 12
HEAD_DIM = 64
LAYERS = 2
BLK = 128
WINDOW = 64
PIC_LEN = 256


def normalize(residual, gain, bias):
    mean_value = jnp.mean(residual, axis=-1, keepdims=True)
    centered = residual - mean_value
    variance = jnp.mean(centered * centered, axis=-1, keepdims=True)
    return centered * lax.rsqrt(variance + 1e-05) * gain + bias


def gelu_tanh(value):
    return jax.nn.gelu(value, approximate=True)


def log_sigmoid(value):
    return -(jnp.maximum(-value, 0.0) + jnp.log1p(jnp.exp(-jnp.abs(value))))


def split_heads(tensor):
    return jnp.moveaxis(tensor.reshape(tensor.shape[:-1] + (HEADS, HEAD_DIM)), 2, 0)


def join_heads(tensor):
    moved = jnp.moveaxis(tensor, 0, 2)
    return moved.reshape(moved.shape[:2] + (HEADS * HEAD_DIM,))


def masked_logits(queries, keys, scores, kept, base, causal, key_block):
    logits = jnp.einsum(
        "sqd,skd->sqk", queries, keys, preferred_element_type=jnp.float32
    ) * HEAD_DIM ** (-0.5)
    logits = logits + log_sigmoid(scores.astype(jnp.float32))[:, None, :]
    allowed = base | causal[None] & (key_block[None, None, :] == kept[:, :, None])
    return (logits, allowed)


def attend_head(items, base, causal, key_block):
    queries, keys, values, scores, kept = items
    logits, allowed = masked_logits(queries, keys, scores, kept, base, causal, key_block)
    logits = jnp.where(allowed, logits, -1e30)
    largest = jnp.max(logits, axis=-1, keepdims=True)
    weights = jnp.exp(logits - largest)
    totals = jnp.sum(weights, axis=-1, keepdims=True)
    probs_low = (weights / totals).astype(jnp.bfloat16)
    outputs = jnp.einsum("sqk,skd->sqd", probs_low, values, preferred_element_type=jnp.float32)
    return (outputs, (largest + jnp.log(totals))[..., 0])


def query_side_grads(items, base, causal, key_block):
    queries, keys, values, scores, kept, grad_out, log_totals = items
    logits, allowed = masked_logits(queries, keys, scores, kept, base, causal, key_block)
    probs = jnp.where(allowed, jnp.exp(logits - log_totals[..., None]), 0.0)
    grad_probs = jnp.einsum("sqd,skd->sqk", grad_out, values, preferred_element_type=jnp.float32)
    inner = jnp.sum(probs * grad_probs, axis=-1, keepdims=True)
    grad_logits = (probs * (grad_probs - inner)).astype(jnp.bfloat16)
    grad_queries = jnp.einsum(
        "sqk,skd->sqd", grad_logits, keys, preferred_element_type=jnp.float32
    ) * HEAD_DIM ** (-0.5)
    return (grad_queries, inner[..., 0])


def key_side_grads(items, base, causal, key_block):
    queries, keys, values, scores, kept, grad_out, log_totals, inner = items
    logits, allowed = masked_logits(queries, keys, scores, kept, base, causal, key_block)
    probs = jnp.where(allowed, jnp.exp(logits - log_totals[..., None]), 0.0)
    grad_probs = jnp.einsum("sqd,skd->sqk", grad_out, values, preferred_element_type=jnp.float32)
    grad_logits = (probs * (grad_probs - inner[..., None])).astype(jnp.bfloat16)
    grad_values = jnp.einsum(
        "sqk,sqd->skd", probs.astype(jnp.bfloat16), grad_out, preferred_element_type=jnp.float32
    )
    grad_keys = jnp.einsum(
        "sqk,sqd->skd", grad_logits, queries, preferred_element_type=jnp.float32
    ) * HEAD_DIM ** (-0.5)
    grad_scores = jnp.sum(grad_logits.astype(jnp.float32), axis=1) * jax.nn.sigmoid(
        -scores.astype(jnp.float32)
    )
    return (grad_keys, grad_values, grad_scores)


def build_masks(kept_blocks, picture_starts, query_start, query_len, key_start, key_len):
    query_pos = query_start + jnp.arange(query_len, dtype=jnp.int32)
    key_pos = key_start + jnp.arange(key_len, dtype=jnp.int32)
    causal = key_pos[None, :] <= query_pos[:, None]
    local = causal & (query_pos[:, None] - key_pos[None, :] < WINDOW)
    starts = picture_starts[:, :, None]
    inside_query = (query_pos[None, None, :] >= starts) & (
        query_pos[None, None, :] < starts + PIC_LEN
    )
    inside_key = (key_pos[None, None, :] >= starts) & (key_pos[None, None, :] < starts + PIC_LEN)
    picture = jnp.any(inside_query[:, :, :, None] & inside_key[:, :, None, :], axis=1)
    base = local[None] | picture
    kept_all = jnp.repeat(kept_blocks, BLK, axis=2)
    kept_rows = jnp.moveaxis(lax.dynamic_slice_in_dim(kept_all, query_start, query_len, 2), 1, 0)
    return (base, causal, key_pos // BLK, kept_rows)


def forward_layer(residual, weights, masks):
    qkv_w, score_w, out_w, up_w, down_w, gain, bias = weights
    base, causal, key_block, kept_rows = masks
    gains = gain.astype(jnp.float32)
    biases = bias.astype(jnp.float32)
    hidden = normalize(residual, gains[0], biases[0]).astype(jnp.bfloat16)
    qkv = jnp.dot(hidden, qkv_w, preferred_element_type=jnp.float32).astype(jnp.bfloat16)
    scores = jnp.dot(hidden, score_w, preferred_element_type=jnp.float32).astype(jnp.bfloat16)
    queries, keys, values = jnp.split(qkv, 3, axis=-1)
    all_keys, all_values, all_scores = (
        lax.all_gather(keys, "ctx", axis=1, tiled=True),
        lax.all_gather(values, "ctx", axis=1, tiled=True),
        lax.all_gather(scores, "ctx", axis=1, tiled=True),
    )
    head_items = (
        split_heads(queries),
        split_heads(all_keys),
        split_heads(all_values),
        jnp.moveaxis(all_scores, 2, 0),
        kept_rows,
    )
    heads, log_totals = lax.map(
        partial(attend_head, base=base, causal=causal, key_block=key_block), head_items
    )
    mixed = join_heads(heads).astype(jnp.bfloat16)
    after_attn = residual + jnp.dot(mixed, out_w, preferred_element_type=jnp.float32)
    hidden2 = normalize(after_attn, gains[1], biases[1]).astype(jnp.bfloat16)
    up_part = jnp.dot(hidden2, up_w, preferred_element_type=jnp.float32)
    active = gelu_tanh(up_part).astype(jnp.bfloat16)
    result = after_attn + jnp.dot(active, down_w, preferred_element_type=jnp.float32)
    own_side = (queries, keys, values, scores)
    saved = (
        residual,
        hidden,
        head_items,
        log_totals,
        mixed,
        after_attn,
        hidden2,
        up_part,
        active,
        own_side,
    )
    return (result, saved)


def backward_layer(grad, saved, weights, masks, key_masks):
    qkv_w, score_w, out_w, up_w, down_w, gain, bias = weights
    base, causal, key_block, kept_rows = masks
    (
        residual,
        hidden,
        head_items,
        log_totals,
        mixed,
        after_attn,
        hidden2,
        up_part,
        active,
        own_side,
    ) = saved
    gains = gain.astype(jnp.float32)
    biases = bias.astype(jnp.float32)
    grad_down = grad.astype(jnp.bfloat16)
    grad_active = jnp.einsum("sto,io->sti", grad_down, down_w, preferred_element_type=jnp.float32)
    grad_up = jax.vjp(gelu_tanh, up_part)[1](grad_active)[0].astype(jnp.bfloat16)
    grad_hidden2 = jnp.einsum("stf,df->std", grad_up, up_w, preferred_element_type=jnp.float32)
    late_back = jax.vjp(normalize, after_attn, gains[1], biases[1])[1]
    grad_norm_late, gain_late, bias_late = late_back(grad_hidden2)
    grad_after = grad + grad_norm_late
    grad_attn = grad_after.astype(jnp.bfloat16)
    grad_mixed = jnp.einsum(
        "ste,de->std", grad_attn, out_w, preferred_element_type=jnp.float32
    ).astype(jnp.bfloat16)
    grad_items = head_items + (split_heads(grad_mixed), log_totals)
    grad_queries, inner = lax.map(
        partial(query_side_grads, base=base, causal=causal, key_block=key_block), grad_items
    )
    own_queries, own_keys, own_values, own_scores = own_side
    all_queries, all_grad_mixed = (
        lax.all_gather(own_queries, "ctx", axis=1, tiled=True),
        lax.all_gather(grad_mixed, "ctx", axis=1, tiled=True),
    )
    all_totals, all_inner = (
        lax.all_gather(log_totals, "ctx", axis=2, tiled=True),
        lax.all_gather(inner, "ctx", axis=2, tiled=True),
    )
    key_base, key_causal, key_block_own, kept_all_rows = key_masks
    key_items = (
        split_heads(all_queries),
        split_heads(own_keys),
        split_heads(own_values),
        jnp.moveaxis(own_scores, 2, 0),
        kept_all_rows,
        split_heads(all_grad_mixed),
        all_totals,
        all_inner,
    )
    grad_keys, grad_values, grad_scores = lax.map(
        partial(key_side_grads, base=key_base, causal=key_causal, key_block=key_block_own),
        key_items,
    )
    key_part = join_heads(grad_keys)
    value_part = join_heads(grad_values)
    score_part = jnp.moveaxis(grad_scores, 0, 2)
    grad_qkv = jnp.concatenate([join_heads(grad_queries), key_part, value_part], axis=-1).astype(
        jnp.bfloat16
    )
    grad_score_low = score_part.astype(jnp.bfloat16)
    grad_hidden = jnp.einsum("ste,de->std", grad_qkv, qkv_w, preferred_element_type=jnp.float32)
    grad_hidden = grad_hidden + jnp.einsum(
        "sth,dh->std", grad_score_low, score_w, preferred_element_type=jnp.float32
    )
    early_back = jax.vjp(normalize, residual, gains[0], biases[0])[1]
    grad_norm_early, gain_early, bias_early = early_back(grad_hidden)
    grad_residual = grad_after + grad_norm_early
    inputs = (hidden, mixed, hidden2, active, grad_score_low)
    outputs = (grad_qkv, grad_attn, grad_up, grad_down)
    norms = (jnp.stack([gain_early, gain_late]), jnp.stack([bias_early, bias_late]))
    return (grad_residual, inputs, outputs, norms)


def weight_terms(inputs, outputs, norms):
    all_hidden, all_mixed, all_hidden2, all_active, all_score = (
        lax.all_gather(inputs[0], "ctx", axis=1, tiled=True),
        lax.all_gather(inputs[1], "ctx", axis=1, tiled=True),
        lax.all_gather(inputs[2], "ctx", axis=1, tiled=True),
        lax.all_gather(inputs[3], "ctx", axis=1, tiled=True),
        lax.all_gather(inputs[4], "ctx", axis=1, tiled=True),
    )
    col_qkv, col_attn, col_up, col_down = (
        lax.all_to_all(outputs[0], "ctx", split_axis=2, concat_axis=1, tiled=True),
        lax.all_to_all(outputs[1], "ctx", split_axis=2, concat_axis=1, tiled=True),
        lax.all_to_all(outputs[2], "ctx", split_axis=2, concat_axis=1, tiled=True),
        lax.all_to_all(outputs[3], "ctx", split_axis=2, concat_axis=1, tiled=True),
    )
    gain_total, bias_total = lax.psum((norms[0], norms[1]), "ctx")
    qkv_term = jnp.einsum("std,ste->de", all_hidden, col_qkv, preferred_element_type=jnp.float32)
    score_term = jnp.einsum(
        "std,sth->dh", all_hidden, all_score, preferred_element_type=jnp.float32
    )
    out_term = jnp.einsum("std,ste->de", all_mixed, col_attn, preferred_element_type=jnp.float32)
    up_term = jnp.einsum("std,stf->df", all_hidden2, col_up, preferred_element_type=jnp.float32)
    down_term = jnp.einsum("sti,sto->io", all_active, col_down, preferred_element_type=jnp.float32)
    return (qkv_term, score_term, out_term, up_term, down_term, gain_total, bias_total)


def per_device(
    tokens,
    cotangent,
    kept_blocks,
    picture_starts,
    qkv_weight,
    score_weight,
    out_weight,
    up_weight,
    down_weight,
    norm_gain,
    norm_bias,
):
    local_len = tokens.shape[1]
    whole_len = local_len * lax.axis_size("ctx")
    own_start = lax.axis_index("ctx") * local_len
    masks = build_masks(kept_blocks, picture_starts, own_start, local_len, 0, whole_len)
    key_masks = build_masks(kept_blocks, picture_starts, 0, whole_len, own_start, local_len)
    residual = tokens.astype(jnp.float32)
    kept_weights = []
    saved_all = []
    for layer_index in range(LAYERS):
        rows = (
            lax.all_gather(qkv_weight[layer_index], "fsdp", axis=0, tiled=True),
            lax.all_gather(score_weight[layer_index], "fsdp", axis=0, tiled=True),
            lax.all_gather(out_weight[layer_index], "fsdp", axis=0, tiled=True),
            lax.all_gather(up_weight[layer_index], "fsdp", axis=0, tiled=True),
            lax.all_gather(down_weight[layer_index], "fsdp", axis=0, tiled=True),
            lax.all_gather(norm_gain[layer_index], "fsdp", axis=1, tiled=True),
            lax.all_gather(norm_bias[layer_index], "fsdp", axis=1, tiled=True),
        )
        full_qkv, full_out, full_up, full_down = (
            lax.all_gather(rows[0], "ctx", axis=1, tiled=True),
            lax.all_gather(rows[2], "ctx", axis=1, tiled=True),
            lax.all_gather(rows[3], "ctx", axis=1, tiled=True),
            lax.all_gather(rows[4], "ctx", axis=1, tiled=True),
        )
        weights = (full_qkv, rows[1], full_out, full_up, full_down, rows[5], rows[6])
        kept_weights.append(weights)
        residual, saved = forward_layer(residual, weights, masks)
        saved_all.append(saved)
    grad = cotangent.astype(jnp.float32)
    layer_terms = []
    for layer_index in reversed(range(LAYERS)):
        rows = (
            lax.all_gather(qkv_weight[layer_index], "fsdp", axis=0, tiled=True),
            lax.all_gather(score_weight[layer_index], "fsdp", axis=0, tiled=True),
            lax.all_gather(out_weight[layer_index], "fsdp", axis=0, tiled=True),
            lax.all_gather(up_weight[layer_index], "fsdp", axis=0, tiled=True),
            lax.all_gather(down_weight[layer_index], "fsdp", axis=0, tiled=True),
            lax.all_gather(norm_gain[layer_index], "fsdp", axis=1, tiled=True),
            lax.all_gather(norm_bias[layer_index], "fsdp", axis=1, tiled=True),
        )
        full_qkv, full_out, full_up, full_down = (
            lax.all_gather(rows[0], "ctx", axis=1, tiled=True),
            lax.all_gather(rows[2], "ctx", axis=1, tiled=True),
            lax.all_gather(rows[3], "ctx", axis=1, tiled=True),
            lax.all_gather(rows[4], "ctx", axis=1, tiled=True),
        )
        weights = (full_qkv, rows[1], full_out, full_up, full_down, rows[5], rows[6])
        grad, inputs, outputs, norms = backward_layer(
            grad, saved_all[layer_index], weights, masks, key_masks
        )
        terms = weight_terms(inputs, outputs, norms)
        layer_terms.insert(0, terms)
    stacked = [jnp.stack([entry[number] for entry in layer_terms]) for number in range(7)]
    summed = (
        lax.psum_scatter(
            stacked[0].astype(jnp.bfloat16), "fsdp", scatter_dimension=1, tiled=True
        ).astype(jnp.float32),
        lax.psum_scatter(
            stacked[1].astype(jnp.bfloat16), "fsdp", scatter_dimension=1, tiled=True
        ).astype(jnp.float32),
        lax.psum_scatter(
            stacked[2].astype(jnp.bfloat16), "fsdp", scatter_dimension=1, tiled=True
        ).astype(jnp.float32),
        lax.psum_scatter(
            stacked[3].astype(jnp.bfloat16), "fsdp", scatter_dimension=1, tiled=True
        ).astype(jnp.float32),
        lax.psum_scatter(
            stacked[4].astype(jnp.bfloat16), "fsdp", scatter_dimension=1, tiled=True
        ).astype(jnp.float32),
        lax.psum_scatter(
            stacked[5].astype(jnp.bfloat16), "fsdp", scatter_dimension=2, tiled=True
        ).astype(jnp.float32),
        lax.psum_scatter(
            stacked[6].astype(jnp.bfloat16), "fsdp", scatter_dimension=2, tiled=True
        ).astype(jnp.float32),
    )
    return (
        residual,
        grad,
        summed[0],
        summed[1],
        summed[2],
        summed[3],
        summed[4],
        summed[5],
        summed[6],
    )


D = 768
FF = 3072
HALF = 384
TOK = 512
SEQ = 1024
ROWS = 48
DROWS = 192
NEG = -1e30
F32 = jnp.float32
BF16 = jnp.bfloat16
VM = pl.BlockSpec(memory_space=pltpu.VMEM)
HB = pl.BlockSpec(memory_space=pl.ANY)
SM = pl.BlockSpec(memory_space=pltpu.SMEM)


def nn(a, b):
    return lax.dot_general(a, b, (((1,), (0,)), ((), ())), preferred_element_type=F32)


def nt(a, b):
    return lax.dot_general(a, b, (((1,), (1,)), ((), ())), preferred_element_type=F32)


def tn(a, b):
    return lax.dot_general(a, b, (((0,), (0,)), ((), ())), preferred_element_type=F32)


def sds(shape, dtype):
    return jax.ShapeDtypeStruct(shape, dtype)


def kernel_call(body, ins, in_specs, outs, out_specs, scratch, flops, limit_mib, name):
    moved = sum(v.size * v.dtype.itemsize for v in ins)
    moved += sum(math.prod(o.shape) * jnp.dtype(o.dtype).itemsize for o in outs)
    return pl.pallas_call(
        body,
        out_shape=tuple(outs),
        in_specs=in_specs,
        out_specs=tuple(out_specs),
        scratch_shapes=scratch,
        compiler_params=pltpu.CompilerParams(vmem_limit_bytes=limit_mib << 20),
        cost_estimate=pl.CostEstimate(flops=flops, bytes_accessed=moved, transcendentals=0),
        name=name,
    )(*ins)


def aligned(v, m):
    return pl.multiple_of(v, m)


def layer_norm_parts(x):
    centered = x - jnp.mean(x, axis=-1, keepdims=True)
    variance = jnp.mean(centered * centered, axis=-1, keepdims=True)
    scale = lax.rsqrt(variance + 1e-05)
    return centered * scale, scale


def split_blocks(src, keep, send, c, rows):
    for b in range(8):
        keep[b] = src[pl.ds(aligned((2 * b + c) * rows, 16), rows), :]
        send[b] = src[pl.ds(aligned((2 * b + 1 - c) * rows, 16), rows), :]


def device_of(f, q, pz):
    return f ^ (pz * 4 + (q & 1) * 2 + (q >> 2))


def qkv_kernel(idx, res, gb, sw0, sw1, *refs):
    wa, wb = refs[:8], refs[8:16]
    keep, send, htk, hts, wout, w, h, ht, sem, osem = refs[16:]
    f, y, c = idx[0], idx[1], idx[2]

    def fetch(pz, carry):
        for q in range(8):
            row = aligned(device_of(f, q, pz) * ROWS, 16)
            y2 = y ^ ((q >> 1) & 1)
            for g in range(3):
                src = wa[q].at[pz, :, pl.ds(g * HALF, HALF)] if g < 2 else wb[q].at[pz, :, pl.ds(0, HALF)]
                pltpu.make_async_copy(src, w.at[y2 * 3 + g, pl.ds(row, ROWS), :], sem).start()
        return carry

    lax.fori_loop(0, 4, fetch, 0)
    gain, bias = gb[0:1, :], gb[2:3, :]
    for t in range(4):
        rows = pl.ds(t * 128, 128)
        n, _ = layer_norm_parts(res[rows, :])
        v = n * gain + bias
        h[rows, :] = v.astype(BF16)
        ht[:, rows] = v.T.astype(BF16)
    split_blocks(ht, htk, hts, c, ROWS)
    pltpu.make_async_copy(w, w, sem).wait()
    out = pltpu.make_async_copy(w, wout, osem)
    out.start()

    def tile(t, carry):
        rows = pl.ds(aligned(t * 256, 256), 256)
        hv = h[rows, :]
        for j in range(3):
            cols = pl.ds(j * HALF, HALF)
            keep[rows, cols] = nn(hv, w[2 * j + c]).astype(BF16)
            send[rows, cols] = nn(hv, w[2 * j + 1 - c]).astype(BF16)
        keep[rows, pl.ds(1152, 128)] = nt(hv, sw0[...]).astype(BF16)
        send[rows, pl.ds(1152, 128)] = nt(hv, sw1[...]).astype(BF16)
        return carry

    lax.fori_loop(0, 2, tile, 0)
    out.wait()


def qkv_call(idx, res, gb, sw0, sw1, wa, wb):
    return kernel_call(
        qkv_kernel,
        [idx, res, gb, sw0, sw1, *wa, *wb],
        [SM, VM, VM, VM, VM] + [HB] * 16,
        [
            sds((TOK, 1280), BF16),
            sds((TOK, 1280), BF16),
            sds((8, ROWS, TOK), BF16),
            sds((8, ROWS, TOK), BF16),
            sds((6, D, HALF), BF16),
        ],
        [VM, VM, VM, VM, HB],
        [
            pltpu.VMEM((6, D, HALF), BF16),
            pltpu.VMEM((TOK, D), BF16),
            pltpu.VMEM((D, TOK), BF16),
            pltpu.SemaphoreType.DMA,
            pltpu.SemaphoreType.DMA,
        ],
        2 * TOK * D * 2304,
        32,
        "qkv",
    )


def load_halves(pairs, c, pad, sem):
    copies = []
    for number, (own, other, dst) in enumerate(pairs):
        for k, (src, half) in enumerate(((own, c), (other, 1 - c))):
            rows = pl.ds(aligned(pad + half * TOK, 128), TOK)
            copy = pltpu.make_async_copy(src, dst.at[rows, :], sem.at[2 * number + k])
            copy.start()
            copies.append(copy)
    return copies


def mask_tiles(tab):
    key = lax.broadcasted_iota(jnp.int32, (BLK, BLK), 0)
    query = lax.broadcasted_iota(jnp.int32, (BLK, BLK), 1)
    gap = query - key
    tab[0] = jnp.where((gap >= 0) & (gap < WINDOW), 0.0, NEG)
    tab[1] = jnp.where(gap >= 0, 0.0, NEG)
    tab[2] = jnp.zeros((BLK, BLK), F32)
    tab[3] = jnp.where(gap + BLK < WINDOW, 0.0, NEG)
    tab[4] = jnp.full((BLK, BLK), NEG, F32)


def log_sigmoid_of(v):
    return -(jnp.maximum(-v, 0.0) + jnp.log1p(jnp.exp(-jnp.abs(v))))


def picture_flags(pics, i):
    p0, p1 = pics[0] // BLK, pics[1] // BLK
    starts = (p0 == i) | (p1 == i)
    follows = (p0 == i - 1) | (p1 == i - 1)
    return starts, follows


def block_probs(s, ls, tab, kept, i, h, blocks, starts, follows):
    pair, odd = h // 2, h % 2
    lane = lax.broadcasted_iota(jnp.int32, (BLK, BLK), 1)
    mine = (lane >= 64) if odd else (lane < 64)
    base = aligned(i * BLK, BLK)
    cols = pair * BLK
    q = s[pl.ds(base + BLK, BLK), pl.ds(cols, BLK)] * jnp.asarray(HEAD_DIM**-0.5, BF16)
    q = jnp.where(mine, q, jnp.zeros_like(q))
    near, chosen = pl.ds(base, blocks * BLK), kept[h, i]
    far = pl.ds(aligned((chosen + 1) * BLK, BLK), BLK)
    kcols, vcols = pl.ds(HALF + cols, BLK), pl.ds(2 * HALF + cols, BLK)
    k = jnp.concatenate([s[near, kcols], s[far, kcols]], axis=0)
    v = jnp.concatenate([s[near, vcols], s[far, vcols]], axis=0)
    before = jnp.where(i == 0, 4, jnp.where(follows | (chosen == i - 1), 2, 3))
    here = jnp.where(starts | follows, 2, jnp.where(chosen == i, 1, 0))
    beyond = jnp.where(chosen < i - 1, 0.0, NEG).astype(F32)
    logits = nt(k, q)
    parts = [
        logits[0:BLK] + (tab[before] + ls[pl.ds(base, BLK), h : h + 1]),
        logits[BLK : 2 * BLK] + (tab[here] + ls[pl.ds(base + BLK, BLK), h : h + 1]),
    ]
    if blocks == 3:
        parts.append(logits[2 * BLK : 3 * BLK] + ls[pl.ds(base + 2 * BLK, BLK), h : h + 1])
    parts.append(logits[blocks * BLK :] + (ls[far, h : h + 1] + beyond))
    logits = jnp.concatenate(parts, axis=0)
    largest = jnp.max(logits, axis=0, keepdims=True)
    weights = jnp.exp(logits - largest)
    probs = weights * (1.0 / jnp.sum(weights, axis=0, keepdims=True))
    return q, k, v, probs, near, far, mine


def attend_kernel(idx, kept, pics, own, other, okeep, osend, s, ls, o, tab, sem):
    c = idx[2]
    copies = load_halves([(own, other, s)], c, BLK, sem)
    s[0:BLK, :] = jnp.zeros((BLK, 1280), BF16)
    mask_tiles(tab)
    for copy in copies:
        copy.wait()
    ls[...] = log_sigmoid_of(s[:, 1152:1280].astype(F32))

    def step(i, carry):
        starts, follows = picture_flags(pics, i)

        def run(blocks):
            rows = pl.ds(aligned(i * BLK, BLK), BLK)
            for pair in range(3):
                halves = []
                for odd in range(2):
                    _, _, v, probs, _, _, mine = block_probs(
                        s, ls, tab, kept, i, 2 * pair + odd, blocks, starts, follows
                    )
                    halves.append(tn(probs.astype(BF16), v))
                o[rows, pl.ds(pair * BLK, BLK)] = jnp.where(mine, halves[1], halves[0]).astype(BF16)

        @pl.when(starts)
        def _():
            run(3)

        @pl.when(jnp.logical_not(starts))
        def _():
            run(2)

        return carry

    lax.fori_loop(0, 8, step, 0)
    okeep[...] = o[pl.ds(aligned(c * TOK, TOK), TOK), :]
    osend[...] = o[pl.ds(aligned((1 - c) * TOK, TOK), TOK), :]


def attend_call(idx, kept, pics, own, other):
    return kernel_call(
        attend_kernel,
        [idx, kept, pics, own, other],
        [SM, SM, SM, HB, HB],
        [sds((TOK, HALF), BF16), sds((TOK, HALF), BF16)],
        [VM, VM],
        [
            pltpu.VMEM((SEQ + BLK, 1280), BF16),
            pltpu.VMEM((SEQ + BLK, BLK), F32),
            pltpu.VMEM((SEQ, HALF), BF16),
            pltpu.VMEM((5, BLK, BLK), F32),
            pltpu.SemaphoreType.DMA((2,)),
        ],
        6 * 8 * 4 * BLK * BLK * BLK * 4,
        32,
        "attend",
    )


def up_kernel(idx, res, mk, mr, gb, *refs):
    wo_in, wa, wb = refs[:8], refs[8:16], refs[16:24]
    aa, act, slope, mtk, mts, htk, hts, atk, ats, woo, wuo = refs[24:35]
    wo, wu, h, ht, at, sem, osem = refs[35:]
    f, y, c = idx[0], idx[1], idx[2]

    def fetch_out(pz, carry):
        for q in range(8):
            row = aligned(device_of(f, q, pz) * ROWS, 16)
            y2 = y ^ ((q >> 1) & 1)
            src = wo_in[q].at[pz, :, pl.ds(HALF, HALF)]
            pltpu.make_async_copy(src, wo.at[y2, pl.ds(row, ROWS), :], sem.at[0]).start()
        return carry

    def fetch_up(pz, carry):
        for q in range(8):
            row = aligned(device_of(f, q, pz) * ROWS, 16)
            y2 = y ^ ((q >> 1) & 1)
            for part, w in enumerate((wa, wb)):
                dst = wu.at[y2 * 2 + part, pl.ds(row, ROWS), :]
                pltpu.make_async_copy(w[q].at[pz], dst, sem.at[1]).start()
        return carry

    lax.fori_loop(0, 4, fetch_out, 0)
    lax.fori_loop(0, 4, fetch_up, 0)
    for t in range(4):
        rows = pl.ds(t * 128, 128)
        ht[pl.ds(aligned(c * HALF, HALF), HALF), rows] = mk[rows, :].astype(F32).T.astype(BF16)
        ht[pl.ds(aligned((1 - c) * HALF, HALF), HALF), rows] = mr[rows, :].astype(F32).T.astype(BF16)
    split_blocks(ht, mtk, mts, c, ROWS)
    pltpu.make_async_copy(wo, wo, sem.at[0]).wait()
    out0 = pltpu.make_async_copy(wo, woo, osem.at[0])
    out0.start()
    gain, bias = gb[1:2, :], gb[3:4, :]
    mine, theirs = pl.ds(aligned(c * HALF, HALF), HALF), pl.ds(aligned((1 - c) * HALF, HALF), HALF)
    for t in range(4):
        rows = pl.ds(t * 128, 128)
        for half in range(2):
            cols = pl.ds(half * HALF, HALF)
            part = nn(mk[rows, :], wo[half, mine, :]) + nn(mr[rows, :], wo[half, theirs, :])
            aa[rows, cols] = res[rows, cols] + part
        n, _ = layer_norm_parts(aa[rows, :])
        v = n * gain + bias
        h[rows, :] = v.astype(BF16)
        ht[:, rows] = v.T.astype(BF16)
    split_blocks(ht, htk, hts, c, ROWS)
    pltpu.make_async_copy(wu, wu, sem.at[1]).wait()
    out1 = pltpu.make_async_copy(wu, wuo, osem.at[1])
    out1.start()
    for g in range(4):

        def tile(t, carry):
            rows = pl.ds(aligned(t * 128, 128), 128)
            u = nn(h[rows, :], wu[g])
            inner = 0.7978845608 * (u + 0.044715 * (u * u * u))
            th = jnp.tanh(inner)
            a = 0.5 * u * (1.0 + th)
            d = 0.5 * (1.0 + th) + (0.5 * u) * (1.0 - th * th) * (
                0.7978845608 * (1.0 + (3 * 0.044715) * (u * u))
            )
            cols = pl.ds(g * D, D)
            act[rows, cols] = a.astype(BF16)
            slope[rows, cols] = d.astype(BF16)
            at[cols, rows] = a.T.astype(BF16)
            return carry

        lax.fori_loop(0, 4, tile, 0)
    split_blocks(at, atk, ats, c, DROWS)
    out0.wait()
    out1.wait()


def up_call(idx, res, mk, mr, gb, wo, wa, wb):
    return kernel_call(
        up_kernel,
        [idx, res, mk, mr, gb, *wo, *wa, *wb],
        [SM, VM, VM, VM, VM] + [HB] * 24,
        [
            sds((TOK, D), F32),
            sds((TOK, FF), BF16),
            sds((TOK, FF), BF16),
            sds((8, ROWS, TOK), BF16),
            sds((8, ROWS, TOK), BF16),
            sds((8, ROWS, TOK), BF16),
            sds((8, ROWS, TOK), BF16),
            sds((8, DROWS, TOK), BF16),
            sds((8, DROWS, TOK), BF16),
            sds((2, D, HALF), BF16),
            sds((4, D, D), BF16),
        ],
        [VM] * 9 + [HB, HB],
        [
            pltpu.VMEM((2, D, HALF), BF16),
            pltpu.VMEM((4, D, D), BF16),
            pltpu.VMEM((TOK, D), BF16),
            pltpu.VMEM((D, TOK), BF16),
            pltpu.VMEM((FF, TOK), BF16),
            pltpu.SemaphoreType.DMA((2,)),
            pltpu.SemaphoreType.DMA((2,)),
        ],
        2 * TOK * D * (D + FF),
        48,
        "up",
    )


def down_kernel(idx, act, aa, *refs):
    wa, wb = refs[:8], refs[8:16]
    res, wdo, wd, sem, osem = refs[16:]
    f, y = idx[0], idx[1]

    def fetch(pz, carry):
        for q in range(8):
            row = device_of(f, q, pz) * DROWS
            y2 = y ^ ((q >> 1) & 1)
            for part, w in enumerate((wa, wb)):
                dst = wd.at[y2, pl.ds(aligned(row + part * 96, 16), 96), :]
                pltpu.make_async_copy(w[q].at[pz], dst, sem).start()
        return carry

    lax.fori_loop(0, 4, fetch, 0)
    pltpu.make_async_copy(wd, wd, sem).wait()
    out = pltpu.make_async_copy(wd, wdo, osem)
    out.start()

    def tile(t, carry):
        rows = pl.ds(aligned(t * 256, 256), 256)
        for half in range(2):
            cols = pl.ds(half * HALF, HALF)
            res[rows, cols] = aa[rows, cols] + nn(act[rows, :], wd[half])
        return carry

    lax.fori_loop(0, 2, tile, 0)
    out.wait()


def down_call(idx, act, aa, wa, wb):
    return kernel_call(
        down_kernel,
        [idx, act, aa, *wa, *wb],
        [SM, VM, VM] + [HB] * 16,
        [sds((TOK, D), F32), sds((2, FF, HALF), BF16)],
        [VM, HB],
        [
            pltpu.VMEM((2, FF, HALF), BF16),
            pltpu.SemaphoreType.DMA,
            pltpu.SemaphoreType.DMA,
        ],
        2 * TOK * D * FF,
        32,
        "down",
    )


def down_back_kernel(grad, slope, wd_in, gu, wd, sem):
    copy = pltpu.make_async_copy(wd_in, wd, sem)
    copy.start()
    copy.wait()
    for g in range(4):

        def tile(t, carry):
            rows = pl.ds(aligned(t * 256, 256), 256)
            cols = pl.ds(g * D, D)
            part = nt(grad[rows, 0:HALF], wd[0, cols, :]) + nt(grad[rows, HALF:D], wd[1, cols, :])
            gu[rows, cols] = (part * slope[rows, cols].astype(F32)).astype(BF16)
            return carry

        lax.fori_loop(0, 2, tile, 0)


def down_back_call(grad, slope, wd):
    return kernel_call(
        down_back_kernel,
        [grad, slope, wd],
        [VM, VM, HB],
        [sds((TOK, FF), BF16)],
        [VM],
        [pltpu.VMEM((2, FF, HALF), BF16), pltpu.SemaphoreType.DMA],
        2 * TOK * D * FF,
        32,
        "down_back",
    )[0]


def norm_back(x, grad_out, gain):
    n, scale = layer_norm_parts(x)
    e = grad_out * gain
    back = scale * (
        e - jnp.mean(e, axis=-1, keepdims=True) - n * jnp.mean(e * n, axis=-1, keepdims=True)
    )
    gain_part = jnp.sum(grad_out * n, axis=0, keepdims=True)
    bias_part = jnp.sum(grad_out, axis=0, keepdims=True)
    return back, gain_part, bias_part


def up_back_kernel(idx, grad, gu, aa, gb, wu_in, wo_in, ga, gat, gmk, gms, nrm, wu, wo, sem):
    c = idx[2]
    c0 = pltpu.make_async_copy(wu_in, wu, sem.at[0])
    c1 = pltpu.make_async_copy(wo_in, wo, sem.at[1])
    c0.start()
    c1.start()
    nrm[...] = jnp.zeros_like(nrm)
    gain = gb[1:2, :]
    mine, theirs = pl.ds(aligned(c * HALF, HALF), HALF), pl.ds(aligned((1 - c) * HALF, HALF), HALF)
    c0.wait()
    c1.wait()

    def tile(t, carry):
        rows = pl.ds(aligned(t * 128, 128), 128)
        gh = nt(gu[rows, 0:D], wu[0])
        for g in range(1, 4):
            gh += nt(gu[rows, pl.ds(g * D, D)], wu[g])
        back, gain_part, bias_part = norm_back(aa[rows, :], gh, gain)
        total = grad[rows, :] + back
        ga[rows, :] = total
        low = total.astype(BF16)
        gat[rows, :] = low
        nrm[0:1, :] += gain_part
        nrm[1:2, :] += bias_part
        for dst, part in ((gmk, mine), (gms, theirs)):
            dst[rows, :] = (
                nt(low[:, 0:HALF], wo[0, part, :]) + nt(low[:, HALF:D], wo[1, part, :])
            ).astype(BF16)
        return carry

    lax.fori_loop(0, 4, tile, 0)


def up_back_call(idx, grad, gu, aa, gb, wu, wo):
    return kernel_call(
        up_back_kernel,
        [idx, grad, gu, aa, gb, wu, wo],
        [SM, VM, VM, VM, VM, HB, HB],
        [
            sds((TOK, D), F32),
            sds((TOK, D), BF16),
            sds((TOK, HALF), BF16),
            sds((TOK, HALF), BF16),
            sds((8, D), F32),
        ],
        [VM] * 5,
        [
            pltpu.VMEM((4, D, D), BF16),
            pltpu.VMEM((2, D, HALF), BF16),
            pltpu.SemaphoreType.DMA((2,)),
        ],
        2 * TOK * D * (D + FF),
        40,
        "up_back",
    )


def attend_back_kernel(
    idx, kept, pics, own, other, gown, gother, down_, doth, s, g, ls, d, dk, dv, ds, tab, sem
):
    c = idx[2]
    copies = load_halves([(own, other, s)], c, BLK, sem)
    copies += load_halves([(gown, gother, g)], c, 0, sem.at[pl.ds(2, 2)])
    s[0:BLK, :] = jnp.zeros((BLK, 1280), BF16)
    mask_tiles(tab)
    dk[...] = jnp.zeros_like(dk)
    dv[...] = jnp.zeros_like(dv)
    ds[...] = jnp.zeros_like(ds)
    for copy in copies:
        copy.wait()
    ls[...] = log_sigmoid_of(s[:, 1152:1280].astype(F32))
    lane = lax.broadcasted_iota(jnp.int32, (BLK, BLK), 1)

    def step(i, carry):
        starts, follows = picture_flags(pics, i)

        def run(blocks):
            rows = pl.ds(aligned(i * BLK, BLK), BLK)
            for pair in range(3):
                cols = pl.ds(pair * BLK, BLK)
                gp = g[rows, cols]
                halves = []
                for odd in range(2):
                    h = 2 * pair + odd
                    q, k, v, probs, near, far, mine = block_probs(
                        s, ls, tab, kept, i, h, blocks, starts, follows
                    )
                    gm = jnp.where(mine, gp, jnp.zeros_like(gp))
                    gprob = nt(v, gm)
                    inner = jnp.sum(probs * gprob, axis=0, keepdims=True)
                    gl = (probs * (gprob - inner)).astype(BF16)
                    gv = nn(probs.astype(BF16), gm)
                    ind = jnp.where(lane == h, 1.0, 0.0).astype(BF16)
                    gk = nn(gl, jnp.concatenate([q, ind], axis=1))
                    cut = blocks * BLK
                    dv[near, cols] += gv[:cut]
                    dv[far, cols] += gv[cut:]
                    dk[near, cols] += gk[:cut, :BLK]
                    dk[far, cols] += gk[cut:, :BLK]
                    ds[near, :] += gk[:cut, BLK:]
                    ds[far, :] += gk[cut:, BLK:]
                    halves.append(tn(gl, k))
                d[rows, cols] = (
                    jnp.where(mine, halves[1], halves[0]) * (HEAD_DIM**-0.5)
                ).astype(BF16)

        @pl.when(starts)
        def _():
            run(3)

        @pl.when(jnp.logical_not(starts))
        def _():
            run(2)

        return carry

    lax.fori_loop(0, 8, step, 0)
    keys = pl.ds(BLK, SEQ)
    d[:, HALF : 2 * HALF] = dk[keys, :].astype(BF16)
    d[:, 2 * HALF : 3 * HALF] = dv[keys, :].astype(BF16)
    back = ds[keys, :] * jax.nn.sigmoid(-s[keys, 1152:1280].astype(F32))
    d[:, 1152:1280] = back.astype(BF16)
    down_[...] = d[pl.ds(aligned(c * TOK, TOK), TOK), :]
    doth[...] = d[pl.ds(aligned((1 - c) * TOK, TOK), TOK), :]


def attend_back_call(idx, kept, pics, own, other, gown, gother):
    return kernel_call(
        attend_back_kernel,
        [idx, kept, pics, own, other, gown, gother],
        [SM, SM, SM, HB, HB, HB, HB],
        [sds((TOK, 1280), BF16), sds((TOK, 1280), BF16)],
        [VM, VM],
        [
            pltpu.VMEM((SEQ + BLK, 1280), BF16),
            pltpu.VMEM((SEQ, HALF), BF16),
            pltpu.VMEM((SEQ + BLK, BLK), F32),
            pltpu.VMEM((SEQ, 1280), BF16),
            pltpu.VMEM((SEQ + BLK, HALF), F32),
            pltpu.VMEM((SEQ + BLK, HALF), F32),
            pltpu.VMEM((SEQ + BLK, BLK), F32),
            pltpu.VMEM((5, BLK, BLK), F32),
            pltpu.SemaphoreType.DMA((4,)),
        ],
        6 * 8 * 4 * BLK * BLK * BLK * 10,
        40,
        "attend_back",
    )


def qkv_back_kernel(idx, ga, down_, dr, res, gb, sw0, sw1, w_in, gout, glow, nrm, w, sem):
    c = idx[2]
    copy = pltpu.make_async_copy(w_in, w, sem)
    copy.start()
    nrm[...] = jnp.zeros_like(nrm)
    gain = gb[0:1, :]
    copy.wait()

    def tile(t, carry):
        rows = pl.ds(aligned(t * 128, 128), 128)
        gh = nn(down_[rows, 1152:1280], sw0[...]) + nn(dr[rows, 1152:1280], sw1[...])
        for j in range(3):
            cols = pl.ds(j * HALF, HALF)
            gh += nt(down_[rows, cols], w[2 * j + c]) + nt(dr[rows, cols], w[2 * j + 1 - c])
        back, gain_part, bias_part = norm_back(res[rows, :], gh, gain)
        total = ga[rows, :] + back
        gout[rows, :] = total
        glow[rows, :] = total.astype(BF16)
        nrm[0:1, :] += gain_part
        nrm[1:2, :] += bias_part
        return carry

    lax.fori_loop(0, 4, tile, 0)


def qkv_back_call(idx, ga, down_, dr, res, gb, sw0, sw1, w):
    return kernel_call(
        qkv_back_kernel,
        [idx, ga, down_, dr, res, gb, sw0, sw1, w],
        [SM, VM, VM, VM, VM, VM, VM, VM, HB],
        [sds((TOK, D), F32), sds((TOK, D), BF16), sds((8, D), F32)],
        [VM, VM, VM],
        [pltpu.VMEM((6, D, HALF), BF16), pltpu.SemaphoreType.DMA],
        2 * TOK * D * 2304,
        32,
        "qkv_back",
    )


def scatter_rows(src, f, rows, offset, count, pyy, portion, ka, sa, kb, sb):
    for pxx in range(2):
        for pz in range(4):
            block = (f >> 1) ^ (pz * 2 + pxx)
            value = src[pl.ds(aligned(block * rows + offset, 16), count), :]
            if portion == 0:
                (sa if pxx else ka)[pyy, pz] = value
            else:
                (sb if pyy else kb)[pxx, pz] = value


def up_grad_kernel(idx, xk, xr, gk, gr, ka, sa, kb, sb, tmp):
    f, y = idx[0], idx[1]
    for portion in range(2):
        for pyy in range(2):
            cols = pl.ds(aligned((y ^ pyy) * 1536 + portion * D, 128), D)
            tmp[portion * 2 + pyy] = (nn(xk[...], gk[:, cols]) + nn(xr[...], gr[:, cols])).astype(
                BF16
            )
            scatter_rows(
                tmp.at[portion * 2 + pyy], f, ROWS, 0, ROWS, pyy, portion, ka, sa, kb, sb
            )


def up_grad_call(idx, xk, xr, gk, gr):
    piece = sds((2, 4, ROWS, D), BF16)
    return kernel_call(
        up_grad_kernel,
        [idx, xk.reshape(HALF, TOK), xr.reshape(HALF, TOK), gk, gr],
        [SM, VM, VM, VM, VM],
        [piece] * 4,
        [VM] * 4,
        [pltpu.VMEM((4, HALF, D), BF16)],
        2 * SEQ * HALF * FF,
        32,
        "up_grad",
    )


def down_grad_kernel(idx, xk, xr, gk, gr, ka, sa, kb, sb, tmp):
    f, y = idx[0], idx[1]
    for pyy in range(2):
        cols = pl.ds(aligned((y ^ pyy) * HALF, 128), HALF)

        def tile(t, carry):
            rows = pl.ds(aligned(t * HALF, HALF), HALF)
            tmp[pyy, rows, :] = (nn(xk[rows, :], gk[:, cols]) + nn(xr[rows, :], gr[:, cols])).astype(
                BF16
            )
            return carry

        lax.fori_loop(0, 4, tile, 0)
        for portion in range(2):
            scatter_rows(
                tmp.at[pyy], f, DROWS, portion * 96, 96, pyy, portion, ka, sa, kb, sb
            )


def down_grad_call(idx, xk, xr, gk, gr):
    piece = sds((2, 4, 96, HALF), BF16)
    return kernel_call(
        down_grad_kernel,
        [idx, xk.reshape(4 * HALF, TOK), xr.reshape(4 * HALF, TOK), gk, gr],
        [SM, VM, VM, VM, VM],
        [piece] * 4,
        [VM] * 4,
        [pltpu.VMEM((2, 4 * HALF, HALF), BF16)],
        2 * SEQ * HALF * FF,
        32,
        "down_grad",
    )


def qkv_grad_kernel(
    idx, xk, xr, mk, mr, d00, d01, d10, d11, gk, gr, ka, sa, kb, sb, sc, dy, tmp, tsc, sem
):
    f, y, c = idx[0], idx[1], idx[2]
    copies = []
    for tok, pair in enumerate(((d00, d01), (d10, d11))):
        for k, src in enumerate(pair):
            for j in range(3):
                copy = pltpu.make_async_copy(
                    src.at[:, pl.ds(j * HALF, HALF)],
                    dy.at[tok, 2 * j + (c ^ k)],
                    sem.at[tok * 6 + k * 3 + j],
                )
                copy.start()
                copies.append(copy)
    for tok, pair in enumerate(((d00, d01), (d10, d11))):
        for k, src in enumerate(pair):
            copy = pltpu.make_async_copy(
                src.at[:, pl.ds(1152, 128)], tsc.at[tok * 2 + k], sem.at[12 + tok * 2 + k]
            )
            copy.start()
            copies.append(copy)
    for copy in copies:
        copy.wait()
    for pyy in range(2):
        y2 = y ^ pyy
        for part in range(4):
            portion, side = part // 2, part % 2
            cols = pl.ds(side * HALF, HALF)
            if part < 3:
                g = y2 * 3 + part
                value = nn(xk[...], dy[0, g]) + nn(xr[...], dy[1, g])
            else:
                oc = pl.ds(aligned(y2 * HALF, 128), HALF)
                value = nn(mk[...], gk[:, oc]) + nn(mr[...], gr[:, oc])
            tmp[portion * 2 + pyy, :, cols] = value.astype(BF16)
        for portion in range(2):
            scatter_rows(
                tmp.at[portion * 2 + pyy], f, ROWS, 0, ROWS, pyy, portion, ka, sa, kb, sb
            )
    own = nn(xk[...], tsc[0]) + nn(xr[...], tsc[2])
    theirs = nn(xk[...], tsc[1]) + nn(xr[...], tsc[3])
    first = jnp.where(c == 0, own, theirs)
    second = jnp.where(c == 0, theirs, own)
    both = first + pltpu.roll(second, 64, 1)
    for pxx in range(2):
        for pz in range(4):
            target = (f >> 1) ^ (pz * 2 + pxx)
            for b in range(8):

                @pl.when(target == b)
                def _():
                    sc[pxx, pz] = both[b * ROWS : (b + 1) * ROWS, :]


def qkv_grad_call(idx, xk, xr, mk, mr, d00, d01, d10, d11, gk, gr):
    piece = sds((2, 4, ROWS, D), BF16)
    flat = [v.reshape(HALF, TOK) for v in (xk, xr, mk, mr)]
    return kernel_call(
        qkv_grad_kernel,
        [idx, *flat, d00, d01, d10, d11, gk, gr],
        [SM, VM, VM, VM, VM, HB, HB, HB, HB, VM, VM],
        [piece] * 4 + [sds((2, 4, ROWS, 128), F32)],
        [VM] * 5,
        [
            pltpu.VMEM((2, 6, TOK, HALF), BF16),
            pltpu.VMEM((4, HALF, D), BF16),
            pltpu.VMEM((4, TOK, 128), BF16),
            pltpu.SemaphoreType.DMA((16,)),
        ],
        2 * SEQ * HALF * FF,
        40,
        "qkv_grad",
    )


def pairwise(v, bits):
    return lax.ppermute(v, "fsdp", [(i, i ^ bits) for i in range(16)])


def over_ctx(v):
    return lax.ppermute(v, "ctx", [(0, 1), (1, 0)])


def over_core(v):
    return pairwise(v, 1)


def over_x(v):
    return pairwise(v, 2)


def turn(v):
    perm = [
        ((g * 2 + a) * 2 + b, (g * 2 + b) * 2 + a) for g in range(8) for a in range(2) for b in range(2)
    ]
    return lax.ppermute(v, ("fsdp", "ctx"), perm)


def gather_piece(part_a, part_b):
    both = jnp.stack([part_a, part_b])
    near = [both] + [pairwise(both, k << 2) for k in range(1, 4)]
    a0, b0 = (jnp.stack([v[part] for v in near]) for part in range(2))
    a1 = over_x(a0)
    b2 = over_ctx(b0)
    a = [a0, a1, over_ctx(a0), over_ctx(a1)]
    b = [b0, over_x(b0), b2, over_x(b2)]
    return (a + [over_core(v) for v in a], b + [over_core(v) for v in b])


def reduce_piece(ka, sa, kb, sb):
    def add(mine, received):
        return mine.astype(F32) + received.astype(F32)

    def last(total, received):
        low = total.astype(BF16)
        return total[0] + sum(pairwise(low[k], k << 2).astype(F32) for k in range(1, 4))

    ta = add(ka, over_x(sa))
    tb = add(kb, over_ctx(sb))
    ta = add(ta[0], over_ctx(ta[1].astype(BF16)))
    tb = add(tb[0], over_x(tb[1].astype(BF16)))
    return last(ta, None), last(tb, None)


def pair_device(
    tokens,
    cotangent,
    kept_blocks,
    picture_starts,
    qkv_weight,
    score_weight,
    out_weight,
    up_weight,
    down_weight,
    norm_gain,
    norm_bias,
):
    f = lax.axis_index("fsdp").astype(jnp.int32)
    y = lax.axis_index("ctx").astype(jnp.int32)
    c = f & 1
    idx = jnp.stack([f, y, c])
    start = turn(tokens[0])
    cot = turn(cotangent[0])
    kept = jnp.where(c == y, kept_blocks[0], over_core(kept_blocks[0]))
    pics = jnp.where(c == y, picture_starts[0], over_core(picture_starts[0]))
    kept = lax.dynamic_slice_in_dim(kept, c * 6, 6, 0)
    small = jnp.concatenate(
        [jnp.swapaxes(score_weight, 1, 2), norm_gain, norm_bias], axis=1
    ).reshape(LAYERS * 16, ROWS)
    small = jnp.pad(small, ((0, 0), (0, 128 - ROWS)))
    small = jnp.stack([small] + [pairwise(small, k << 2) for k in range(1, 4)])
    small = jnp.concatenate([small, over_x(small)])
    small = jnp.concatenate([small, over_core(small)])
    away = jnp.arange(16, dtype=jnp.int32) ^ f
    small = jnp.take(small, (away & 1) * 8 + ((away >> 1) & 1) * 4 + (away >> 2), axis=0)
    small = jnp.moveaxis(small[:, :, :ROWS], 0, 1).reshape(LAYERS, 16, D)
    pieces = []
    for l in range(LAYERS):
        qo = gather_piece(
            qkv_weight[l][:, :D], jnp.concatenate([qkv_weight[l][:, D:], out_weight[l]], axis=1)
        )
        up = gather_piece(up_weight[l][:, :D], up_weight[l][:, D:])
        dn = gather_piece(down_weight[l][:96], down_weight[l][96:])
        pieces.append((qo, up, dn))
    residual = start.astype(F32)
    saved = []
    for l in range(LAYERS):
        (qa, qb), (ua, ub), (da, db) = pieces[l]
        gb = jnp.pad(small[l, 12:16].astype(F32), ((0, 4), (0, 0)))
        own_rows = lax.dynamic_slice_in_dim(small[l], c * 6, 6, 0)
        other_rows = lax.dynamic_slice_in_dim(small[l], (1 - c) * 6, 6, 0)
        sw0 = jnp.pad(own_rows, ((0, 122), (0, 0)))
        sw1 = jnp.pad(other_rows, ((0, 122), (0, 0)))
        own, send, xk, xs, w_qkv = qkv_call(idx, residual, gb, sw0, sw1, qa, qb)
        other = over_core(send)
        mixed, msend = attend_call(idx, kept, pics, own, other)
        after, act, slope, mk, ms, hk, hs, ak, as_, w_out, w_up = up_call(
            idx, residual, mixed, over_core(msend), gb, qb, ua, ub
        )
        new, w_down = down_call(idx, act, after, da, db)
        received = tuple(over_core(v) for v in (xs, ms, hs, as_))
        saved.append(
            (residual, gb, sw0, sw1, own, other, after, slope, (xk, mk, hk, ak), received)
            + (w_qkv, w_out, w_up, w_down)
        )
        residual = new
    block_output = turn(residual.astype(BF16)).astype(F32)
    grad = cot.astype(F32)
    grad_low = cot
    grads = [None] * LAYERS
    norms = [None] * LAYERS
    for l in reversed(range(LAYERS)):
        res, gb, sw0, sw1, own, other, after, slope, kept_t, recv_t, w_qkv, w_out, w_up, w_down = saved[l]
        xk, mk, hk, ak = kept_t
        xr, mr, hr, ar = recv_t
        gu = down_back_call(grad_low, slope, w_down)
        gd_r = over_core(grad_low)
        gu_r = over_core(gu)
        down_pieces = reduce_piece(*down_grad_call(idx, ak, ar, grad_low, gd_r))
        ga, gat, gmk, gms, nrm2 = up_back_call(idx, grad, gu, after, gb, w_up, w_out)
        gm_r = over_core(gms)
        gat_r = over_core(gat)
        up_pieces = reduce_piece(*up_grad_call(idx, hk, hr, gu, gu_r))
        d_own, d_oth = attend_back_call(idx, kept, pics, own, other, gmk, gm_r)
        r1 = over_core(d_oth)
        r2 = over_core(d_own)
        *qo, sc = qkv_grad_call(idx, xk, xr, mk, mr, d_own, r1, d_oth, r2, gat, gat_r)
        qo_pieces = reduce_piece(*qo)
        grad, grad_low, nrm1 = qkv_back_call(idx, ga, d_own, r1, res, gb, sw0, sw1, w_qkv)
        sc = sc + over_ctx(sc)
        sc = sc[0] + over_x(sc[1])
        sc = sc[0] + sum(pairwise(sc[k], k << 2) for k in range(1, 4))
        grads[l] = (qo_pieces, up_pieces, down_pieces, sc)
        norms[l] = jnp.concatenate([nrm1[0:1], nrm2[0:1], nrm1[1:2], nrm2[1:2]])
    token_grad = turn(grad_low).astype(F32)
    nrm = jnp.concatenate(norms)
    nrm = nrm + over_core(nrm)
    nrm = nrm + over_ctx(nrm)
    nrm = nrm + over_x(nrm)
    nrm = nrm + sum(pairwise(nrm, k << 2) for k in range(1, 4))
    nrm = lax.dynamic_slice_in_dim(nrm, f * ROWS, ROWS, 1).reshape(LAYERS, 2, 2, ROWS)
    qkv_grad = jnp.stack([jnp.concatenate([a, b[:, :HALF]], 1) for (a, b), _, _, _ in grads])
    out_grad = jnp.stack([b[:, HALF:] for (_, b), _, _, _ in grads])
    up_grad = jnp.stack([jnp.concatenate([a, b], 1) for _, (a, b), _, _ in grads])
    down_grad = jnp.stack([jnp.concatenate([a, b], 0) for _, _, (a, b), _ in grads])
    score_grad = jnp.stack(
        [jnp.concatenate([s[:, 0:6], s[:, 64:70]], 1) for _, _, _, s in grads]
    )
    return (
        block_output[None],
        token_grad[None],
        qkv_grad,
        score_grad,
        out_grad,
        up_grad,
        down_grad,
        nrm[:, 0],
        nrm[:, 1],
    )


def solution(mesh):
    in_specs = (
        P("fsdp", "ctx", None),
        P("fsdp", "ctx", None),
        P("fsdp", None, None),
        P("fsdp", None),
        P(None, "fsdp", "ctx"),
        P(None, "fsdp", None),
        P(None, "fsdp", "ctx"),
        P(None, "fsdp", "ctx"),
        P(None, "fsdp", "ctx"),
        P(None, None, "fsdp"),
        P(None, None, "fsdp"),
    )
    out_specs = (
        P("fsdp", "ctx", None),
        P("fsdp", "ctx", None),
        P(None, "fsdp", "ctx"),
        P(None, "fsdp", None),
        P(None, "fsdp", "ctx"),
        P(None, "fsdp", "ctx"),
        P(None, "fsdp", "ctx"),
        P(None, None, "fsdp"),
        P(None, None, "fsdp"),
    )
    pairs = mesh.shape["fsdp"] == 16 and mesh.shape["ctx"] == 2
    return jax.shard_map(
        pair_device if pairs else per_device, mesh=mesh, in_specs=in_specs, out_specs=out_specs, check_vma=False
    )
```

```python
import math
from functools import partial

import jax
import jax.numpy as jnp
from jax import lax
from jax.experimental import pallas as pl
from jax.experimental.pallas import tpu as pltpu
from jax.sharding import Mesh
from jax.sharding import PartitionSpec as P

HEADS = 12
HEAD_DIM = 64
LAYERS = 2
BLK = 128
WINDOW = 64
PIC_LEN = 256


def normalize(residual, gain, bias):
    mean_value = jnp.mean(residual, axis=-1, keepdims=True)
    centered = residual - mean_value
    variance = jnp.mean(centered * centered, axis=-1, keepdims=True)
    return centered * lax.rsqrt(variance + 1e-05) * gain + bias


def gelu_tanh(value):
    return jax.nn.gelu(value, approximate=True)


def log_sigmoid(value):
    return -(jnp.maximum(-value, 0.0) + jnp.log1p(jnp.exp(-jnp.abs(value))))


def split_heads(tensor):
    return jnp.moveaxis(tensor.reshape(tensor.shape[:-1] + (HEADS, HEAD_DIM)), 2, 0)


def join_heads(tensor):
    moved = jnp.moveaxis(tensor, 0, 2)
    return moved.reshape(moved.shape[:2] + (HEADS * HEAD_DIM,))


def masked_logits(queries, keys, scores, kept, base, causal, key_block):
    logits = jnp.einsum(
        "sqd,skd->sqk", queries, keys, preferred_element_type=jnp.float32
    ) * HEAD_DIM ** (-0.5)
    logits = logits + log_sigmoid(scores.astype(jnp.float32))[:, None, :]
    allowed = base | causal[None] & (key_block[None, None, :] == kept[:, :, None])
    return (logits, allowed)


def attend_head(items, base, causal, key_block):
    queries, keys, values, scores, kept = items
    logits, allowed = masked_logits(queries, keys, scores, kept, base, causal, key_block)
    logits = jnp.where(allowed, logits, -1e30)
    largest = jnp.max(logits, axis=-1, keepdims=True)
    weights = jnp.exp(logits - largest)
    totals = jnp.sum(weights, axis=-1, keepdims=True)
    probs_low = (weights / totals).astype(jnp.bfloat16)
    outputs = jnp.einsum("sqk,skd->sqd", probs_low, values, preferred_element_type=jnp.float32)
    return (outputs, (largest + jnp.log(totals))[..., 0])


def query_side_grads(items, base, causal, key_block):
    queries, keys, values, scores, kept, grad_out, log_totals = items
    logits, allowed = masked_logits(queries, keys, scores, kept, base, causal, key_block)
    probs = jnp.where(allowed, jnp.exp(logits - log_totals[..., None]), 0.0)
    grad_probs = jnp.einsum("sqd,skd->sqk", grad_out, values, preferred_element_type=jnp.float32)
    inner = jnp.sum(probs * grad_probs, axis=-1, keepdims=True)
    grad_logits = (probs * (grad_probs - inner)).astype(jnp.bfloat16)
    grad_queries = jnp.einsum(
        "sqk,skd->sqd", grad_logits, keys, preferred_element_type=jnp.float32
    ) * HEAD_DIM ** (-0.5)
    return (grad_queries, inner[..., 0])


def key_side_grads(items, base, causal, key_block):
    queries, keys, values, scores, kept, grad_out, log_totals, inner = items
    logits, allowed = masked_logits(queries, keys, scores, kept, base, causal, key_block)
    probs = jnp.where(allowed, jnp.exp(logits - log_totals[..., None]), 0.0)
    grad_probs = jnp.einsum("sqd,skd->sqk", grad_out, values, preferred_element_type=jnp.float32)
    grad_logits = (probs * (grad_probs - inner[..., None])).astype(jnp.bfloat16)
    grad_values = jnp.einsum(
        "sqk,sqd->skd", probs.astype(jnp.bfloat16), grad_out, preferred_element_type=jnp.float32
    )
    grad_keys = jnp.einsum(
        "sqk,sqd->skd", grad_logits, queries, preferred_element_type=jnp.float32
    ) * HEAD_DIM ** (-0.5)
    grad_scores = jnp.sum(grad_logits.astype(jnp.float32), axis=1) * jax.nn.sigmoid(
        -scores.astype(jnp.float32)
    )
    return (grad_keys, grad_values, grad_scores)


def build_masks(kept_blocks, picture_starts, query_start, query_len, key_start, key_len):
    query_pos = query_start + jnp.arange(query_len, dtype=jnp.int32)
    key_pos = key_start + jnp.arange(key_len, dtype=jnp.int32)
    causal = key_pos[None, :] <= query_pos[:, None]
    local = causal & (query_pos[:, None] - key_pos[None, :] < WINDOW)
    starts = picture_starts[:, :, None]
    inside_query = (query_pos[None, None, :] >= starts) & (
        query_pos[None, None, :] < starts + PIC_LEN
    )
    inside_key = (key_pos[None, None, :] >= starts) & (key_pos[None, None, :] < starts + PIC_LEN)
    picture = jnp.any(inside_query[:, :, :, None] & inside_key[:, :, None, :], axis=1)
    base = local[None] | picture
    kept_all = jnp.repeat(kept_blocks, BLK, axis=2)
    kept_rows = jnp.moveaxis(lax.dynamic_slice_in_dim(kept_all, query_start, query_len, 2), 1, 0)
    return (base, causal, key_pos // BLK, kept_rows)


def forward_layer(residual, weights, masks):
    qkv_w, score_w, out_w, up_w, down_w, gain, bias = weights
    base, causal, key_block, kept_rows = masks
    gains = gain.astype(jnp.float32)
    biases = bias.astype(jnp.float32)
    hidden = normalize(residual, gains[0], biases[0]).astype(jnp.bfloat16)
    qkv = jnp.dot(hidden, qkv_w, preferred_element_type=jnp.float32).astype(jnp.bfloat16)
    scores = jnp.dot(hidden, score_w, preferred_element_type=jnp.float32).astype(jnp.bfloat16)
    queries, keys, values = jnp.split(qkv, 3, axis=-1)
    all_keys, all_values, all_scores = (
        lax.all_gather(keys, "ctx", axis=1, tiled=True),
        lax.all_gather(values, "ctx", axis=1, tiled=True),
        lax.all_gather(scores, "ctx", axis=1, tiled=True),
    )
    head_items = (
        split_heads(queries),
        split_heads(all_keys),
        split_heads(all_values),
        jnp.moveaxis(all_scores, 2, 0),
        kept_rows,
    )
    heads, log_totals = lax.map(
        partial(attend_head, base=base, causal=causal, key_block=key_block), head_items
    )
    mixed = join_heads(heads).astype(jnp.bfloat16)
    after_attn = residual + jnp.dot(mixed, out_w, preferred_element_type=jnp.float32)
    hidden2 = normalize(after_attn, gains[1], biases[1]).astype(jnp.bfloat16)
    up_part = jnp.dot(hidden2, up_w, preferred_element_type=jnp.float32)
    active = gelu_tanh(up_part).astype(jnp.bfloat16)
    result = after_attn + jnp.dot(active, down_w, preferred_element_type=jnp.float32)
    own_side = (queries, keys, values, scores)
    saved = (
        residual,
        hidden,
        head_items,
        log_totals,
        mixed,
        after_attn,
        hidden2,
        up_part,
        active,
        own_side,
    )
    return (result, saved)


def backward_layer(grad, saved, weights, masks, key_masks):
    qkv_w, score_w, out_w, up_w, down_w, gain, bias = weights
    base, causal, key_block, kept_rows = masks
    (
        residual,
        hidden,
        head_items,
        log_totals,
        mixed,
        after_attn,
        hidden2,
        up_part,
        active,
        own_side,
    ) = saved
    gains = gain.astype(jnp.float32)
    biases = bias.astype(jnp.float32)
    grad_down = grad.astype(jnp.bfloat16)
    grad_active = jnp.einsum("sto,io->sti", grad_down, down_w, preferred_element_type=jnp.float32)
    grad_up = jax.vjp(gelu_tanh, up_part)[1](grad_active)[0].astype(jnp.bfloat16)
    grad_hidden2 = jnp.einsum("stf,df->std", grad_up, up_w, preferred_element_type=jnp.float32)
    late_back = jax.vjp(normalize, after_attn, gains[1], biases[1])[1]
    grad_norm_late, gain_late, bias_late = late_back(grad_hidden2)
    grad_after = grad + grad_norm_late
    grad_attn = grad_after.astype(jnp.bfloat16)
    grad_mixed = jnp.einsum(
        "ste,de->std", grad_attn, out_w, preferred_element_type=jnp.float32
    ).astype(jnp.bfloat16)
    grad_items = head_items + (split_heads(grad_mixed), log_totals)
    grad_queries, inner = lax.map(
        partial(query_side_grads, base=base, causal=causal, key_block=key_block), grad_items
    )
    own_queries, own_keys, own_values, own_scores = own_side
    all_queries, all_grad_mixed = (
        lax.all_gather(own_queries, "ctx", axis=1, tiled=True),
        lax.all_gather(grad_mixed, "ctx", axis=1, tiled=True),
    )
    all_totals, all_inner = (
        lax.all_gather(log_totals, "ctx", axis=2, tiled=True),
        lax.all_gather(inner, "ctx", axis=2, tiled=True),
    )
    key_base, key_causal, key_block_own, kept_all_rows = key_masks
    key_items = (
        split_heads(all_queries),
        split_heads(own_keys),
        split_heads(own_values),
        jnp.moveaxis(own_scores, 2, 0),
        kept_all_rows,
        split_heads(all_grad_mixed),
        all_totals,
        all_inner,
    )
    grad_keys, grad_values, grad_scores = lax.map(
        partial(key_side_grads, base=key_base, causal=key_causal, key_block=key_block_own),
        key_items,
    )
    key_part = join_heads(grad_keys)
    value_part = join_heads(grad_values)
    score_part = jnp.moveaxis(grad_scores, 0, 2)
    grad_qkv = jnp.concatenate([join_heads(grad_queries), key_part, value_part], axis=-1).astype(
        jnp.bfloat16
    )
    grad_score_low = score_part.astype(jnp.bfloat16)
    grad_hidden = jnp.einsum("ste,de->std", grad_qkv, qkv_w, preferred_element_type=jnp.float32)
    grad_hidden = grad_hidden + jnp.einsum(
        "sth,dh->std", grad_score_low, score_w, preferred_element_type=jnp.float32
    )
    early_back = jax.vjp(normalize, residual, gains[0], biases[0])[1]
    grad_norm_early, gain_early, bias_early = early_back(grad_hidden)
    grad_residual = grad_after + grad_norm_early
    inputs = (hidden, mixed, hidden2, active, grad_score_low)
    outputs = (grad_qkv, grad_attn, grad_up, grad_down)
    norms = (jnp.stack([gain_early, gain_late]), jnp.stack([bias_early, bias_late]))
    return (grad_residual, inputs, outputs, norms)


def weight_terms(inputs, outputs, norms):
    all_hidden, all_mixed, all_hidden2, all_active, all_score = (
        lax.all_gather(inputs[0], "ctx", axis=1, tiled=True),
        lax.all_gather(inputs[1], "ctx", axis=1, tiled=True),
        lax.all_gather(inputs[2], "ctx", axis=1, tiled=True),
        lax.all_gather(inputs[3], "ctx", axis=1, tiled=True),
        lax.all_gather(inputs[4], "ctx", axis=1, tiled=True),
    )
    col_qkv, col_attn, col_up, col_down = (
        lax.all_to_all(outputs[0], "ctx", split_axis=2, concat_axis=1, tiled=True),
        lax.all_to_all(outputs[1], "ctx", split_axis=2, concat_axis=1, tiled=True),
        lax.all_to_all(outputs[2], "ctx", split_axis=2, concat_axis=1, tiled=True),
        lax.all_to_all(outputs[3], "ctx", split_axis=2, concat_axis=1, tiled=True),
    )
    gain_total, bias_total = lax.psum((norms[0], norms[1]), "ctx")
    qkv_term = jnp.einsum("std,ste->de", all_hidden, col_qkv, preferred_element_type=jnp.float32)
    score_term = jnp.einsum(
        "std,sth->dh", all_hidden, all_score, preferred_element_type=jnp.float32
    )
    out_term = jnp.einsum("std,ste->de", all_mixed, col_attn, preferred_element_type=jnp.float32)
    up_term = jnp.einsum("std,stf->df", all_hidden2, col_up, preferred_element_type=jnp.float32)
    down_term = jnp.einsum("sti,sto->io", all_active, col_down, preferred_element_type=jnp.float32)
    return (qkv_term, score_term, out_term, up_term, down_term, gain_total, bias_total)


def per_device(
    tokens,
    cotangent,
    kept_blocks,
    picture_starts,
    qkv_weight,
    score_weight,
    out_weight,
    up_weight,
    down_weight,
    norm_gain,
    norm_bias,
):
    local_len = tokens.shape[1]
    whole_len = local_len * lax.axis_size("ctx")
    own_start = lax.axis_index("ctx") * local_len
    masks = build_masks(kept_blocks, picture_starts, own_start, local_len, 0, whole_len)
    key_masks = build_masks(kept_blocks, picture_starts, 0, whole_len, own_start, local_len)
    residual = tokens.astype(jnp.float32)
    kept_weights = []
    saved_all = []
    for layer_index in range(LAYERS):
        rows = (
            lax.all_gather(qkv_weight[layer_index], "fsdp", axis=0, tiled=True),
            lax.all_gather(score_weight[layer_index], "fsdp", axis=0, tiled=True),
            lax.all_gather(out_weight[layer_index], "fsdp", axis=0, tiled=True),
            lax.all_gather(up_weight[layer_index], "fsdp", axis=0, tiled=True),
            lax.all_gather(down_weight[layer_index], "fsdp", axis=0, tiled=True),
            lax.all_gather(norm_gain[layer_index], "fsdp", axis=1, tiled=True),
            lax.all_gather(norm_bias[layer_index], "fsdp", axis=1, tiled=True),
        )
        full_qkv, full_out, full_up, full_down = (
            lax.all_gather(rows[0], "ctx", axis=1, tiled=True),
            lax.all_gather(rows[2], "ctx", axis=1, tiled=True),
            lax.all_gather(rows[3], "ctx", axis=1, tiled=True),
            lax.all_gather(rows[4], "ctx", axis=1, tiled=True),
        )
        weights = (full_qkv, rows[1], full_out, full_up, full_down, rows[5], rows[6])
        kept_weights.append(weights)
        residual, saved = forward_layer(residual, weights, masks)
        saved_all.append(saved)
    grad = cotangent.astype(jnp.float32)
    layer_terms = []
    for layer_index in reversed(range(LAYERS)):
        rows = (
            lax.all_gather(qkv_weight[layer_index], "fsdp", axis=0, tiled=True),
            lax.all_gather(score_weight[layer_index], "fsdp", axis=0, tiled=True),
            lax.all_gather(out_weight[layer_index], "fsdp", axis=0, tiled=True),
            lax.all_gather(up_weight[layer_index], "fsdp", axis=0, tiled=True),
            lax.all_gather(down_weight[layer_index], "fsdp", axis=0, tiled=True),
            lax.all_gather(norm_gain[layer_index], "fsdp", axis=1, tiled=True),
            lax.all_gather(norm_bias[layer_index], "fsdp", axis=1, tiled=True),
        )
        full_qkv, full_out, full_up, full_down = (
            lax.all_gather(rows[0], "ctx", axis=1, tiled=True),
            lax.all_gather(rows[2], "ctx", axis=1, tiled=True),
            lax.all_gather(rows[3], "ctx", axis=1, tiled=True),
            lax.all_gather(rows[4], "ctx", axis=1, tiled=True),
        )
        weights = (full_qkv, rows[1], full_out, full_up, full_down, rows[5], rows[6])
        grad, inputs, outputs, norms = backward_layer(
            grad, saved_all[layer_index], weights, masks, key_masks
        )
        terms = weight_terms(inputs, outputs, norms)
        layer_terms.insert(0, terms)
    stacked = [jnp.stack([entry[number] for entry in layer_terms]) for number in range(7)]
    summed = (
        lax.psum_scatter(
            stacked[0].astype(jnp.bfloat16), "fsdp", scatter_dimension=1, tiled=True
        ).astype(jnp.float32),
        lax.psum_scatter(
            stacked[1].astype(jnp.bfloat16), "fsdp", scatter_dimension=1, tiled=True
        ).astype(jnp.float32),
        lax.psum_scatter(
            stacked[2].astype(jnp.bfloat16), "fsdp", scatter_dimension=1, tiled=True
        ).astype(jnp.float32),
        lax.psum_scatter(
            stacked[3].astype(jnp.bfloat16), "fsdp", scatter_dimension=1, tiled=True
        ).astype(jnp.float32),
        lax.psum_scatter(
            stacked[4].astype(jnp.bfloat16), "fsdp", scatter_dimension=1, tiled=True
        ).astype(jnp.float32),
        lax.psum_scatter(
            stacked[5].astype(jnp.bfloat16), "fsdp", scatter_dimension=2, tiled=True
        ).astype(jnp.float32),
        lax.psum_scatter(
            stacked[6].astype(jnp.bfloat16), "fsdp", scatter_dimension=2, tiled=True
        ).astype(jnp.float32),
    )
    return (
        residual,
        grad,
        summed[0],
        summed[1],
        summed[2],
        summed[3],
        summed[4],
        summed[5],
        summed[6],
    )


D = 768
FF = 3072
HALF = 384
TOK = 512
SEQ = 1024
ROWS = 48
DROWS = 192
NEG = -1e30
FULL = 58 << 20
F32 = jnp.float32
BF16 = jnp.bfloat16
VM = pl.BlockSpec(memory_space=pltpu.VMEM)
HB = pl.BlockSpec(memory_space=pltpu.HBM)
SM = pl.BlockSpec(memory_space=pltpu.SMEM)


def nn(a, b):
    return lax.dot_general(a, b, (((1,), (0,)), ((), ())), preferred_element_type=F32)


def nt(a, b):
    return lax.dot_general(a, b, (((1,), (1,)), ((), ())), preferred_element_type=F32)


def tn(a, b):
    return lax.dot_general(a, b, (((0,), (0,)), ((), ())), preferred_element_type=F32)


def sds(shape, dtype):
    return jax.ShapeDtypeStruct(shape, dtype)


COST = dict(qkv=7, attend=12, ffn=20, down_back=6, up_back=10, ffn_grad=11)
COST |= dict(attend_back=16, qkv_grad=8, qkv_back=9, cross=4, own=4)


def duration(us):
    flops = int(us * 1.15e9)
    return pl.CostEstimate(flops=flops, bytes_accessed=1 << 20, transcendentals=0)


def kernel_call(body, ins, in_specs, outs, out_specs, scratch, name, limit=None):
    held = [v for v, spec in zip((*ins, *outs), (*in_specs, *out_specs)) if spec is VM]
    held += [b for b in scratch if getattr(b, "memory_space", None) == pltpu.VMEM]
    held = sum(math.prod(v.shape) * jnp.dtype(v.dtype).itemsize for v in held)
    return pl.pallas_call(
        body,
        out_shape=tuple(outs),
        in_specs=in_specs,
        out_specs=tuple(out_specs),
        scratch_shapes=scratch,
        compiler_params=pltpu.CompilerParams(vmem_limit_bytes=FULL),
        cost_estimate=duration(COST[name]),
        name=name,
    )(*ins)


def aligned(v, m):
    return pl.multiple_of(v, m)


def layer_norm_parts(x):
    centered = x - jnp.mean(x, axis=-1, keepdims=True)
    variance = jnp.mean(centered * centered, axis=-1, keepdims=True)
    scale = lax.rsqrt(variance + 1e-05)
    return centered * scale, scale


def split_blocks(src, keep, send, c, rows):
    for b in range(8):
        keep[b] = src[pl.ds(aligned((2 * b + c) * rows, 16), rows), :]
        send[b] = src[pl.ds(aligned((2 * b + 1 - c) * rows, 16), rows), :]


def visit(f, y, arrays, n, fns):
    if len(arrays) == 16:
        for q in range(8):
            device = (f & 3) ^ ((q & 1) * 2 + (q >> 2))
            for part, fn in enumerate(fns):
                fn(arrays[part * 8 + q].at[:, n], device, y ^ ((q >> 1) & 1))
        return
    for pxx in range(2):
        for pc in range(2):
            for y2 in range(2):
                for part, fn in enumerate(fns):
                    device = pxx * 2 + ((f & 1) ^ pc)
                    fn(arrays[pc].at[:, pxx, y2, part, n], device, y2)


QKV_W = pltpu.VMEM((6, 4, 4, ROWS, HALF), BF16)
OUT_W = pltpu.VMEM((2, 4, 4, ROWS, HALF), BF16)
UP_W = pltpu.VMEM((4, 4, 4, ROWS, D), BF16)
DOWN_W = pltpu.VMEM((2, 4, 4, 4, ROWS, HALF), BF16)


def fetch_qkv(f, y, parts, w, sem):
    def put(src, cols, group, device, y2):
        dst = w.at[y2 * 3 + group, :, device]
        pltpu.make_async_copy(src.at[:, :, cols], dst, sem).start()

    def fetch_a(src, device, y2):
        put(src, pl.ds(0, HALF), 0, device, y2)
        put(src, pl.ds(HALF, HALF), 1, device, y2)

    def fetch_b(src, device, y2):
        put(src, pl.ds(0, HALF), 2, device, y2)

    visit(f, y, parts, 0, (fetch_a, fetch_b))


def fetch_out(f, y, parts, wo, sem):
    def fetch(src, device, y2):
        dst = wo.at[y2, :, device]
        pltpu.make_async_copy(src.at[:, :, pl.ds(HALF, HALF)], dst, sem).start()

    visit(f, y, parts, 0, (lambda *_: None, fetch))


def fetch_up(f, y, parts, wu, sem):
    def fetch(part):
        def copy(src, device, y2):
            pltpu.make_async_copy(src, wu.at[y2 * 2 + part, :, device], sem).start()

        return copy

    visit(f, y, parts, 0, (fetch(0), fetch(1)))


def fetch_down(f, y, parts, wd, sem):
    def fetch(part):
        def copy(src, device, y2):
            for k in range(2):
                dst = wd.at[y2, :, device, part * 2 + k]
                pltpu.make_async_copy(src.at[:, :, pl.ds(k * HALF, HALF)], dst, sem).start()

        return copy

    visit(f, y, parts, 1, (fetch(0), fetch(1)))


def arrived(w, sem):
    pltpu.make_async_copy(w, w, sem).wait()


def load(pairs, sem):
    copies = [pltpu.make_async_copy(a, b, sem.at[k]) for k, (a, b) in enumerate(pairs)]
    for copy in copies:
        copy.start()
    return copies


def qkv_kernel(idx, res, gb, sw0, sw1, *refs):
    parts, refs = refs[:-8], refs[-8:]
    keep, send, htk, hts, w, h, ht, sem = refs
    f, y, c = idx[0], idx[1], idx[2]

    fetch_qkv(f, y, parts, w, sem)
    gain, bias = gb[0:1, :], gb[2:3, :]
    for t in range(4):
        rows = pl.ds(t * 128, 128)
        n, _ = layer_norm_parts(res[rows, :])
        v = n * gain + bias
        h[rows, :] = v.astype(BF16)
        ht[:, rows] = v.T.astype(BF16)
    split_blocks(ht, htk, hts, c, ROWS)
    pltpu.make_async_copy(w, w, sem).wait()

    def tile(t, carry):
        rows = pl.ds(aligned(t * 256, 256), 256)
        hv = h[rows, :]
        for j in range(3):
            cols = pl.ds(j * HALF, HALF)
            keep[rows, cols] = nn(hv, w[2 * j + c].reshape(D, HALF)).astype(BF16)
            send[rows, cols] = nn(hv, w[2 * j + 1 - c].reshape(D, HALF)).astype(BF16)
        keep[rows, pl.ds(1152, 128)] = nt(hv, sw0[...]).astype(BF16)
        send[rows, pl.ds(1152, 128)] = nt(hv, sw1[...]).astype(BF16)
        return carry

    lax.fori_loop(0, 2, tile, 0)


def qkv_call(idx, res, gb, sw0, sw1, w):
    return kernel_call(
        qkv_kernel,
        [idx, res, gb, sw0, sw1, *w],
        [SM, VM, VM, VM, VM] + [HB] * len(w),
        [
            sds((TOK, 1280), BF16),
            sds((TOK, 1280), BF16),
            sds((8, ROWS, TOK), BF16),
            sds((8, ROWS, TOK), BF16),
        ],
        [VM, VM, VM, VM],
        [
            QKV_W,
            pltpu.VMEM((TOK, D), BF16),
            pltpu.VMEM((D, TOK), BF16),
            pltpu.SemaphoreType.DMA,
        ],
        "qkv",
        FULL,
    )


def load_halves(pairs, c, pad, sem):
    copies = []
    for number, (own, other, dst) in enumerate(pairs):
        for k, (src, half) in enumerate(((own, c), (other, 1 - c))):
            rows = pl.ds(aligned(pad + half * TOK, 128), TOK)
            copy = pltpu.make_async_copy(src, dst.at[rows, :], sem.at[2 * number + k])
            copy.start()
            copies.append(copy)
    return copies


def mask_tiles(tab):
    key = lax.broadcasted_iota(jnp.int32, (BLK, BLK), 0)
    query = lax.broadcasted_iota(jnp.int32, (BLK, BLK), 1)
    gap = query - key
    tab[0] = jnp.where((gap >= 0) & (gap < WINDOW), 0.0, NEG)
    tab[1] = jnp.where(gap >= 0, 0.0, NEG)
    tab[2] = jnp.zeros((BLK, BLK), F32)
    tab[3] = jnp.where(gap + BLK < WINDOW, 0.0, NEG)
    tab[4] = jnp.full((BLK, BLK), NEG, F32)


def log_sigmoid_of(v):
    return -(jnp.maximum(-v, 0.0) + jnp.log1p(jnp.exp(-jnp.abs(v))))


def picture_flags(pics, i):
    p0, p1 = pics[0] // BLK, pics[1] // BLK
    starts = (p0 == i) | (p1 == i)
    follows = (p0 == i - 1) | (p1 == i - 1)
    return starts, follows


def split_log_sigmoid(s, la):
    value = log_sigmoid_of(s[:, 1152:1280].astype(F32))
    lane = lax.broadcasted_iota(jnp.int32, value.shape, 1)
    value = jnp.where(lane < 6, value, 0.0)
    high = value.astype(BF16).astype(F32)
    middle = (value - high).astype(BF16).astype(F32)
    low = value - high - middle
    la[...] = (high + pltpu.roll(middle, 8, 1) + pltpu.roll(low, 16, 1)).astype(BF16)


def pair_logits(s, la, tab, kept, i, pair, blocks, starts, follows):
    lane = lax.broadcasted_iota(jnp.int32, (BLK, BLK), 1)
    first = lane < 64
    base = aligned(i * BLK, BLK)
    cols = pair * BLK
    q = s[pl.ds(base + BLK, BLK), pl.ds(cols, BLK)] * jnp.asarray(HEAD_DIM**-0.5, BF16)
    zero = jnp.zeros_like(q)
    q = jnp.concatenate([jnp.where(first, q, zero), jnp.where(first, zero, q)], axis=0)
    terms = [((lane & 7) == 2 * pair + odd) & (lane < 24) for odd in range(2)]
    ones = jnp.concatenate([jnp.where(t, 1.0, 0.0) for t in terms], axis=0).astype(BF16)
    near = pl.ds(base, blocks * BLK)
    chosen = [kept[2 * pair + odd, i] for odd in range(2)]
    far = [pl.ds(aligned((b + 1) * BLK, BLK), BLK) for b in chosen]

    def rows_of(cols):
        far_rows = jnp.where(first, s[far[0], cols], s[far[1], cols])
        return jnp.concatenate([s[near, cols], far_rows], axis=0)

    k = rows_of(pl.ds(HALF + cols, BLK))
    v = rows_of(pl.ds(2 * HALF + cols, BLK))
    bias = jnp.where(terms[0], la[far[0], :], la[far[1], :])
    bias = jnp.concatenate([la[near, :], bias], axis=0)
    logits = nt(jnp.concatenate([k, bias], axis=1), jnp.concatenate([q, ones], axis=1))
    before, here, beyond = [], [], []
    for block in chosen:
        before.append(tab[jnp.where(i == 0, 4, jnp.where(follows | (block == i - 1), 2, 3))])
        here.append(tab[jnp.where(starts | follows, 2, jnp.where(block == i, 1, 0))])
        beyond.append(jnp.full((1, BLK), jnp.where(block < i - 1, 0.0, NEG), F32))
    parts = [
        logits[0:BLK] + jnp.concatenate(before, axis=1),
        logits[BLK : 2 * BLK] + jnp.concatenate(here, axis=1),
    ]
    if blocks == 3:
        parts.append(logits[2 * BLK : 3 * BLK])
    parts.append(logits[blocks * BLK :] + jnp.concatenate(beyond, axis=1))
    return jnp.concatenate(parts, axis=0), q, k, v, near, far, first


def block_probs(s, ls, tab, kept, i, h, blocks, starts, follows):
    pair, odd = h // 2, h % 2
    lane = lax.broadcasted_iota(jnp.int32, (BLK, BLK), 1)
    mine = (lane >= 64) if odd else (lane < 64)
    base = aligned(i * BLK, BLK)
    cols = pair * BLK
    q = s[pl.ds(base + BLK, BLK), pl.ds(cols, BLK)] * jnp.asarray(HEAD_DIM**-0.5, BF16)
    q = jnp.where(mine, q, jnp.zeros_like(q))
    near, chosen = pl.ds(base, blocks * BLK), kept[h, i]
    far = pl.ds(aligned((chosen + 1) * BLK, BLK), BLK)
    kcols, vcols = pl.ds(HALF + cols, BLK), pl.ds(2 * HALF + cols, BLK)
    k = jnp.concatenate([s[near, kcols], s[far, kcols]], axis=0)
    v = jnp.concatenate([s[near, vcols], s[far, vcols]], axis=0)
    before = jnp.where(i == 0, 4, jnp.where(follows | (chosen == i - 1), 2, 3))
    here = jnp.where(starts | follows, 2, jnp.where(chosen == i, 1, 0))
    beyond = jnp.where(chosen < i - 1, 0.0, NEG).astype(F32)
    logits = nt(k, q)
    parts = [
        logits[0:BLK] + (tab[before] + ls[pl.ds(base, BLK), h : h + 1]),
        logits[BLK : 2 * BLK] + (tab[here] + ls[pl.ds(base + BLK, BLK), h : h + 1]),
    ]
    if blocks == 3:
        parts.append(logits[2 * BLK : 3 * BLK] + ls[pl.ds(base + 2 * BLK, BLK), h : h + 1])
    parts.append(logits[blocks * BLK :] + (ls[far, h : h + 1] + beyond))
    logits = jnp.concatenate(parts, axis=0)
    largest = jnp.max(logits, axis=0, keepdims=True)
    weights = jnp.exp(logits - largest)
    total = jnp.sum(weights, axis=0, keepdims=True)
    probs = weights * (1.0 / total)
    return probs, v, mine, largest + jnp.log(total)


def attend_kernel(idx, kept, pics, own, other, okeep, osend, lse, s, ls, o, tab, sem):
    c = idx[2]
    copies = load_halves([(own, other, s)], c, BLK, sem)
    s[0:BLK, :] = jnp.zeros((BLK, 1280), BF16)
    mask_tiles(tab)
    for copy in copies:
        copy.wait()
    ls[...] = log_sigmoid_of(s[:, 1152:1280].astype(F32))
    lse[...] = jnp.zeros_like(lse)

    def step(i, carry):
        starts, follows = picture_flags(pics, i)

        def run(blocks):
            rows = pl.ds(aligned(i * BLK, BLK), BLK)
            for pair in range(3):
                halves = []
                for odd in range(2):
                    h = 2 * pair + odd
                    probs, v, mine, logs = block_probs(
                        s, ls, tab, kept, i, h, blocks, starts, follows
                    )
                    halves.append(tn(probs.astype(BF16), v))
                    lse[h : h + 1, rows] = logs
                o[rows, pl.ds(pair * BLK, BLK)] = jnp.where(mine, halves[1], halves[0]).astype(BF16)

        @pl.when(starts)
        def _():
            run(3)

        @pl.when(jnp.logical_not(starts))
        def _():
            run(2)

        return carry

    lax.fori_loop(0, 8, step, 0)
    okeep[...] = o[pl.ds(aligned(c * TOK, TOK), TOK), :]
    osend[...] = o[pl.ds(aligned((1 - c) * TOK, TOK), TOK), :]


def attend_call(idx, kept, pics, own, other):
    return kernel_call(
        attend_kernel,
        [idx, kept, pics, own, other],
        [SM, SM, SM, HB, HB],
        [sds((TOK, HALF), BF16), sds((TOK, HALF), BF16), sds((8, SEQ), F32)],
        [VM, VM, VM],
        [
            pltpu.VMEM((SEQ + BLK, 1280), BF16),
            pltpu.VMEM((SEQ + BLK, BLK), F32),
            pltpu.VMEM((SEQ, HALF), BF16),
            pltpu.VMEM((5, BLK, BLK), F32),
            pltpu.SemaphoreType.DMA((2,)),
        ],
        "attend",
        FULL,
    )


def ffn_kernel(idx, res_in, mk, mr, gb, *refs):
    qo, ffn, refs = refs[:16], refs[16:-23], refs[-23:]
    aa, new, low, mtk, mts, htk, hts, slope_o, atk, ats = refs[:10]
    wo, wu, wd, res, h, ht, act, slope, at, sem, isem, osem, asem = refs[10:]
    f, y, c = idx[0], idx[1], idx[2]
    (res_copy,) = load([(res_in, res)], isem)
    fetch_out(f, y, qo, wo, sem.at[0])
    fetch_up(f, y, ffn, wu, sem.at[1])
    fetch_down(f, y, ffn, wd, sem.at[2])
    ht[pl.ds(aligned(c * HALF, HALF), HALF), :] = mk[...].T
    ht[pl.ds(aligned((1 - c) * HALF, HALF), HALF), :] = mr[...].T
    split_blocks(ht, mtk, mts, c, ROWS)
    arrived(wo, sem.at[0])
    res_copy.wait()
    gain, bias = gb[1:2, :], gb[3:4, :]
    mine, theirs = pl.ds(c * 2, 2), pl.ds((1 - c) * 2, 2)
    for half in range(2):
        cols = pl.ds(half * HALF, HALF)
        part = nn(mk[...], wo[half, mine].reshape(HALF, HALF))
        part += nn(mr[...], wo[half, theirs].reshape(HALF, HALF))
        aa[:, cols] = res[:, cols] + part
    for t in range(4):
        rows = pl.ds(t * 128, 128)
        n, _ = layer_norm_parts(aa[rows, :])
        v = (n * gain + bias).astype(BF16)
        h[rows, :] = v
        ht[:, rows] = v.T
    split_blocks(ht, htk, hts, c, ROWS)
    arrived(wu, sem.at[1])
    outs = []
    for g in range(4):

        def tile(t, carry):
            rows = pl.ds(aligned(t * 256, 256), 256)
            u = nn(h[rows, :], wu[g].reshape(D, D))
            square = u * u
            th = jnp.tanh(u * (0.7978845608 + (0.7978845608 * 0.044715) * square))
            share = 0.5 + 0.5 * th
            a = u * share
            bend = 2 * 0.7978845608 + (6 * 0.7978845608 * 0.044715) * square
            d = share + a * (1.0 - share) * bend
            cols = pl.ds(g * D, D)
            a = a.astype(BF16)
            act[rows, cols] = a
            slope[rows, cols] = d.astype(BF16)
            at[cols, rows] = a.T
            return carry

        lax.fori_loop(0, 2, tile, 0)
        cols = pl.ds(g * D, D)
        outs.append(pltpu.make_async_copy(slope.at[:, cols], slope_o.at[:, cols], osem.at[g]))
        outs[-1].start()
        for b in (2 * g, 2 * g + 1):
            for k, (dst, row) in enumerate(((atk, 2 * b + c), (ats, 2 * b + 1 - c))):
                src = at.at[pl.ds(aligned(row * DROWS, 16), DROWS), :]
                outs.append(pltpu.make_async_copy(src, dst.at[b], asem.at[2 * b + k]))
                outs[-1].start()
    arrived(wd, sem.at[2])

    def tile(t, carry):
        rows = pl.ds(aligned(t * 256, 256), 256)
        for half in range(2):
            cols = pl.ds(half * HALF, HALF)
            total = aa[rows, cols] + nn(act[rows, :], wd[half].reshape(FF, HALF))
            new[rows, cols] = total
            low[rows, cols] = total.astype(BF16)
        return carry

    lax.fori_loop(0, 2, tile, 0)
    for copy in outs:
        copy.wait()


def ffn_call(idx, res, mk, mr, gb, qo, ffn):
    return kernel_call(
        ffn_kernel,
        [idx, res, mk, mr, gb, *qo, *ffn],
        [SM, HB, VM, VM, VM] + [HB] * (len(qo) + len(ffn)),
        [
            sds((TOK, D), F32),
            sds((TOK, D), F32),
            sds((TOK, D), BF16),
            sds((8, ROWS, TOK), BF16),
            sds((8, ROWS, TOK), BF16),
            sds((8, ROWS, TOK), BF16),
            sds((8, ROWS, TOK), BF16),
            sds((TOK, FF), BF16),
            sds((8, DROWS, TOK), BF16),
            sds((8, DROWS, TOK), BF16),
        ],
        [VM] * 7 + [HB] * 3,
        [
            OUT_W,
            UP_W,
            DOWN_W,
            pltpu.VMEM((TOK, D), F32),
            pltpu.VMEM((TOK, D), BF16),
            pltpu.VMEM((D, TOK), BF16),
            pltpu.VMEM((TOK, FF), BF16),
            pltpu.VMEM((TOK, FF), BF16),
            pltpu.VMEM((FF, TOK), BF16),
            pltpu.SemaphoreType.DMA((3,)),
            pltpu.SemaphoreType.DMA((1,)),
            pltpu.SemaphoreType.DMA((4,)),
            pltpu.SemaphoreType.DMA((16,)),
        ],
        "ffn",
        FULL,
    )


def down_back_kernel(idx, grad, slope_in, *refs):
    parts, refs = refs[:-5], refs[-5:]
    gu, wd, slope, sem, isem = refs
    copies = load([(slope_in.at[:, pl.ds(g * D, D)], slope.at[g]) for g in range(4)], isem)
    fetch_down(idx[0], idx[1], parts, wd, sem)
    arrived(wd, sem)
    for g in range(4):
        copies[g].wait()
        left = wd[0, g].reshape(D, HALF)
        right = wd[1, g].reshape(D, HALF)

        def tile(t, carry):
            rows = pl.ds(aligned(t * 256, 256), 256)
            part = nt(grad[rows, 0:HALF], left) + nt(grad[rows, HALF:D], right)
            gu[rows, pl.ds(g * D, D)] = (part * slope[g, rows, :].astype(F32)).astype(BF16)
            return carry

        lax.fori_loop(0, 2, tile, 0)


def down_back_call(idx, grad, slope, w):
    return kernel_call(
        down_back_kernel,
        [idx, grad, slope, *w],
        [SM, VM, HB] + [HB] * len(w),
        [sds((TOK, FF), BF16)],
        [VM],
        [
            DOWN_W,
            pltpu.VMEM((4, TOK, D), BF16),
            pltpu.SemaphoreType.DMA,
            pltpu.SemaphoreType.DMA((4,)),
        ],
        "down_back",
    )[0]


def norm_back(x, grad_out, gain):
    n, scale = layer_norm_parts(x)
    e = grad_out * gain
    back = scale * (
        e - jnp.mean(e, axis=-1, keepdims=True) - n * jnp.mean(e * n, axis=-1, keepdims=True)
    )
    gain_part = jnp.sum(grad_out * n, axis=0, keepdims=True)
    bias_part = jnp.sum(grad_out, axis=0, keepdims=True)
    return back, gain_part, bias_part


def up_back_kernel(idx, grad_in, gu, aa_in, gb, *refs):
    qo, ffn, refs = refs[:16], refs[16:-12], refs[-12:]
    ga, gat, gmk, gms, nrm, wu, wo, grad, aa, gh, sem, isem = refs
    f, y, c = idx[0], idx[1], idx[2]
    fetch_up(f, y, ffn, wu, sem.at[0])
    copies = load([(aa_in, aa), (grad_in, grad)], isem)
    fetch_out(f, y, qo, wo, sem.at[1])
    nrm[...] = jnp.zeros_like(nrm)
    gain = gb[1:2, :]
    mine, theirs = pl.ds(c * 2, 2), pl.ds((1 - c) * 2, 2)
    arrived(wu, sem.at[0])

    def wide(t, carry):
        rows = pl.ds(aligned(t * 256, 256), 256)
        total = nt(gu[rows, 0:D], wu[0].reshape(D, D))
        for g in range(1, 4):
            total += nt(gu[rows, pl.ds(g * D, D)], wu[g].reshape(D, D))
        gh[rows, :] = total
        return carry

    lax.fori_loop(0, 2, wide, 0)
    for copy in copies:
        copy.wait()

    def tile(t, carry):
        rows = pl.ds(aligned(t * 128, 128), 128)
        back, gain_part, bias_part = norm_back(aa[rows, :], gh[rows, :], gain)
        total = grad[rows, :] + back
        ga[rows, :] = total
        gat[rows, :] = total.astype(BF16)
        nrm[0:1, :] += gain_part
        nrm[1:2, :] += bias_part
        return carry

    lax.fori_loop(0, 4, tile, 0)
    arrived(wo, sem.at[1])
    for dst, part in ((gmk, mine), (gms, theirs)):
        dst[...] = (
            nt(gat[:, 0:HALF], wo[0, part].reshape(HALF, HALF))
            + nt(gat[:, HALF:D], wo[1, part].reshape(HALF, HALF))
        ).astype(BF16)


def up_back_call(idx, grad, gu, aa, gb, qo, ffn):
    return kernel_call(
        up_back_kernel,
        [idx, grad, gu, aa, gb, *qo, *ffn],
        [SM, HB, VM, HB, VM] + [HB] * (len(qo) + len(ffn)),
        [
            sds((TOK, D), F32),
            sds((TOK, D), BF16),
            sds((TOK, HALF), BF16),
            sds((TOK, HALF), BF16),
            sds((8, D), F32),
        ],
        [VM] * 5,
        [
            UP_W,
            OUT_W,
            pltpu.VMEM((TOK, D), F32),
            pltpu.VMEM((TOK, D), F32),
            pltpu.VMEM((TOK, D), F32),
            pltpu.SemaphoreType.DMA((2,)),
            pltpu.SemaphoreType.DMA((2,)),
        ],
        "up_back",
    )


def attend_back_kernel(
    idx, kept, pics, lse, own, other, gown, gother, down_, doth, s, g, la, d, dk, dv, ds, tab, sem
):
    c = idx[2]
    copies = load_halves([(own, other, s)], c, BLK, sem)
    copies += load_halves([(gown, gother, g)], c, 0, sem.at[pl.ds(2, 2)])
    s[0:BLK, :] = jnp.zeros((BLK, 1280), BF16)
    mask_tiles(tab)
    dk[...] = jnp.zeros_like(dk)
    dv[...] = jnp.zeros_like(dv)
    ds[...] = jnp.zeros_like(ds)
    for copy in copies:
        copy.wait()
    split_log_sigmoid(s, la)
    lane = lax.broadcasted_iota(jnp.int32, (BLK, BLK), 1)

    def step(i, carry):
        starts, follows = picture_flags(pics, i)

        def run(blocks):
            rows = pl.ds(aligned(i * BLK, BLK), BLK)
            cut = blocks * BLK
            for pair in range(3):
                cols = pl.ds(pair * BLK, BLK)
                logits, q, k, v, near, far, first = pair_logits(
                    s, la, tab, kept, i, pair, blocks, starts, follows
                )
                logs = [lse[2 * pair + odd : 2 * pair + odd + 1, rows] for odd in range(2)]
                probs = jnp.exp(logits - jnp.concatenate(logs, axis=1))
                gm = g[rows, cols]
                zero = jnp.zeros_like(gm)
                gm = jnp.concatenate([jnp.where(first, gm, zero), jnp.where(first, zero, gm)], axis=0)
                gprob = nt(v, gm)
                inner = jnp.sum(probs * gprob, axis=0, keepdims=True)
                gl = (probs * (gprob - inner)).astype(BF16)
                gv = nn(probs.astype(BF16), gm)
                heads = [jnp.where(lane == 2 * pair + odd, 1.0, 0.0) for odd in range(2)]
                heads = jnp.concatenate(heads, axis=0).astype(BF16)
                gk = nn(gl, jnp.concatenate([q, heads], axis=1))
                dv[near, cols] += gv[:cut]
                dk[near, cols] += gk[:cut, :BLK]
                ds[near, :] += gk[:cut, BLK:]
                for odd in range(2):
                    mine = jnp.logical_not(first) if odd else first
                    dv[far[odd], cols] += jnp.where(mine, gv[cut:], 0.0)
                    dk[far[odd], cols] += jnp.where(mine, gk[cut:, :BLK], 0.0)
                    ds[far[odd], :] += jnp.where(lane == 2 * pair + odd, gk[cut:, BLK:], 0.0)
                dq = tn(gl, k)
                dq = jnp.where(first, dq[:BLK], dq[BLK:]) * (HEAD_DIM**-0.5)
                d[rows, cols] = dq.astype(BF16)

        @pl.when(starts)
        def _():
            run(3)

        @pl.when(jnp.logical_not(starts))
        def _():
            run(2)

        return carry

    lax.fori_loop(0, 8, step, 0)
    keys = pl.ds(BLK, SEQ)
    d[:, HALF : 2 * HALF] = dk[keys, :].astype(BF16)
    d[:, 2 * HALF : 3 * HALF] = dv[keys, :].astype(BF16)
    back = ds[keys, :] * jax.nn.sigmoid(-s[keys, 1152:1280].astype(F32))
    d[:, 1152:1280] = back.astype(BF16)
    down_[...] = d[pl.ds(aligned(c * TOK, TOK), TOK), :]
    doth[...] = d[pl.ds(aligned((1 - c) * TOK, TOK), TOK), :]


def attend_back_call(idx, kept, pics, lse, own, other, gown, gother):
    return kernel_call(
        attend_back_kernel,
        [idx, kept, pics, lse, own, other, gown, gother],
        [SM, SM, SM, VM, HB, HB, HB, HB],
        [sds((TOK, 1280), BF16), sds((TOK, 1280), BF16)],
        [VM, VM],
        [
            pltpu.VMEM((SEQ + BLK, 1280), BF16),
            pltpu.VMEM((SEQ, HALF), BF16),
            pltpu.VMEM((SEQ + BLK, BLK), BF16),
            pltpu.VMEM((SEQ, 1280), BF16),
            pltpu.VMEM((SEQ + BLK, HALF), F32),
            pltpu.VMEM((SEQ + BLK, HALF), F32),
            pltpu.VMEM((SEQ + BLK, BLK), F32),
            pltpu.VMEM((5, BLK, BLK), F32),
            pltpu.SemaphoreType.DMA((4,)),
        ],
        "attend_back",
    )


def qkv_back_kernel(idx, ga_in, down_, dr, res_in, gb, sw0, sw1, *refs):
    parts, refs = refs[:-9], refs[-9:]
    gout, glow, nrm, w, ga, res, gh, sem, isem = refs
    c = idx[2]
    fetch_qkv(idx[0], idx[1], parts, w, sem)
    copies = load([(res_in, res), (ga_in, ga)], isem)
    nrm[...] = jnp.zeros_like(nrm)
    gain = gb[0:1, :]
    arrived(w, sem)

    def wide(t, carry):
        rows = pl.ds(aligned(t * 256, 256), 256)
        total = nn(down_[rows, 1152:1280], sw0[...]) + nn(dr[rows, 1152:1280], sw1[...])
        for j in range(3):
            cols = pl.ds(j * HALF, HALF)
            total += nt(down_[rows, cols], w[2 * j + c].reshape(D, HALF))
            total += nt(dr[rows, cols], w[2 * j + 1 - c].reshape(D, HALF))
        gh[rows, :] = total
        return carry

    lax.fori_loop(0, 2, wide, 0)
    for copy in copies:
        copy.wait()

    def tile(t, carry):
        rows = pl.ds(aligned(t * 128, 128), 128)
        back, gain_part, bias_part = norm_back(res[rows, :], gh[rows, :], gain)
        total = ga[rows, :] + back
        gout[rows, :] = total
        glow[rows, :] = total.astype(BF16)
        nrm[0:1, :] += gain_part
        nrm[1:2, :] += bias_part
        return carry

    lax.fori_loop(0, 4, tile, 0)


def qkv_back_call(idx, ga, down_, dr, res, gb, sw0, sw1, w):
    return kernel_call(
        qkv_back_kernel,
        [idx, ga, down_, dr, res, gb, sw0, sw1, *w],
        [SM, HB, VM, VM, HB, VM, VM, VM] + [HB] * len(w),
        [sds((TOK, D), F32), sds((TOK, D), BF16), sds((8, D), F32)],
        [VM, VM, VM],
        [
            QKV_W,
            pltpu.VMEM((TOK, D), F32),
            pltpu.VMEM((TOK, D), F32),
            pltpu.VMEM((TOK, D), F32),
            pltpu.SemaphoreType.DMA,
            pltpu.SemaphoreType.DMA((2,)),
        ],
        "qkv_back",
    )


def scatter_rows(src, f, rows, offset, pyy, portion, outs, n, cols):
    if len(outs) == 1:
        for block in range(8):
            value = src[pl.ds(block * rows + offset, ROWS), :]
            outs[0][2 * block + pyy, portion, n, :, cols] = value
        return
    ka, sa, kb, sb = outs
    for pxx in range(2):
        for pz in range(4):
            block = (f >> 1) ^ (pz * 2 + pxx)
            value = src[pl.ds(aligned(block * rows + offset, 16), ROWS), :]
            if portion == 0:
                (sa if pxx else ka)[pyy, pz, n, :, cols] = value
            else:
                (sb if pyy else kb)[pxx, pz, n, :, cols] = value


def up_grads_into(f, y, xk, xr, gk, gr, outs, tmp):
    for portion in range(2):
        for pyy in range(2):
            cols = pl.ds(aligned((y ^ pyy) * 1536 + portion * D, 128), D)
            slot = portion * 2 + pyy
            tmp[slot] = (nn(xk[...], gk[:, cols]) + nn(xr[...], gr[:, cols])).astype(BF16)
            scatter_rows(tmp.at[slot], f, ROWS, 0, pyy, portion, outs, 0, pl.ds(0, D))


def down_grads_into(f, y, ak, ar, dk, dr, outs, tmp):
    for pyy in range(2):
        cols = pl.ds(aligned((y ^ pyy) * HALF, 128), HALF)

        def tile(t, carry):
            rows = pl.ds(aligned(t * HALF, HALF), HALF)
            value = nn(ak[rows, :], dk[:, cols]) + nn(ar[rows, :], dr[:, cols])
            tmp[pyy, rows, :] = value.astype(BF16)
            return carry

        lax.fori_loop(0, 4, tile, 0)
        for portion in range(2):
            for k in range(2):
                offset, half = (portion * 2 + k) * ROWS, pl.ds(k * HALF, HALF)
                scatter_rows(tmp.at[pyy], f, DROWS, offset, pyy, portion, outs, 1, half)


def ffn_grad_kernel(count, idx, xk, xr, gk, gr, ak, ar, dk, dr, *refs):
    outs, tmp, tmp2 = refs[:count], refs[count], refs[count + 1]
    f, y = (idx[0], idx[1]) if count == 4 else (0, 0)
    up_grads_into(f, y, xk, xr, gk, gr, outs, tmp)
    down_grads_into(f, y, ak, ar, dk, dr, outs, tmp2)


def ffn_grad_call(idx, xk, xr, gk, gr, ak, ar, dk, dr, by_position):
    ins = [idx] + [v.reshape(HALF, TOK) for v in (xk, xr)] + [gk, gr]
    ins += [v.reshape(4 * HALF, TOK) for v in (ak, ar)] + [dk, dr]
    outs = [sds((16, 2, 2, ROWS, D), BF16)]
    if by_position:
        outs = [sds((2, 4, 2, ROWS, D), BF16)] * 4
    return kernel_call(
        partial(ffn_grad_kernel, len(outs)),
        ins,
        [SM] + [VM] * 8,
        outs,
        [VM] * len(outs),
        [pltpu.VMEM((4, HALF, D), BF16), pltpu.VMEM((2, 4 * HALF, HALF), BF16)],
        "ffn_grad",
    )


def qkv_grad_kernel(
    idx, xk, xr, mk, mr, d00, d01, d10, d11, gk, gr, ka, sa, kb, sb, sc, dy, tmp, tsc, sem
):
    outs = (ka, sa, kb, sb)
    f, y, c = idx[0], idx[1], idx[2]
    copies = []
    for tok, pair in enumerate(((d00, d01), (d10, d11))):
        for k, src in enumerate(pair):
            for j in range(3):
                copy = pltpu.make_async_copy(
                    src.at[:, pl.ds(j * HALF, HALF)],
                    dy.at[tok, 2 * j + (c ^ k)],
                    sem.at[tok * 6 + k * 3 + j],
                )
                copy.start()
                copies.append(copy)
    for tok, pair in enumerate(((d00, d01), (d10, d11))):
        for k, src in enumerate(pair):
            copy = pltpu.make_async_copy(
                src.at[:, pl.ds(1152, 128)], tsc.at[tok * 2 + k], sem.at[12 + tok * 2 + k]
            )
            copy.start()
            copies.append(copy)
    for copy in copies:
        copy.wait()
    for pyy in range(2):
        y2 = y ^ pyy
        for part in range(4):
            portion, side = part // 2, part % 2
            cols = pl.ds(side * HALF, HALF)
            if part < 3:
                g = y2 * 3 + part
                value = nn(xk[...], dy[0, g]) + nn(xr[...], dy[1, g])
            else:
                oc = pl.ds(aligned(y2 * HALF, 128), HALF)
                value = nn(mk[...], gk[:, oc]) + nn(mr[...], gr[:, oc])
            tmp[portion * 2 + pyy, :, cols] = value.astype(BF16)
        for portion in range(2):
            scatter_rows(
                tmp.at[portion * 2 + pyy], f, ROWS, 0, pyy, portion, outs, 0, pl.ds(0, D)
            )
    own = nn(xk[...], tsc[0]) + nn(xr[...], tsc[2])
    theirs = nn(xk[...], tsc[1]) + nn(xr[...], tsc[3])
    first = jnp.where(c == 0, own, theirs)
    second = jnp.where(c == 0, theirs, own)
    both = first + pltpu.roll(second, 64, 1)
    for pxx in range(2):
        for pz in range(4):
            target = (f >> 1) ^ (pz * 2 + pxx)
            for b in range(8):

                @pl.when(target == b)
                def _():
                    sc[pxx, pz] = both[b * ROWS : (b + 1) * ROWS, :]


def qkv_grad_call(idx, xk, xr, mk, mr, d00, d01, d10, d11, gk, gr):
    flat = [v.reshape(HALF, TOK) for v in (xk, xr, mk, mr)]
    return kernel_call(
        qkv_grad_kernel,
        [idx, *flat, d00, d01, d10, d11, gk, gr],
        [SM, VM, VM, VM, VM, HB, HB, HB, HB, VM, VM],
        [sds((2, 4, 1, ROWS, D), BF16)] * 4 + [sds((2, 4, ROWS, 128), F32)],
        [VM] * 5,
        [
            pltpu.VMEM((2, 6, TOK, HALF), BF16),
            pltpu.VMEM((4, HALF, D), BF16),
            pltpu.VMEM((4, TOK, 128), BF16),
            pltpu.SemaphoreType.DMA((16,)),
        ],
        "qkv_grad",
    )


def cross_kernel(ka, ra, kb, rb, qa, qb):
    for k, r, q in ((ka, ra, qa), (kb, rb, qb)):
        q[...] = (k[...].astype(F32) + r[...].astype(F32)).astype(BF16)[0]


def cross_call(ka, ra, kb, rb):
    n = ka.shape[2]
    block = pl.BlockSpec((1, 1, n, ROWS, D), lambda z: (1, z, 0, 0, 0))
    out = pl.BlockSpec((1, n, ROWS, D), lambda z: (z, 0, 0, 0))
    return pl.pallas_call(
        cross_kernel,
        out_shape=(sds((4, n, ROWS, D), BF16),) * 2,
        grid=(4,),
        in_specs=[block] * 4,
        out_specs=(out,) * 2,
        cost_estimate=duration(COST["cross"]),
        name="cross",
    )(ka, ra, kb, rb)


def own_kernel(ka, ra, ca, kb, rb, cb, *outs):
    z = pl.program_id(0)
    for part, (k, r, q) in enumerate(((ka, ra, ca), (kb, rb, cb))):
        total = k[0, 0].astype(F32) + r[0, 0].astype(F32) + q[0].astype(F32)
        for t in range(4):

            @pl.when(z == t)
            def _():
                outs[t][part] = total.astype(outs[t].dtype)


def own_call(ka, ra, ca, kb, rb, cb):
    n = ka.shape[2]
    block = pl.BlockSpec((1, 1, n, ROWS, D), lambda z: (0, z, 0, 0, 0))
    quarter = pl.BlockSpec((1, n, ROWS, D), lambda z: (z, 0, 0, 0))
    out = pl.BlockSpec((2, n, ROWS, D), lambda z: (0, 0, 0, 0))
    return pl.pallas_call(
        own_kernel,
        out_shape=tuple(sds((2, n, ROWS, D), F32 if t == 0 else BF16) for t in range(4)),
        grid=(4,),
        in_specs=[block, block, quarter] * 2,
        out_specs=(out,) * 4,
        cost_estimate=duration(COST["own"]),
        name="own",
    )(ka, ra, ca, kb, rb, cb)


def pairwise(v, bits):
    return lax.ppermute(v, "zx", [(i, i ^ bits) for i in range(8)])


def over_ctx(v):
    return lax.ppermute(v, "ctx", [(0, 1), (1, 0)])


def over_core(v):
    return lax.ppermute(v, "core", [(0, 1), (1, 0)])


def over_x(v):
    return pairwise(v, 1)


def diagonal(v):
    return lax.ppermute(v, ("zx", "ctx"), [(i, i ^ 3) for i in range(16)])


def turn(v):
    return lax.ppermute(v, ("core", "ctx"), [(0, 0), (1, 2), (2, 1), (3, 3)])


class Chain:
    def __init__(self, stages):
        self.stages, self.result = stages, None
        self.flying = next(stages)

    def advance(self, arrived):
        try:
            self.flying = self.stages.send(arrived)
        except StopIteration as stop:
            self.flying, self.result = None, stop.value


class Order:
    def __init__(self, idx):
        self.gate = idx

    def after(self, value):
        return lax.optimization_barrier((value, self.gate))[0]

    def passed(self, value):
        self.gate, value = lax.optimization_barrier((self.gate, value))
        return value

    def meet(self, *chains):
        for chain, items in zip(chains, self.passed([c.flying for c in chains])):
            chain.advance(items)


def gather_stages(both, z):
    near = yield [pairwise(both, k << 1) for k in range(1, 4)]
    near = [both] + near
    near = [lax.select_n(z, *(near[k ^ t] for t in range(4))) for k in range(4)]
    a, b = (jnp.stack([v[part] for v in near]) for part in range(2))
    xa, yb, ya, xb = yield [over_x(a), over_ctx(b), over_ctx(a), over_x(b)]
    a, b = [a, xa, ya], [b, xb, yb]
    da, db, *other = yield [over_ctx(xa), over_x(yb)] + [over_core(v) for v in a + b]
    ca, cb = yield [over_core(da), over_core(db)]
    return a + [da] + other[:3] + [ca] + b + [db] + other[3:] + [cb]


def small_gather_stages(small, start):
    *near, start = yield [pairwise(small, k << 1) for k in range(1, 4)] + [start]
    small = jnp.stack([small] + near)
    (r,) = yield [over_x(small)]
    small = jnp.concatenate([small, r])
    (r,) = yield [over_core(small)]
    return jnp.concatenate([small, r]), start


def reduce_stages(ka, sa, kb, sb):
    ra, rb = yield [over_x(sa), over_ctx(sb)]
    qa, qb = cross_call(ka, ra, kb, rb)
    ca, cb = yield [over_ctx(qa), over_x(qb)]
    total, *low = own_call(ka, ra, ca, kb, rb, cb)
    rest = yield [pairwise(v, k << 1) for k, v in enumerate(low, 1)]
    return total + sum(v.astype(F32) for v in rest)


def small_stages(t):
    ry, rx, rd = yield [over_ctx(t[0]), over_x(t[1]), diagonal(t[1])]
    t = t[0] + ry + (rx + rd)
    rest = yield [pairwise(t[k], k << 1) for k in range(1, 4)]
    return t[0] + sum(rest)


def pair_device(
    tokens,
    cotangent,
    kept_blocks,
    picture_starts,
    qkv_weight,
    score_weight,
    out_weight,
    up_weight,
    down_weight,
    norm_gain,
    norm_bias,
):
    zx = lax.axis_index("zx").astype(jnp.int32)
    y = lax.axis_index("ctx").astype(jnp.int32)
    c = lax.axis_index("core").astype(jnp.int32)
    f = zx * 2 + c
    idx = jnp.stack([f, y, c])
    order = Order(idx)

    def shards(l):
        joined = jnp.concatenate([qkv_weight[l], out_weight[l]], axis=1)
        up = up_weight[l].reshape(ROWS, 2, D).swapaxes(0, 1)
        down = down_weight[l].reshape(2, 2, ROWS, HALF).swapaxes(1, 2).reshape(2, ROWS, D)
        return jnp.stack([joined[:, :D], joined[:, D:]]), up, down

    def gather(v):
        return Chain(gather_stages(order.after(v), zx >> 1))

    w = [shards(l) for l in range(LAYERS)]
    qo0 = gather(w[0][0][:, None])
    kept = jnp.where(c == y, kept_blocks[0], over_core(kept_blocks[0]))
    pics = jnp.where(c == y, picture_starts[0], over_core(picture_starts[0]))
    kept = lax.dynamic_slice_in_dim(kept, c * 6, 6, 0)
    small = jnp.concatenate(
        [jnp.swapaxes(score_weight, 1, 2), norm_gain, norm_bias], axis=1
    ).reshape(LAYERS * 16, ROWS)
    small = jnp.pad(small, ((0, 0), (0, 128 - ROWS)))
    small = Chain(small_gather_stages(small, turn(tokens[0])))
    ffn0 = lax.all_gather(jnp.stack(w[0][1:], axis=1), ("zx", "ctx"), axis=0, tiled=False)
    order.meet(qo0, small)
    order.meet(qo0, small)
    order.meet(qo0, small)
    order.meet(qo0)
    qo0 = qo0.result
    small, residual = small.result
    residual = residual.astype(F32)
    away = jnp.arange(16, dtype=jnp.int32) ^ f
    small = jnp.take(small, (away & 1) * 8 + ((away >> 1) & 1) * 4 + (away >> 2), axis=0)
    small = jnp.moveaxis(small[:, :, :ROWS], 0, 1).reshape(LAYERS, 16, D)
    scale = []
    for l in range(LAYERS):
        gb = jnp.pad(small[l, 12:16].astype(F32), ((0, 4), (0, 0)))
        own_rows = lax.dynamic_slice_in_dim(small[l], c * 6, 6, 0)
        other_rows = lax.dynamic_slice_in_dim(small[l], (1 - c) * 6, 6, 0)
        pad = ((0, 122), (0, 0))
        scale.append((gb, jnp.pad(own_rows, pad), jnp.pad(other_rows, pad)))

    def qkv(l, residual, w):
        own, send, xk, xs = order.passed(qkv_call(order.gate, residual, *scale[l], w))
        return own, over_core(send), xk, over_core(xs)

    def attend(head):
        mixed, send, lse = order.passed(attend_call(order.gate, kept, pics, head[0], head[1]))
        return (mixed, over_core(send)), lse

    def feed(l, residual, mixed, qo, ffn):
        outs = ffn_call(order.gate, residual, *mixed, scale[l][0], qo, ffn)
        after, new, low, mk, ms, hk, hs, slope, ak, as_ = order.passed(outs)
        hr, ar, mr = over_core(hs), over_core(as_), over_core(ms)
        return new, low, (after, slope, (hk, hr), (ak, ar), (mk, mr))

    qo1 = gather(w[1][0][:, None])
    head0 = qkv(0, residual, qo0)
    order.meet(qo1)
    ffn1 = gather(jnp.stack(w[1][1:], axis=1))
    mixed, lse0 = attend(head0)
    order.meet(qo1, ffn1)
    order.meet(qo1)
    ffn0 = order.passed(ffn0)
    ffn0 = order.passed([v.reshape(4, 2, 2, 2, 2, ROWS, D) for v in (ffn0, over_core(ffn0))])
    res1, _, out0 = feed(0, residual, mixed, qo0, ffn0)
    order.meet(qo1, ffn1)
    qo1 = qo1.result
    head1 = qkv(1, res1, qo1)
    order.meet(ffn1)
    mixed, lse1 = attend(head1)
    order.meet(ffn1)
    ffn1 = ffn1.result
    cot = turn(order.after(cotangent[0]))
    _, low, out1 = feed(1, res1, mixed, qo1, ffn1)
    block_output = turn(low).astype(F32)

    weights = ((qo0, ffn0), (qo1, ffn1))

    def down_back(l, low, out):
        gu = order.passed(down_back_call(order.gate, low, out[1], weights[l][1]))
        return gu, over_core(gu)

    def up_back(l, grad, gu, out):
        ga, gat, gmk, gms, nrm = order.passed(
            up_back_call(order.gate, grad, gu, out[0], scale[l][0], *weights[l])
        )
        return ga, nrm, (gmk, over_core(gms)), (gat, over_core(gat))

    def attend_back(head, lse, gm):
        d_own, d_oth = order.passed(
            attend_back_call(order.gate, kept, pics, lse, head[0], head[1], *gm)
        )
        return d_own, over_core(d_oth), d_oth, over_core(d_own)

    def qkv_grads(head, out, d, gat):
        return order.passed(qkv_grad_call(order.gate, head[2], head[3], *out[4], *d, *gat))

    def qkv_back(l, ga, d, res, head):
        return order.passed(qkv_back_call(order.gate, ga, d[0], d[1], res, *scale[l], weights[l][0]))

    scores, norms = [None] * LAYERS, [None] * LAYERS
    low, low_r = cot, over_core(cot)
    gu, gu_r = down_back(1, low, out1)
    ga, nrm2, gm, gat = up_back(1, cot.astype(F32), gu, out1)
    grads = ffn_grad_call(order.gate, *out1[2], gu, gu_r, *out1[3], low, low_r, False)
    ffn1 = order.passed(grads[0])
    ffn1 = lax.psum_scatter(ffn1, ("zx", "ctx"), scatter_dimension=0, tiled=False)
    d = attend_back(head1, lse1, gm)
    grad, low, nrm1 = qkv_back(1, ga, d, res1, head1)
    low_r = over_core(low)
    *g, scores[1] = qkv_grads(head1, out1, d, gat)
    norms[1] = jnp.concatenate([nrm1[0:1], nrm2[0:1], nrm1[1:2], nrm2[1:2]])
    qo1 = Chain(reduce_stages(*g))
    gu, gu_r = down_back(0, low, out0)
    ga, nrm2, gm, gat = up_back(0, grad, gu, out0)
    order.meet(qo1)
    grads = ffn_grad_call(order.gate, *out0[2], gu, gu_r, *out0[3], low, low_r, True)
    ffn0 = Chain(reduce_stages(*order.passed(grads)))
    order.meet(qo1)
    d = attend_back(head0, lse0, gm)
    order.meet(ffn0, qo1)
    *g, scores[0] = qkv_grads(head0, out0, d, gat)
    qo0 = Chain(reduce_stages(*g))
    grad, low, nrm1 = qkv_back(0, ga, d, residual, head0)
    norms[0] = jnp.concatenate([nrm1[0:1], nrm2[0:1], nrm1[1:2], nrm2[1:2]])
    nrm = jnp.concatenate(norms).reshape(8, 8, 2, ROWS)
    mine, theirs = (lax.dynamic_index_in_dim(nrm, b, 2, keepdims=False) for b in (c, 1 - c))
    nrm = jnp.moveaxis(mine + over_core(theirs), 0, 2)
    nrm = jnp.take(nrm, zx ^ jnp.array([0, 2, 4, 6, 1, 3, 5, 7], jnp.int32), axis=0)
    nrm = nrm.reshape(2, 4, ROWS, 8)
    lanes = [jnp.concatenate([s[..., :6], s[..., 64:70]], -1) for s in scores] + [nrm]
    lanes = jnp.pad(jnp.concatenate(lanes, -1), ((0, 0), (0, 0), (0, 0), (0, 96)))
    lanes = Chain(small_stages(lanes))
    token_grad = turn(low)
    order.meet(ffn0, qo0)
    order.meet(qo0, lanes)
    order.meet(ffn0, lanes)
    order.meet(qo0)
    token_grad = order.passed(token_grad).astype(F32)
    lanes = order.after(lanes.result)
    score_grad = jnp.stack([lanes[:, 0:12], lanes[:, 12:24]])
    nrm = lanes[:, 24:32].T.reshape(LAYERS, 2, 2, ROWS)
    qo = [qo0.result[:, 0], qo1.result[:, 0]]
    qkv_grad = jnp.stack([jnp.concatenate([v[0], v[1, :, :HALF]], 1) for v in qo])
    out_grad = jnp.stack([v[1, :, HALF:] for v in qo])
    ffn = [ffn0.result, ffn1.astype(F32)]
    up_grad = jnp.stack([jnp.concatenate([v[0, 0], v[1, 0]], 1) for v in ffn])
    down_grad = jnp.stack(
        [v[:, 1].reshape(2, ROWS, 2, HALF).swapaxes(1, 2).reshape(DROWS, HALF) for v in ffn]
    )
    return (
        block_output[None],
        token_grad[None],
        qkv_grad,
        score_grad,
        out_grad,
        up_grad,
        down_grad,
        nrm[:, 0],
        nrm[:, 1],
    )


def solution(mesh):
    in_specs = (
        P("fsdp", "ctx", None),
        P("fsdp", "ctx", None),
        P("fsdp", None, None),
        P("fsdp", None),
        P(None, "fsdp", "ctx"),
        P(None, "fsdp", None),
        P(None, "fsdp", "ctx"),
        P(None, "fsdp", "ctx"),
        P(None, "fsdp", "ctx"),
        P(None, None, "fsdp"),
        P(None, None, "fsdp"),
    )
    out_specs = (
        P("fsdp", "ctx", None),
        P("fsdp", "ctx", None),
        P(None, "fsdp", "ctx"),
        P(None, "fsdp", None),
        P(None, "fsdp", "ctx"),
        P(None, "fsdp", "ctx"),
        P(None, "fsdp", "ctx"),
        P(None, None, "fsdp"),
        P(None, None, "fsdp"),
    )
    step = per_device
    if mesh.shape["fsdp"] == 16 and mesh.shape["ctx"] == 2:
        step = pair_device
        mesh = Mesh(mesh.devices.reshape(8, 2, 2), ("zx", "core", "ctx"))
        in_specs, out_specs = (
            tuple(P(*(("zx", "core") if a == "fsdp" else a for a in spec)) for spec in specs)
            for specs in (in_specs, out_specs)
        )
    return jax.shard_map(
        step, mesh=mesh, in_specs=in_specs, out_specs=out_specs, check_vma=False
    )
```

```python
import math
from functools import partial

import jax
import jax.numpy as jnp
from jax import lax
from jax.experimental import pallas as pl
from jax.experimental.pallas import tpu as pltpu
from jax.sharding import Mesh
from jax.sharding import PartitionSpec as P

HEADS = 12
HEAD_DIM = 64
LAYERS = 2
BLK = 128
WINDOW = 64
PIC_LEN = 256


def normalize(residual, gain, bias):
    mean_value = jnp.mean(residual, axis=-1, keepdims=True)
    centered = residual - mean_value
    variance = jnp.mean(centered * centered, axis=-1, keepdims=True)
    return centered * lax.rsqrt(variance + 1e-05) * gain + bias


def gelu_tanh(value):
    return jax.nn.gelu(value, approximate=True)


def log_sigmoid(value):
    return -(jnp.maximum(-value, 0.0) + jnp.log1p(jnp.exp(-jnp.abs(value))))


def split_heads(tensor):
    return jnp.moveaxis(tensor.reshape(tensor.shape[:-1] + (HEADS, HEAD_DIM)), 2, 0)


def join_heads(tensor):
    moved = jnp.moveaxis(tensor, 0, 2)
    return moved.reshape(moved.shape[:2] + (HEADS * HEAD_DIM,))


def masked_logits(queries, keys, scores, kept, base, causal, key_block):
    logits = jnp.einsum(
        "sqd,skd->sqk", queries, keys, preferred_element_type=jnp.float32
    ) * HEAD_DIM ** (-0.5)
    logits = logits + log_sigmoid(scores.astype(jnp.float32))[:, None, :]
    allowed = base | causal[None] & (key_block[None, None, :] == kept[:, :, None])
    return (logits, allowed)


def attend_head(items, base, causal, key_block):
    queries, keys, values, scores, kept = items
    logits, allowed = masked_logits(queries, keys, scores, kept, base, causal, key_block)
    logits = jnp.where(allowed, logits, -1e30)
    largest = jnp.max(logits, axis=-1, keepdims=True)
    weights = jnp.exp(logits - largest)
    totals = jnp.sum(weights, axis=-1, keepdims=True)
    probs_low = (weights / totals).astype(jnp.bfloat16)
    outputs = jnp.einsum("sqk,skd->sqd", probs_low, values, preferred_element_type=jnp.float32)
    return (outputs, (largest + jnp.log(totals))[..., 0])


def query_side_grads(items, base, causal, key_block):
    queries, keys, values, scores, kept, grad_out, log_totals = items
    logits, allowed = masked_logits(queries, keys, scores, kept, base, causal, key_block)
    probs = jnp.where(allowed, jnp.exp(logits - log_totals[..., None]), 0.0)
    grad_probs = jnp.einsum("sqd,skd->sqk", grad_out, values, preferred_element_type=jnp.float32)
    inner = jnp.sum(probs * grad_probs, axis=-1, keepdims=True)
    grad_logits = (probs * (grad_probs - inner)).astype(jnp.bfloat16)
    grad_queries = jnp.einsum(
        "sqk,skd->sqd", grad_logits, keys, preferred_element_type=jnp.float32
    ) * HEAD_DIM ** (-0.5)
    return (grad_queries, inner[..., 0])


def key_side_grads(items, base, causal, key_block):
    queries, keys, values, scores, kept, grad_out, log_totals, inner = items
    logits, allowed = masked_logits(queries, keys, scores, kept, base, causal, key_block)
    probs = jnp.where(allowed, jnp.exp(logits - log_totals[..., None]), 0.0)
    grad_probs = jnp.einsum("sqd,skd->sqk", grad_out, values, preferred_element_type=jnp.float32)
    grad_logits = (probs * (grad_probs - inner[..., None])).astype(jnp.bfloat16)
    grad_values = jnp.einsum(
        "sqk,sqd->skd", probs.astype(jnp.bfloat16), grad_out, preferred_element_type=jnp.float32
    )
    grad_keys = jnp.einsum(
        "sqk,sqd->skd", grad_logits, queries, preferred_element_type=jnp.float32
    ) * HEAD_DIM ** (-0.5)
    grad_scores = jnp.sum(grad_logits.astype(jnp.float32), axis=1) * jax.nn.sigmoid(
        -scores.astype(jnp.float32)
    )
    return (grad_keys, grad_values, grad_scores)


def build_masks(kept_blocks, picture_starts, query_start, query_len, key_start, key_len):
    query_pos = query_start + jnp.arange(query_len, dtype=jnp.int32)
    key_pos = key_start + jnp.arange(key_len, dtype=jnp.int32)
    causal = key_pos[None, :] <= query_pos[:, None]
    local = causal & (query_pos[:, None] - key_pos[None, :] < WINDOW)
    starts = picture_starts[:, :, None]
    inside_query = (query_pos[None, None, :] >= starts) & (
        query_pos[None, None, :] < starts + PIC_LEN
    )
    inside_key = (key_pos[None, None, :] >= starts) & (key_pos[None, None, :] < starts + PIC_LEN)
    picture = jnp.any(inside_query[:, :, :, None] & inside_key[:, :, None, :], axis=1)
    base = local[None] | picture
    kept_all = jnp.repeat(kept_blocks, BLK, axis=2)
    kept_rows = jnp.moveaxis(lax.dynamic_slice_in_dim(kept_all, query_start, query_len, 2), 1, 0)
    return (base, causal, key_pos // BLK, kept_rows)


def forward_layer(residual, weights, masks):
    qkv_w, score_w, out_w, up_w, down_w, gain, bias = weights
    base, causal, key_block, kept_rows = masks
    gains = gain.astype(jnp.float32)
    biases = bias.astype(jnp.float32)
    hidden = normalize(residual, gains[0], biases[0]).astype(jnp.bfloat16)
    qkv = jnp.dot(hidden, qkv_w, preferred_element_type=jnp.float32).astype(jnp.bfloat16)
    scores = jnp.dot(hidden, score_w, preferred_element_type=jnp.float32).astype(jnp.bfloat16)
    queries, keys, values = jnp.split(qkv, 3, axis=-1)
    all_keys, all_values, all_scores = (
        lax.all_gather(keys, "ctx", axis=1, tiled=True),
        lax.all_gather(values, "ctx", axis=1, tiled=True),
        lax.all_gather(scores, "ctx", axis=1, tiled=True),
    )
    head_items = (
        split_heads(queries),
        split_heads(all_keys),
        split_heads(all_values),
        jnp.moveaxis(all_scores, 2, 0),
        kept_rows,
    )
    heads, log_totals = lax.map(
        partial(attend_head, base=base, causal=causal, key_block=key_block), head_items
    )
    mixed = join_heads(heads).astype(jnp.bfloat16)
    after_attn = residual + jnp.dot(mixed, out_w, preferred_element_type=jnp.float32)
    hidden2 = normalize(after_attn, gains[1], biases[1]).astype(jnp.bfloat16)
    up_part = jnp.dot(hidden2, up_w, preferred_element_type=jnp.float32)
    active = gelu_tanh(up_part).astype(jnp.bfloat16)
    result = after_attn + jnp.dot(active, down_w, preferred_element_type=jnp.float32)
    own_side = (queries, keys, values, scores)
    saved = (
        residual,
        hidden,
        head_items,
        log_totals,
        mixed,
        after_attn,
        hidden2,
        up_part,
        active,
        own_side,
    )
    return (result, saved)


def backward_layer(grad, saved, weights, masks, key_masks):
    qkv_w, score_w, out_w, up_w, down_w, gain, bias = weights
    base, causal, key_block, kept_rows = masks
    (
        residual,
        hidden,
        head_items,
        log_totals,
        mixed,
        after_attn,
        hidden2,
        up_part,
        active,
        own_side,
    ) = saved
    gains = gain.astype(jnp.float32)
    biases = bias.astype(jnp.float32)
    grad_down = grad.astype(jnp.bfloat16)
    grad_active = jnp.einsum("sto,io->sti", grad_down, down_w, preferred_element_type=jnp.float32)
    grad_up = jax.vjp(gelu_tanh, up_part)[1](grad_active)[0].astype(jnp.bfloat16)
    grad_hidden2 = jnp.einsum("stf,df->std", grad_up, up_w, preferred_element_type=jnp.float32)
    late_back = jax.vjp(normalize, after_attn, gains[1], biases[1])[1]
    grad_norm_late, gain_late, bias_late = late_back(grad_hidden2)
    grad_after = grad + grad_norm_late
    grad_attn = grad_after.astype(jnp.bfloat16)
    grad_mixed = jnp.einsum(
        "ste,de->std", grad_attn, out_w, preferred_element_type=jnp.float32
    ).astype(jnp.bfloat16)
    grad_items = head_items + (split_heads(grad_mixed), log_totals)
    grad_queries, inner = lax.map(
        partial(query_side_grads, base=base, causal=causal, key_block=key_block), grad_items
    )
    own_queries, own_keys, own_values, own_scores = own_side
    all_queries, all_grad_mixed = (
        lax.all_gather(own_queries, "ctx", axis=1, tiled=True),
        lax.all_gather(grad_mixed, "ctx", axis=1, tiled=True),
    )
    all_totals, all_inner = (
        lax.all_gather(log_totals, "ctx", axis=2, tiled=True),
        lax.all_gather(inner, "ctx", axis=2, tiled=True),
    )
    key_base, key_causal, key_block_own, kept_all_rows = key_masks
    key_items = (
        split_heads(all_queries),
        split_heads(own_keys),
        split_heads(own_values),
        jnp.moveaxis(own_scores, 2, 0),
        kept_all_rows,
        split_heads(all_grad_mixed),
        all_totals,
        all_inner,
    )
    grad_keys, grad_values, grad_scores = lax.map(
        partial(key_side_grads, base=key_base, causal=key_causal, key_block=key_block_own),
        key_items,
    )
    key_part = join_heads(grad_keys)
    value_part = join_heads(grad_values)
    score_part = jnp.moveaxis(grad_scores, 0, 2)
    grad_qkv = jnp.concatenate([join_heads(grad_queries), key_part, value_part], axis=-1).astype(
        jnp.bfloat16
    )
    grad_score_low = score_part.astype(jnp.bfloat16)
    grad_hidden = jnp.einsum("ste,de->std", grad_qkv, qkv_w, preferred_element_type=jnp.float32)
    grad_hidden = grad_hidden + jnp.einsum(
        "sth,dh->std", grad_score_low, score_w, preferred_element_type=jnp.float32
    )
    early_back = jax.vjp(normalize, residual, gains[0], biases[0])[1]
    grad_norm_early, gain_early, bias_early = early_back(grad_hidden)
    grad_residual = grad_after + grad_norm_early
    inputs = (hidden, mixed, hidden2, active, grad_score_low)
    outputs = (grad_qkv, grad_attn, grad_up, grad_down)
    norms = (jnp.stack([gain_early, gain_late]), jnp.stack([bias_early, bias_late]))
    return (grad_residual, inputs, outputs, norms)


def weight_terms(inputs, outputs, norms):
    all_hidden, all_mixed, all_hidden2, all_active, all_score = (
        lax.all_gather(inputs[0], "ctx", axis=1, tiled=True),
        lax.all_gather(inputs[1], "ctx", axis=1, tiled=True),
        lax.all_gather(inputs[2], "ctx", axis=1, tiled=True),
        lax.all_gather(inputs[3], "ctx", axis=1, tiled=True),
        lax.all_gather(inputs[4], "ctx", axis=1, tiled=True),
    )
    col_qkv, col_attn, col_up, col_down = (
        lax.all_to_all(outputs[0], "ctx", split_axis=2, concat_axis=1, tiled=True),
        lax.all_to_all(outputs[1], "ctx", split_axis=2, concat_axis=1, tiled=True),
        lax.all_to_all(outputs[2], "ctx", split_axis=2, concat_axis=1, tiled=True),
        lax.all_to_all(outputs[3], "ctx", split_axis=2, concat_axis=1, tiled=True),
    )
    gain_total, bias_total = lax.psum((norms[0], norms[1]), "ctx")
    qkv_term = jnp.einsum("std,ste->de", all_hidden, col_qkv, preferred_element_type=jnp.float32)
    score_term = jnp.einsum(
        "std,sth->dh", all_hidden, all_score, preferred_element_type=jnp.float32
    )
    out_term = jnp.einsum("std,ste->de", all_mixed, col_attn, preferred_element_type=jnp.float32)
    up_term = jnp.einsum("std,stf->df", all_hidden2, col_up, preferred_element_type=jnp.float32)
    down_term = jnp.einsum("sti,sto->io", all_active, col_down, preferred_element_type=jnp.float32)
    return (qkv_term, score_term, out_term, up_term, down_term, gain_total, bias_total)


def per_device(
    tokens,
    cotangent,
    kept_blocks,
    picture_starts,
    qkv_weight,
    score_weight,
    out_weight,
    up_weight,
    down_weight,
    norm_gain,
    norm_bias,
):
    local_len = tokens.shape[1]
    whole_len = local_len * lax.axis_size("ctx")
    own_start = lax.axis_index("ctx") * local_len
    masks = build_masks(kept_blocks, picture_starts, own_start, local_len, 0, whole_len)
    key_masks = build_masks(kept_blocks, picture_starts, 0, whole_len, own_start, local_len)
    residual = tokens.astype(jnp.float32)
    kept_weights = []
    saved_all = []
    for layer_index in range(LAYERS):
        rows = (
            lax.all_gather(qkv_weight[layer_index], "fsdp", axis=0, tiled=True),
            lax.all_gather(score_weight[layer_index], "fsdp", axis=0, tiled=True),
            lax.all_gather(out_weight[layer_index], "fsdp", axis=0, tiled=True),
            lax.all_gather(up_weight[layer_index], "fsdp", axis=0, tiled=True),
            lax.all_gather(down_weight[layer_index], "fsdp", axis=0, tiled=True),
            lax.all_gather(norm_gain[layer_index], "fsdp", axis=1, tiled=True),
            lax.all_gather(norm_bias[layer_index], "fsdp", axis=1, tiled=True),
        )
        full_qkv, full_out, full_up, full_down = (
            lax.all_gather(rows[0], "ctx", axis=1, tiled=True),
            lax.all_gather(rows[2], "ctx", axis=1, tiled=True),
            lax.all_gather(rows[3], "ctx", axis=1, tiled=True),
            lax.all_gather(rows[4], "ctx", axis=1, tiled=True),
        )
        weights = (full_qkv, rows[1], full_out, full_up, full_down, rows[5], rows[6])
        kept_weights.append(weights)
        residual, saved = forward_layer(residual, weights, masks)
        saved_all.append(saved)
    grad = cotangent.astype(jnp.float32)
    layer_terms = []
    for layer_index in reversed(range(LAYERS)):
        rows = (
            lax.all_gather(qkv_weight[layer_index], "fsdp", axis=0, tiled=True),
            lax.all_gather(score_weight[layer_index], "fsdp", axis=0, tiled=True),
            lax.all_gather(out_weight[layer_index], "fsdp", axis=0, tiled=True),
            lax.all_gather(up_weight[layer_index], "fsdp", axis=0, tiled=True),
            lax.all_gather(down_weight[layer_index], "fsdp", axis=0, tiled=True),
            lax.all_gather(norm_gain[layer_index], "fsdp", axis=1, tiled=True),
            lax.all_gather(norm_bias[layer_index], "fsdp", axis=1, tiled=True),
        )
        full_qkv, full_out, full_up, full_down = (
            lax.all_gather(rows[0], "ctx", axis=1, tiled=True),
            lax.all_gather(rows[2], "ctx", axis=1, tiled=True),
            lax.all_gather(rows[3], "ctx", axis=1, tiled=True),
            lax.all_gather(rows[4], "ctx", axis=1, tiled=True),
        )
        weights = (full_qkv, rows[1], full_out, full_up, full_down, rows[5], rows[6])
        grad, inputs, outputs, norms = backward_layer(
            grad, saved_all[layer_index], weights, masks, key_masks
        )
        terms = weight_terms(inputs, outputs, norms)
        layer_terms.insert(0, terms)
    stacked = [jnp.stack([entry[number] for entry in layer_terms]) for number in range(7)]
    summed = (
        lax.psum_scatter(
            stacked[0].astype(jnp.bfloat16), "fsdp", scatter_dimension=1, tiled=True
        ).astype(jnp.float32),
        lax.psum_scatter(
            stacked[1].astype(jnp.bfloat16), "fsdp", scatter_dimension=1, tiled=True
        ).astype(jnp.float32),
        lax.psum_scatter(
            stacked[2].astype(jnp.bfloat16), "fsdp", scatter_dimension=1, tiled=True
        ).astype(jnp.float32),
        lax.psum_scatter(
            stacked[3].astype(jnp.bfloat16), "fsdp", scatter_dimension=1, tiled=True
        ).astype(jnp.float32),
        lax.psum_scatter(
            stacked[4].astype(jnp.bfloat16), "fsdp", scatter_dimension=1, tiled=True
        ).astype(jnp.float32),
        lax.psum_scatter(
            stacked[5].astype(jnp.bfloat16), "fsdp", scatter_dimension=2, tiled=True
        ).astype(jnp.float32),
        lax.psum_scatter(
            stacked[6].astype(jnp.bfloat16), "fsdp", scatter_dimension=2, tiled=True
        ).astype(jnp.float32),
    )
    return (
        residual,
        grad,
        summed[0],
        summed[1],
        summed[2],
        summed[3],
        summed[4],
        summed[5],
        summed[6],
    )


D = 768
FF = 3072
HALF = 384
TOK = 512
SEQ = 1024
ROWS = 48
DROWS = 192
NEG = -1e30
FULL = 58 << 20
F32 = jnp.float32
BF16 = jnp.bfloat16
VM = pl.BlockSpec(memory_space=pltpu.VMEM)
HB = pl.BlockSpec(memory_space=pltpu.HBM)
SM = pl.BlockSpec(memory_space=pltpu.SMEM)


def nn(a, b):
    return lax.dot_general(a, b, (((1,), (0,)), ((), ())), preferred_element_type=F32)


def nt(a, b):
    return lax.dot_general(a, b, (((1,), (1,)), ((), ())), preferred_element_type=F32)


def tn(a, b):
    return lax.dot_general(a, b, (((0,), (0,)), ((), ())), preferred_element_type=F32)


def sds(shape, dtype):
    return jax.ShapeDtypeStruct(shape, dtype)


COST = dict(layer_grad=20, qkv=7, attend=12, ffn=20, down_back=6, up_back=10, ffn_grad=11)
COST |= dict(attend_back=16, qkv_grad=8, qkv_back=9, cross=4, own=4)


def duration(us):
    flops = int(us * 0.4e9)
    return pl.CostEstimate(flops=flops, bytes_accessed=1 << 20, transcendentals=0)


def kernel_call(body, ins, in_specs, outs, out_specs, scratch, name, limit=None):
    held = [v for v, spec in zip((*ins, *outs), (*in_specs, *out_specs)) if spec is VM]
    held += [b for b in scratch if getattr(b, "memory_space", None) == pltpu.VMEM]
    held = sum(math.prod(v.shape) * jnp.dtype(v.dtype).itemsize for v in held)
    return pl.pallas_call(
        body,
        out_shape=tuple(outs),
        in_specs=in_specs,
        out_specs=tuple(out_specs),
        scratch_shapes=scratch,
        compiler_params=pltpu.CompilerParams(vmem_limit_bytes=FULL),
        cost_estimate=duration(COST[name]),
        name=name,
    )(*ins)


def aligned(v, m):
    return pl.multiple_of(v, m)


def layer_norm_parts(x):
    centered = x - jnp.mean(x, axis=-1, keepdims=True)
    variance = jnp.mean(centered * centered, axis=-1, keepdims=True)
    scale = lax.rsqrt(variance + 1e-05)
    return centered * scale, scale


def split_blocks(src, keep, send, c, rows):
    for b in range(8):
        keep[b] = src[pl.ds(aligned((2 * b + c) * rows, 16), rows), :]
        send[b] = src[pl.ds(aligned((2 * b + 1 - c) * rows, 16), rows), :]


def visit(f, y, arrays, n, fns):
    if len(arrays) == 16:
        for q in range(8):
            device = (f & 3) ^ ((q & 1) * 2 + (q >> 2))
            for part, fn in enumerate(fns):
                fn(arrays[part * 8 + q].at[:, n], device, y ^ ((q >> 1) & 1))
        return
    for pxx in range(2):
        for pc in range(2):
            for y2 in range(2):
                for part, fn in enumerate(fns):
                    device = pxx * 2 + ((f & 1) ^ pc)
                    fn(arrays[pc].at[:, pxx, y2, part, n], device, y2)


QKV_W = pltpu.VMEM((6, 4, 4, ROWS, HALF), BF16)
OUT_W = pltpu.VMEM((2, 4, 4, ROWS, HALF), BF16)
UP_W = pltpu.VMEM((4, 4, 4, ROWS, D), BF16)
DOWN_W = pltpu.VMEM((2, 4, 4, 4, ROWS, HALF), BF16)


def fetch_qkv(f, y, parts, w, sem):
    def put(src, cols, group, device, y2):
        dst = w.at[y2 * 3 + group, :, device]
        pltpu.make_async_copy(src.at[:, :, cols], dst, sem).start()

    def fetch_a(src, device, y2):
        put(src, pl.ds(0, HALF), 0, device, y2)
        put(src, pl.ds(HALF, HALF), 1, device, y2)

    def fetch_b(src, device, y2):
        put(src, pl.ds(0, HALF), 2, device, y2)

    visit(f, y, parts, 0, (fetch_a, fetch_b))


def fetch_out(f, y, parts, wo, sem):
    def fetch(src, device, y2):
        dst = wo.at[y2, :, device]
        pltpu.make_async_copy(src.at[:, :, pl.ds(HALF, HALF)], dst, sem).start()

    visit(f, y, parts, 0, (lambda *_: None, fetch))


def fetch_up(f, y, parts, wu, sem):
    def fetch(part):
        def copy(src, device, y2):
            pltpu.make_async_copy(src, wu.at[y2 * 2 + part, :, device], sem).start()

        return copy

    visit(f, y, parts, 0, (fetch(0), fetch(1)))


def fetch_down(f, y, parts, wd, sem):
    def fetch(part):
        def copy(src, device, y2):
            for k in range(2):
                dst = wd.at[y2, :, device, part * 2 + k]
                pltpu.make_async_copy(src.at[:, :, pl.ds(k * HALF, HALF)], dst, sem).start()

        return copy

    visit(f, y, parts, 1, (fetch(0), fetch(1)))


def arrived(w, sem):
    pltpu.make_async_copy(w, w, sem).wait()


def load(pairs, sem):
    copies = [pltpu.make_async_copy(a, b, sem.at[k]) for k, (a, b) in enumerate(pairs)]
    for copy in copies:
        copy.start()
    return copies


def qkv_kernel(idx, res, gb, sw0, sw1, *refs):
    parts, refs = refs[:-8], refs[-8:]
    keep, send, htk, hts, w, h, ht, sem = refs
    f, y, c = idx[0], idx[1], idx[2]

    fetch_qkv(f, y, parts, w, sem)
    gain, bias = gb[0:1, :], gb[2:3, :]
    for t in range(4):
        rows = pl.ds(t * 128, 128)
        n, _ = layer_norm_parts(res[rows, :])
        v = n * gain + bias
        h[rows, :] = v.astype(BF16)
        ht[:, rows] = v.T.astype(BF16)
    split_blocks(ht, htk, hts, c, ROWS)
    pltpu.make_async_copy(w, w, sem).wait()

    def tile(t, carry):
        rows = pl.ds(aligned(t * 256, 256), 256)
        hv = h[rows, :]
        for j in range(3):
            cols = pl.ds(j * HALF, HALF)
            keep[rows, cols] = nn(hv, w[2 * j + c].reshape(D, HALF)).astype(BF16)
            send[rows, cols] = nn(hv, w[2 * j + 1 - c].reshape(D, HALF)).astype(BF16)
        keep[rows, pl.ds(1152, 128)] = nt(hv, sw0[...]).astype(BF16)
        send[rows, pl.ds(1152, 128)] = nt(hv, sw1[...]).astype(BF16)
        return carry

    lax.fori_loop(0, 2, tile, 0)


def qkv_call(idx, res, gb, sw0, sw1, w):
    return kernel_call(
        qkv_kernel,
        [idx, res, gb, sw0, sw1, *w],
        [SM, VM, VM, VM, VM] + [HB] * len(w),
        [
            sds((TOK, 1280), BF16),
            sds((TOK, 1280), BF16),
            sds((8, ROWS, TOK), BF16),
            sds((8, ROWS, TOK), BF16),
        ],
        [VM, VM, VM, VM],
        [
            QKV_W,
            pltpu.VMEM((TOK, D), BF16),
            pltpu.VMEM((D, TOK), BF16),
            pltpu.SemaphoreType.DMA,
        ],
        "qkv",
        FULL,
    )


def load_halves(pairs, c, pad, sem):
    copies = []
    for number, (own, other, dst) in enumerate(pairs):
        for k, (src, half) in enumerate(((own, c), (other, 1 - c))):
            rows = pl.ds(aligned(pad + half * TOK, 128), TOK)
            copy = pltpu.make_async_copy(src, dst.at[rows, :], sem.at[2 * number + k])
            copy.start()
            copies.append(copy)
    return copies


def mask_tiles(tab):
    key = lax.broadcasted_iota(jnp.int32, (BLK, BLK), 0)
    query = lax.broadcasted_iota(jnp.int32, (BLK, BLK), 1)
    gap = query - key
    tab[0] = jnp.where((gap >= 0) & (gap < WINDOW), 0.0, NEG)
    tab[1] = jnp.where(gap >= 0, 0.0, NEG)
    tab[2] = jnp.zeros((BLK, BLK), F32)
    tab[3] = jnp.where(gap + BLK < WINDOW, 0.0, NEG)
    tab[4] = jnp.full((BLK, BLK), NEG, F32)


def log_sigmoid_of(v):
    return -(jnp.maximum(-v, 0.0) + jnp.log1p(jnp.exp(-jnp.abs(v))))


def picture_flags(pics, i):
    p0, p1 = pics[0] // BLK, pics[1] // BLK
    starts = (p0 == i) | (p1 == i)
    follows = (p0 == i - 1) | (p1 == i - 1)
    return starts, follows


def split_log_sigmoid(s, la):
    value = log_sigmoid_of(s[:, 1152:1280].astype(F32))
    lane = lax.broadcasted_iota(jnp.int32, value.shape, 1)
    value = jnp.where(lane < 6, value, 0.0)
    high = value.astype(BF16).astype(F32)
    middle = (value - high).astype(BF16).astype(F32)
    low = value - high - middle
    la[...] = (high + pltpu.roll(middle, 8, 1) + pltpu.roll(low, 16, 1)).astype(BF16)


def pair_logits(s, la, tab, kept, i, pair, blocks, starts, follows):
    lane = lax.broadcasted_iota(jnp.int32, (BLK, BLK), 1)
    first = lane < 64
    base = aligned(i * BLK, BLK)
    cols = pair * BLK
    q = s[pl.ds(base + BLK, BLK), pl.ds(cols, BLK)] * jnp.asarray(HEAD_DIM**-0.5, BF16)
    zero = jnp.zeros_like(q)
    q = jnp.concatenate([jnp.where(first, q, zero), jnp.where(first, zero, q)], axis=0)
    terms = [((lane & 7) == 2 * pair + odd) & (lane < 24) for odd in range(2)]
    ones = jnp.concatenate([jnp.where(t, 1.0, 0.0) for t in terms], axis=0).astype(BF16)
    near = pl.ds(base, blocks * BLK)
    chosen = [kept[2 * pair + odd, i] for odd in range(2)]
    far = [pl.ds(aligned((b + 1) * BLK, BLK), BLK) for b in chosen]

    def rows_of(cols):
        far_rows = jnp.where(first, s[far[0], cols], s[far[1], cols])
        return jnp.concatenate([s[near, cols], far_rows], axis=0)

    k = rows_of(pl.ds(HALF + cols, BLK))
    v = rows_of(pl.ds(2 * HALF + cols, BLK))
    bias = jnp.where(terms[0], la[far[0], :], la[far[1], :])
    bias = jnp.concatenate([la[near, :], bias], axis=0)
    logits = nt(jnp.concatenate([k, bias], axis=1), jnp.concatenate([q, ones], axis=1))
    before, here, beyond = [], [], []
    for block in chosen:
        before.append(tab[jnp.where(i == 0, 4, jnp.where(follows | (block == i - 1), 2, 3))])
        here.append(tab[jnp.where(starts | follows, 2, jnp.where(block == i, 1, 0))])
        beyond.append(jnp.full((1, BLK), jnp.where(block < i - 1, 0.0, NEG), F32))
    parts = [
        logits[0:BLK] + jnp.concatenate(before, axis=1),
        logits[BLK : 2 * BLK] + jnp.concatenate(here, axis=1),
    ]
    if blocks == 3:
        parts.append(logits[2 * BLK : 3 * BLK])
    parts.append(logits[blocks * BLK :] + jnp.concatenate(beyond, axis=1))
    return jnp.concatenate(parts, axis=0), q, k, v, near, far, first


def block_probs(s, ls, tab, kept, i, h, blocks, starts, follows):
    pair, odd = h // 2, h % 2
    lane = lax.broadcasted_iota(jnp.int32, (BLK, BLK), 1)
    mine = (lane >= 64) if odd else (lane < 64)
    base = aligned(i * BLK, BLK)
    cols = pair * BLK
    q = s[pl.ds(base + BLK, BLK), pl.ds(cols, BLK)] * jnp.asarray(HEAD_DIM**-0.5, BF16)
    q = jnp.where(mine, q, jnp.zeros_like(q))
    near, chosen = pl.ds(base, blocks * BLK), kept[h, i]
    far = pl.ds(aligned((chosen + 1) * BLK, BLK), BLK)
    kcols, vcols = pl.ds(HALF + cols, BLK), pl.ds(2 * HALF + cols, BLK)
    k = jnp.concatenate([s[near, kcols], s[far, kcols]], axis=0)
    v = jnp.concatenate([s[near, vcols], s[far, vcols]], axis=0)
    before = jnp.where(i == 0, 4, jnp.where(follows | (chosen == i - 1), 2, 3))
    here = jnp.where(starts | follows, 2, jnp.where(chosen == i, 1, 0))
    beyond = jnp.where(chosen < i - 1, 0.0, NEG).astype(F32)
    logits = nt(k, q)
    parts = [
        logits[0:BLK] + (tab[before] + ls[pl.ds(base, BLK), h : h + 1]),
        logits[BLK : 2 * BLK] + (tab[here] + ls[pl.ds(base + BLK, BLK), h : h + 1]),
    ]
    if blocks == 3:
        parts.append(logits[2 * BLK : 3 * BLK] + ls[pl.ds(base + 2 * BLK, BLK), h : h + 1])
    parts.append(logits[blocks * BLK :] + (ls[far, h : h + 1] + beyond))
    logits = jnp.concatenate(parts, axis=0)
    largest = jnp.max(logits, axis=0, keepdims=True)
    weights = jnp.exp(logits - largest)
    total = jnp.sum(weights, axis=0, keepdims=True)
    probs = weights * (1.0 / total)
    return probs, v, mine, largest + jnp.log(total)


def attend_kernel(idx, kept, pics, own, other, okeep, osend, lse, s, ls, o, tab, sem):
    c = idx[2]
    copies = load_halves([(own, other, s)], c, BLK, sem)
    s[0:BLK, :] = jnp.zeros((BLK, 1280), BF16)
    mask_tiles(tab)
    for copy in copies:
        copy.wait()
    ls[...] = log_sigmoid_of(s[:, 1152:1280].astype(F32))
    lse[...] = jnp.zeros_like(lse)

    def step(i, carry):
        starts, follows = picture_flags(pics, i)

        def run(blocks):
            rows = pl.ds(aligned(i * BLK, BLK), BLK)
            for pair in range(3):
                halves = []
                for odd in range(2):
                    h = 2 * pair + odd
                    probs, v, mine, logs = block_probs(
                        s, ls, tab, kept, i, h, blocks, starts, follows
                    )
                    halves.append(tn(probs.astype(BF16), v))
                    lse[h : h + 1, rows] = logs
                o[rows, pl.ds(pair * BLK, BLK)] = jnp.where(mine, halves[1], halves[0]).astype(BF16)

        @pl.when(starts)
        def _():
            run(3)

        @pl.when(jnp.logical_not(starts))
        def _():
            run(2)

        return carry

    lax.fori_loop(0, 8, step, 0)
    okeep[...] = o[pl.ds(aligned(c * TOK, TOK), TOK), :]
    osend[...] = o[pl.ds(aligned((1 - c) * TOK, TOK), TOK), :]


def attend_call(idx, kept, pics, own, other):
    return kernel_call(
        attend_kernel,
        [idx, kept, pics, own, other],
        [SM, SM, SM, HB, HB],
        [sds((TOK, HALF), BF16), sds((TOK, HALF), BF16), sds((8, SEQ), F32)],
        [VM, VM, VM],
        [
            pltpu.VMEM((SEQ + BLK, 1280), BF16),
            pltpu.VMEM((SEQ + BLK, BLK), F32),
            pltpu.VMEM((SEQ, HALF), BF16),
            pltpu.VMEM((5, BLK, BLK), F32),
            pltpu.SemaphoreType.DMA((2,)),
        ],
        "attend",
        FULL,
    )


def ffn_kernel(idx, res_in, mk, mr, gb, *refs):
    qo, ffn, refs = refs[:16], refs[16:-23], refs[-23:]
    aa, new, low, mtk, mts, htk, hts, slope_o, atk, ats = refs[:10]
    wo, wu, wd, res, h, ht, act, slope, at, sem, isem, osem, asem = refs[10:]
    f, y, c = idx[0], idx[1], idx[2]
    (res_copy,) = load([(res_in, res)], isem)
    fetch_out(f, y, qo, wo, sem.at[0])
    fetch_up(f, y, ffn, wu, sem.at[1])
    fetch_down(f, y, ffn, wd, sem.at[2])
    ht[pl.ds(aligned(c * HALF, HALF), HALF), :] = mk[...].T
    ht[pl.ds(aligned((1 - c) * HALF, HALF), HALF), :] = mr[...].T
    split_blocks(ht, mtk, mts, c, ROWS)
    arrived(wo, sem.at[0])
    res_copy.wait()
    gain, bias = gb[1:2, :], gb[3:4, :]
    mine, theirs = pl.ds(c * 2, 2), pl.ds((1 - c) * 2, 2)
    for half in range(2):
        cols = pl.ds(half * HALF, HALF)
        part = nn(mk[...], wo[half, mine].reshape(HALF, HALF))
        part += nn(mr[...], wo[half, theirs].reshape(HALF, HALF))
        aa[:, cols] = res[:, cols] + part
    for t in range(4):
        rows = pl.ds(t * 128, 128)
        n, _ = layer_norm_parts(aa[rows, :])
        v = (n * gain + bias).astype(BF16)
        h[rows, :] = v
        ht[:, rows] = v.T
    split_blocks(ht, htk, hts, c, ROWS)
    arrived(wu, sem.at[1])
    outs = []
    for g in range(4):

        def tile(t, carry):
            rows = pl.ds(aligned(t * 256, 256), 256)
            u = nn(h[rows, :], wu[g].reshape(D, D))
            square = u * u
            th = jnp.tanh(u * (0.7978845608 + (0.7978845608 * 0.044715) * square))
            share = 0.5 + 0.5 * th
            a = u * share
            bend = 2 * 0.7978845608 + (6 * 0.7978845608 * 0.044715) * square
            d = share + a * (1.0 - share) * bend
            cols = pl.ds(g * D, D)
            a = a.astype(BF16)
            act[rows, cols] = a
            slope[rows, cols] = d.astype(BF16)
            at[cols, rows] = a.T
            return carry

        lax.fori_loop(0, 2, tile, 0)
        cols = pl.ds(g * D, D)
        outs.append(pltpu.make_async_copy(slope.at[:, cols], slope_o.at[:, cols], osem.at[g]))
        outs[-1].start()
        for b in (2 * g, 2 * g + 1):
            for k, (dst, row) in enumerate(((atk, 2 * b + c), (ats, 2 * b + 1 - c))):
                src = at.at[pl.ds(aligned(row * DROWS, 16), DROWS), :]
                outs.append(pltpu.make_async_copy(src, dst.at[b], asem.at[2 * b + k]))
                outs[-1].start()
    arrived(wd, sem.at[2])

    def tile(t, carry):
        rows = pl.ds(aligned(t * 256, 256), 256)
        for half in range(2):
            cols = pl.ds(half * HALF, HALF)
            total = aa[rows, cols] + nn(act[rows, :], wd[half].reshape(FF, HALF))
            new[rows, cols] = total
            low[rows, cols] = total.astype(BF16)
        return carry

    lax.fori_loop(0, 2, tile, 0)
    for copy in outs:
        copy.wait()


def ffn_call(idx, res, mk, mr, gb, qo, ffn):
    return kernel_call(
        ffn_kernel,
        [idx, res, mk, mr, gb, *qo, *ffn],
        [SM, HB, VM, VM, VM] + [HB] * (len(qo) + len(ffn)),
        [
            sds((TOK, D), F32),
            sds((TOK, D), F32),
            sds((TOK, D), BF16),
            sds((8, ROWS, TOK), BF16),
            sds((8, ROWS, TOK), BF16),
            sds((8, ROWS, TOK), BF16),
            sds((8, ROWS, TOK), BF16),
            sds((TOK, FF), BF16),
            sds((8, DROWS, TOK), BF16),
            sds((8, DROWS, TOK), BF16),
        ],
        [VM] * 7 + [HB] * 3,
        [
            OUT_W,
            UP_W,
            DOWN_W,
            pltpu.VMEM((TOK, D), F32),
            pltpu.VMEM((TOK, D), BF16),
            pltpu.VMEM((D, TOK), BF16),
            pltpu.VMEM((TOK, FF), BF16),
            pltpu.VMEM((TOK, FF), BF16),
            pltpu.VMEM((FF, TOK), BF16),
            pltpu.SemaphoreType.DMA((3,)),
            pltpu.SemaphoreType.DMA((1,)),
            pltpu.SemaphoreType.DMA((4,)),
            pltpu.SemaphoreType.DMA((16,)),
        ],
        "ffn",
        FULL,
    )


def down_back_kernel(idx, grad, slope_in, *refs):
    parts, refs = refs[:-5], refs[-5:]
    gu, wd, slope, sem, isem = refs
    copies = load([(slope_in.at[:, pl.ds(g * D, D)], slope.at[g]) for g in range(4)], isem)
    fetch_down(idx[0], idx[1], parts, wd, sem)
    arrived(wd, sem)
    for g in range(4):
        copies[g].wait()
        left = wd[0, g].reshape(D, HALF)
        right = wd[1, g].reshape(D, HALF)

        def tile(t, carry):
            rows = pl.ds(aligned(t * 256, 256), 256)
            part = nt(grad[rows, 0:HALF], left) + nt(grad[rows, HALF:D], right)
            gu[rows, pl.ds(g * D, D)] = (part * slope[g, rows, :].astype(F32)).astype(BF16)
            return carry

        lax.fori_loop(0, 2, tile, 0)


def down_back_call(idx, grad, slope, w):
    return kernel_call(
        down_back_kernel,
        [idx, grad, slope, *w],
        [SM, VM, HB] + [HB] * len(w),
        [sds((TOK, FF), BF16)],
        [VM],
        [
            DOWN_W,
            pltpu.VMEM((4, TOK, D), BF16),
            pltpu.SemaphoreType.DMA,
            pltpu.SemaphoreType.DMA((4,)),
        ],
        "down_back",
    )[0]


def norm_back(x, grad_out, gain):
    n, scale = layer_norm_parts(x)
    e = grad_out * gain
    back = scale * (
        e - jnp.mean(e, axis=-1, keepdims=True) - n * jnp.mean(e * n, axis=-1, keepdims=True)
    )
    gain_part = jnp.sum(grad_out * n, axis=0, keepdims=True)
    bias_part = jnp.sum(grad_out, axis=0, keepdims=True)
    return back, gain_part, bias_part


def up_back_kernel(idx, grad_in, gu, aa_in, gb, *refs):
    qo, ffn, refs = refs[:16], refs[16:-12], refs[-12:]
    ga, gat, gmk, gms, nrm, wu, wo, grad, aa, gh, sem, isem = refs
    f, y, c = idx[0], idx[1], idx[2]
    fetch_up(f, y, ffn, wu, sem.at[0])
    copies = load([(aa_in, aa), (grad_in, grad)], isem)
    fetch_out(f, y, qo, wo, sem.at[1])
    nrm[...] = jnp.zeros_like(nrm)
    gain = gb[1:2, :]
    mine, theirs = pl.ds(c * 2, 2), pl.ds((1 - c) * 2, 2)
    arrived(wu, sem.at[0])

    def wide(t, carry):
        rows = pl.ds(aligned(t * 256, 256), 256)
        total = nt(gu[rows, 0:D], wu[0].reshape(D, D))
        for g in range(1, 4):
            total += nt(gu[rows, pl.ds(g * D, D)], wu[g].reshape(D, D))
        gh[rows, :] = total
        return carry

    lax.fori_loop(0, 2, wide, 0)
    for copy in copies:
        copy.wait()

    def tile(t, carry):
        rows = pl.ds(aligned(t * 128, 128), 128)
        back, gain_part, bias_part = norm_back(aa[rows, :], gh[rows, :], gain)
        total = grad[rows, :] + back
        ga[rows, :] = total
        gat[rows, :] = total.astype(BF16)
        nrm[0:1, :] += gain_part
        nrm[1:2, :] += bias_part
        return carry

    lax.fori_loop(0, 4, tile, 0)
    arrived(wo, sem.at[1])
    for dst, part in ((gmk, mine), (gms, theirs)):
        dst[...] = (
            nt(gat[:, 0:HALF], wo[0, part].reshape(HALF, HALF))
            + nt(gat[:, HALF:D], wo[1, part].reshape(HALF, HALF))
        ).astype(BF16)


def up_back_call(idx, grad, gu, aa, gb, qo, ffn):
    return kernel_call(
        up_back_kernel,
        [idx, grad, gu, aa, gb, *qo, *ffn],
        [SM, HB, VM, HB, VM] + [HB] * (len(qo) + len(ffn)),
        [
            sds((TOK, D), F32),
            sds((TOK, D), BF16),
            sds((TOK, HALF), BF16),
            sds((TOK, HALF), BF16),
            sds((8, D), F32),
        ],
        [VM] * 5,
        [
            UP_W,
            OUT_W,
            pltpu.VMEM((TOK, D), F32),
            pltpu.VMEM((TOK, D), F32),
            pltpu.VMEM((TOK, D), F32),
            pltpu.SemaphoreType.DMA((2,)),
            pltpu.SemaphoreType.DMA((2,)),
        ],
        "up_back",
    )


def attend_back_kernel(
    idx, kept, pics, lse, own, other, gown, gother, down_, doth, s, g, la, d, dk, dv, ds, tab, sem
):
    c = idx[2]
    copies = load_halves([(own, other, s)], c, BLK, sem)
    copies += load_halves([(gown, gother, g)], c, 0, sem.at[pl.ds(2, 2)])
    s[0:BLK, :] = jnp.zeros((BLK, 1280), BF16)
    mask_tiles(tab)
    dk[...] = jnp.zeros_like(dk)
    dv[...] = jnp.zeros_like(dv)
    ds[...] = jnp.zeros_like(ds)
    for copy in copies:
        copy.wait()
    split_log_sigmoid(s, la)
    lane = lax.broadcasted_iota(jnp.int32, (BLK, BLK), 1)

    def step(i, carry):
        starts, follows = picture_flags(pics, i)

        def run(blocks):
            rows = pl.ds(aligned(i * BLK, BLK), BLK)
            cut = blocks * BLK
            for pair in range(3):
                cols = pl.ds(pair * BLK, BLK)
                logits, q, k, v, near, far, first = pair_logits(
                    s, la, tab, kept, i, pair, blocks, starts, follows
                )
                logs = [lse[2 * pair + odd : 2 * pair + odd + 1, rows] for odd in range(2)]
                probs = jnp.exp(logits - jnp.concatenate(logs, axis=1))
                gm = g[rows, cols]
                zero = jnp.zeros_like(gm)
                gm = jnp.concatenate([jnp.where(first, gm, zero), jnp.where(first, zero, gm)], axis=0)
                gprob = nt(v, gm)
                inner = jnp.sum(probs * gprob, axis=0, keepdims=True)
                gl = (probs * (gprob - inner)).astype(BF16)
                gv = nn(probs.astype(BF16), gm)
                heads = [jnp.where(lane == 2 * pair + odd, 1.0, 0.0) for odd in range(2)]
                heads = jnp.concatenate(heads, axis=0).astype(BF16)
                gk = nn(gl, jnp.concatenate([q, heads], axis=1))
                dv[near, cols] += gv[:cut]
                dk[near, cols] += gk[:cut, :BLK]
                ds[near, :] += gk[:cut, BLK:]
                for odd in range(2):
                    mine = jnp.logical_not(first) if odd else first
                    dv[far[odd], cols] += jnp.where(mine, gv[cut:], 0.0)
                    dk[far[odd], cols] += jnp.where(mine, gk[cut:, :BLK], 0.0)
                    ds[far[odd], :] += jnp.where(lane == 2 * pair + odd, gk[cut:, BLK:], 0.0)
                dq = tn(gl, k)
                dq = jnp.where(first, dq[:BLK], dq[BLK:]) * (HEAD_DIM**-0.5)
                d[rows, cols] = dq.astype(BF16)

        @pl.when(starts)
        def _():
            run(3)

        @pl.when(jnp.logical_not(starts))
        def _():
            run(2)

        return carry

    lax.fori_loop(0, 8, step, 0)
    keys = pl.ds(BLK, SEQ)
    d[:, HALF : 2 * HALF] = dk[keys, :].astype(BF16)
    d[:, 2 * HALF : 3 * HALF] = dv[keys, :].astype(BF16)
    back = ds[keys, :] * jax.nn.sigmoid(-s[keys, 1152:1280].astype(F32))
    d[:, 1152:1280] = back.astype(BF16)
    down_[...] = d[pl.ds(aligned(c * TOK, TOK), TOK), :]
    doth[...] = d[pl.ds(aligned((1 - c) * TOK, TOK), TOK), :]


def attend_back_call(idx, kept, pics, lse, own, other, gown, gother):
    return kernel_call(
        attend_back_kernel,
        [idx, kept, pics, lse, own, other, gown, gother],
        [SM, SM, SM, VM, HB, HB, HB, HB],
        [sds((TOK, 1280), BF16), sds((TOK, 1280), BF16)],
        [VM, VM],
        [
            pltpu.VMEM((SEQ + BLK, 1280), BF16),
            pltpu.VMEM((SEQ, HALF), BF16),
            pltpu.VMEM((SEQ + BLK, BLK), BF16),
            pltpu.VMEM((SEQ, 1280), BF16),
            pltpu.VMEM((SEQ + BLK, HALF), F32),
            pltpu.VMEM((SEQ + BLK, HALF), F32),
            pltpu.VMEM((SEQ + BLK, BLK), F32),
            pltpu.VMEM((5, BLK, BLK), F32),
            pltpu.SemaphoreType.DMA((4,)),
        ],
        "attend_back",
    )


def qkv_back_kernel(idx, ga_in, down_, dr, res_in, gb, sw0, sw1, *refs):
    parts, refs = refs[:-9], refs[-9:]
    gout, glow, nrm, w, ga, res, gh, sem, isem = refs
    c = idx[2]
    fetch_qkv(idx[0], idx[1], parts, w, sem)
    copies = load([(res_in, res), (ga_in, ga)], isem)
    nrm[...] = jnp.zeros_like(nrm)
    gain = gb[0:1, :]
    arrived(w, sem)

    def wide(t, carry):
        rows = pl.ds(aligned(t * 256, 256), 256)
        total = nn(down_[rows, 1152:1280], sw0[...]) + nn(dr[rows, 1152:1280], sw1[...])
        for j in range(3):
            cols = pl.ds(j * HALF, HALF)
            total += nt(down_[rows, cols], w[2 * j + c].reshape(D, HALF))
            total += nt(dr[rows, cols], w[2 * j + 1 - c].reshape(D, HALF))
        gh[rows, :] = total
        return carry

    lax.fori_loop(0, 2, wide, 0)
    for copy in copies:
        copy.wait()

    def tile(t, carry):
        rows = pl.ds(aligned(t * 128, 128), 128)
        back, gain_part, bias_part = norm_back(res[rows, :], gh[rows, :], gain)
        total = ga[rows, :] + back
        gout[rows, :] = total
        glow[rows, :] = total.astype(BF16)
        nrm[0:1, :] += gain_part
        nrm[1:2, :] += bias_part
        return carry

    lax.fori_loop(0, 4, tile, 0)


def qkv_back_call(idx, ga, down_, dr, res, gb, sw0, sw1, w):
    return kernel_call(
        qkv_back_kernel,
        [idx, ga, down_, dr, res, gb, sw0, sw1, *w],
        [SM, HB, VM, VM, HB, VM, VM, VM] + [HB] * len(w),
        [sds((TOK, D), F32), sds((TOK, D), BF16), sds((8, D), F32)],
        [VM, VM, VM],
        [
            QKV_W,
            pltpu.VMEM((TOK, D), F32),
            pltpu.VMEM((TOK, D), F32),
            pltpu.VMEM((TOK, D), F32),
            pltpu.SemaphoreType.DMA,
            pltpu.SemaphoreType.DMA((2,)),
        ],
        "qkv_back",
    )


def scatter_rows(src, f, rows, offset, pyy, portion, outs, n, cols):
    if len(outs) == 1:
        for block in range(8):
            value = src[pl.ds(block * rows + offset, ROWS), :]
            outs[0][2 * block + pyy, portion, n, :, cols] = value
        return
    ka, sa, kb, sb = outs
    for pxx in range(2):
        for pz in range(4):
            block = (f >> 1) ^ (pz * 2 + pxx)
            value = src[pl.ds(aligned(block * rows + offset, 16), ROWS), :]
            if portion == 0:
                (sa if pxx else ka)[pyy, pz, n, :, cols] = value
            else:
                (sb if pyy else kb)[pxx, pz, n, :, cols] = value


def up_grads_into(f, y, xk, xr, gk, gr, outs, tmp, n):
    for portion in range(2):
        for pyy in range(2):
            cols = pl.ds(aligned((y ^ pyy) * 1536 + portion * D, 128), D)
            slot = portion * 2 + pyy
            tmp[slot] = (nn(xk[...], gk[:, cols]) + nn(xr[...], gr[:, cols])).astype(BF16)
            scatter_rows(tmp.at[slot], f, ROWS, 0, pyy, portion, outs, n, pl.ds(0, D))


def down_grads_into(f, y, ak, ar, dk, dr, outs, tmp, n):
    for pyy in range(2):
        cols = pl.ds(aligned((y ^ pyy) * HALF, 128), HALF)

        def tile(t, carry):
            rows = pl.ds(aligned(t * HALF, HALF), HALF)
            value = nn(ak[rows, :], dk[:, cols]) + nn(ar[rows, :], dr[:, cols])
            tmp[pyy, rows, :] = value.astype(BF16)
            return carry

        lax.fori_loop(0, 4, tile, 0)
        for portion in range(2):
            for k in range(2):
                offset, half = (portion * 2 + k) * ROWS, pl.ds(k * HALF, HALF)
                scatter_rows(tmp.at[pyy], f, DROWS, offset, pyy, portion, outs, n, half)


def qkv_grads_into(y, xk, xr, mk, mr, dy, gk, gr, outs, tmp, f):
    for pyy in range(2):
        y2 = y ^ pyy
        for part in range(4):
            portion, side = part // 2, part % 2
            if part < 3:
                g = y2 * 3 + part
                value = nn(xk[...], dy[0, g]) + nn(xr[...], dy[1, g])
            else:
                oc = pl.ds(aligned(y2 * HALF, 128), HALF)
                value = nn(mk[...], gk[:, oc]) + nn(mr[...], gr[:, oc])
            tmp[portion * 2 + pyy, :, pl.ds(side * HALF, HALF)] = value.astype(BF16)
        for portion in range(2):
            slot = portion * 2 + pyy
            scatter_rows(tmp.at[slot], f, ROWS, 0, pyy, portion, outs, 0, pl.ds(0, D))


def score_grads_into(f, c, xk, xr, tsc, sc):
    own = nn(xk[...], tsc[0]) + nn(xr[...], tsc[2])
    theirs = nn(xk[...], tsc[1]) + nn(xr[...], tsc[3])
    first = jnp.where(c == 0, own, theirs)
    second = jnp.where(c == 0, theirs, own)
    both = first + pltpu.roll(second, 64, 1)
    for pxx in range(2):
        for pz in range(4):
            target = (f >> 1) ^ (pz * 2 + pxx)
            for b in range(8):

                @pl.when(target == b)
                def _():
                    sc[pxx, pz] = both[b * ROWS : (b + 1) * ROWS, :]


def start_outputs_grads(c, grads, dy, tsc, sem):
    copies = []
    for tok in range(2):
        for k in range(2):
            src = grads[tok * 2 + k]
            for j in range(3):
                part = src.at[:, pl.ds(j * HALF, HALF)]
                at = sem.at[tok * 8 + k * 4 + j]
                copies.append(pltpu.make_async_copy(part, dy.at[tok, 2 * j + (c ^ k)], at))
            part = src.at[:, pl.ds(1152, 128)]
            at = sem.at[tok * 8 + k * 4 + 3]
            copies.append(pltpu.make_async_copy(part, tsc.at[tok * 2 + k], at))
    for copy in copies:
        copy.start()
    return copies


def wait_all(copies):
    for copy in copies:
        copy.wait()


FFN_SHAPES = [(4 * HALF, TOK)] * 2 + [(TOK, D)] * 2 + [(HALF, TOK)] * 2 + [(TOK, FF)] * 2
QKV_SHAPES = [(HALF, TOK)] * 4 + [(TOK, D)] * 2
DY_SCRATCH = [pltpu.VMEM((2, 6, TOK, HALF), BF16), pltpu.VMEM((4, TOK, 128), BF16)]


def ffn_grad_kernel(idx, *refs):
    ins, outs, refs = refs[:8], refs[8:12], refs[12:]
    held, (tmp, tmp2, sem) = refs[:8], refs[8:]
    copies = load(list(zip(ins, held)), sem)
    ak, ar, dk, dr, xk, xr, gk, gr = held
    wait_all(copies[:4])
    down_grads_into(idx[0], idx[1], ak, ar, dk, dr, outs, tmp2, 1)
    wait_all(copies[4:])
    up_grads_into(idx[0], idx[1], xk, xr, gk, gr, outs, tmp, 0)


def ffn_grad_call(idx, xk, xr, gk, gr, ak, ar, dk, dr):
    ins = [v.reshape(4 * HALF, TOK) for v in (ak, ar)] + [dk, dr]
    ins += [v.reshape(HALF, TOK) for v in (xk, xr)] + [gk, gr]
    return kernel_call(
        ffn_grad_kernel,
        [idx, *ins],
        [SM] + [HB] * 8,
        [sds((2, 4, 2, ROWS, D), BF16)] * 4,
        [VM] * 4,
        [pltpu.VMEM(shape, BF16) for shape in FFN_SHAPES]
        + [pltpu.VMEM((4, HALF, D), BF16), pltpu.VMEM((2, 4 * HALF, HALF), BF16)]
        + [pltpu.SemaphoreType.DMA((8,))],
        "ffn_grad",
    )


def qkv_grad_kernel(idx, *refs):
    ins, grads, outs, sc, refs = refs[:6], refs[6:10], refs[10:14], refs[14], refs[15:]
    held, (dy, tsc, tmp, sem, isem) = refs[:6], refs[6:]
    f, y, c = idx[0], idx[1], idx[2]
    copies = start_outputs_grads(c, grads, dy, tsc, sem) + load(list(zip(ins, held)), isem)
    xk, xr, mk, mr, gk, gr = held
    wait_all(copies)
    qkv_grads_into(y, xk, xr, mk, mr, dy, gk, gr, outs, tmp, f)
    score_grads_into(f, c, xk, xr, tsc, sc)


def qkv_grad_call(idx, xk, xr, mk, mr, d00, d01, d10, d11, gk, gr):
    ins = [v.reshape(HALF, TOK) for v in (xk, xr, mk, mr)] + [gk, gr, d00, d01, d10, d11]
    return kernel_call(
        qkv_grad_kernel,
        [idx, *ins],
        [SM] + [HB] * 10,
        [sds((2, 4, 1, ROWS, D), BF16)] * 4 + [sds((2, 4, ROWS, 128), F32)],
        [VM] * 5,
        [pltpu.VMEM(shape, BF16) for shape in QKV_SHAPES]
        + DY_SCRATCH
        + [pltpu.VMEM((4, HALF, D), BF16)]
        + [pltpu.SemaphoreType.DMA((16,)), pltpu.SemaphoreType.DMA((6,))],
        "qkv_grad",
    )


def layer_grad_kernel(idx, *refs):
    ins, grads, out, sc, refs = refs[:14], refs[14:18], refs[18], refs[19], refs[20:]
    held, (dy, tsc, tmp, tmp2, sem, isem) = refs[:14], refs[14:]
    f, c = idx[0], idx[2]
    copies = load(list(zip(ins, held)), isem)
    more = start_outputs_grads(c, grads, dy, tsc, sem)
    ak, ar, dk, dr, xk, xr, gk, gr = held[:8]
    wait_all(copies[:4])
    down_grads_into(0, 0, ak, ar, dk, dr, [out], tmp2, 2)
    wait_all(copies[4:8])
    up_grads_into(0, 0, xk, xr, gk, gr, [out], tmp, 1)
    wait_all(copies[8:] + more)
    xk, xr, mk, mr, gk, gr = held[8:]
    qkv_grads_into(0, xk, xr, mk, mr, dy, gk, gr, [out], tmp, 0)
    score_grads_into(f, c, xk, xr, tsc, sc)


def layer_grad_call(idx, ffn, qkv):
    xk, xr, gk, gr, ak, ar, dk, dr = ffn
    ins = [v.reshape(4 * HALF, TOK) for v in (ak, ar)] + [dk, dr]
    ins += [v.reshape(HALF, TOK) for v in (xk, xr)] + [gk, gr]
    xk, xr, mk, mr, d00, d01, d10, d11, gk, gr = qkv
    ins += [v.reshape(HALF, TOK) for v in (xk, xr, mk, mr)] + [gk, gr, d00, d01, d10, d11]
    return kernel_call(
        layer_grad_kernel,
        [idx, *ins],
        [SM] + [HB] * 18,
        [sds((16, 2, 3, ROWS, D), BF16), sds((2, 4, ROWS, 128), F32)],
        [VM] * 2,
        [pltpu.VMEM(shape, BF16) for shape in FFN_SHAPES + QKV_SHAPES]
        + DY_SCRATCH
        + [pltpu.VMEM((4, HALF, D), BF16), pltpu.VMEM((2, 4 * HALF, HALF), BF16)]
        + [pltpu.SemaphoreType.DMA((16,)), pltpu.SemaphoreType.DMA((14,))],
        "layer_grad",
    )


def cross_kernel(ka, ra, kb, rb, qa, qb):
    for k, r, q in ((ka, ra, qa), (kb, rb, qb)):
        q[...] = (k[...].astype(F32) + r[...].astype(F32)).astype(BF16)[0]


def cross_call(ka, ra, kb, rb):
    n = ka.shape[2]
    block = pl.BlockSpec((1, 1, n, ROWS, D), lambda z: (1, z, 0, 0, 0))
    out = pl.BlockSpec((1, n, ROWS, D), lambda z: (z, 0, 0, 0))
    return pl.pallas_call(
        cross_kernel,
        out_shape=(sds((4, n, ROWS, D), BF16),) * 2,
        grid=(4,),
        in_specs=[block] * 4,
        out_specs=(out,) * 2,
        cost_estimate=duration(COST["cross"]),
        name="cross",
    )(ka, ra, kb, rb)


def own_kernel(ka, ra, ca, kb, rb, cb, *outs):
    z = pl.program_id(0)
    for part, (k, r, q) in enumerate(((ka, ra, ca), (kb, rb, cb))):
        total = k[0, 0].astype(F32) + r[0, 0].astype(F32) + q[0].astype(F32)
        for t in range(4):

            @pl.when(z == t)
            def _():
                outs[t][part] = total.astype(outs[t].dtype)


def own_call(ka, ra, ca, kb, rb, cb):
    n = ka.shape[2]
    block = pl.BlockSpec((1, 1, n, ROWS, D), lambda z: (0, z, 0, 0, 0))
    quarter = pl.BlockSpec((1, n, ROWS, D), lambda z: (z, 0, 0, 0))
    out = pl.BlockSpec((2, n, ROWS, D), lambda z: (0, 0, 0, 0))
    return pl.pallas_call(
        own_kernel,
        out_shape=tuple(sds((2, n, ROWS, D), F32 if t == 0 else BF16) for t in range(4)),
        grid=(4,),
        in_specs=[block, block, quarter] * 2,
        out_specs=(out,) * 4,
        cost_estimate=duration(COST["own"]),
        name="own",
    )(ka, ra, ca, kb, rb, cb)


def pairwise(v, bits):
    return lax.ppermute(v, "zx", [(i, i ^ bits) for i in range(8)])


def over_ctx(v):
    return lax.ppermute(v, "ctx", [(0, 1), (1, 0)])


def over_core(v):
    return lax.ppermute(v, "core", [(0, 1), (1, 0)])


def over_x(v):
    return pairwise(v, 1)


def diagonal(v):
    return lax.ppermute(v, ("zx", "ctx"), [(i, i ^ 3) for i in range(16)])


def turn(v):
    return lax.ppermute(v, ("core", "ctx"), [(0, 0), (1, 2), (2, 1), (3, 3)])


class Chain:
    def __init__(self, stages):
        self.stages, self.result = stages, None
        self.flying = next(stages)

    def advance(self, arrived):
        try:
            self.flying = self.stages.send(arrived)
        except StopIteration as stop:
            self.flying, self.result = None, stop.value


class Order:
    def __init__(self, idx):
        self.gate = idx

    def after(self, value):
        return lax.optimization_barrier((value, self.gate))[0]

    def passed(self, value):
        self.gate, value = lax.optimization_barrier((self.gate, value))
        return value

    def meet(self, *chains):
        for chain, items in zip(chains, self.passed([c.flying for c in chains])):
            chain.advance(items)


def gather_stages(both, z):
    near = yield [pairwise(both, k << 1) for k in range(1, 4)]
    near = [both] + near
    near = [lax.select_n(z, *(near[k ^ t] for t in range(4))) for k in range(4)]
    a, b = (jnp.stack([v[part] for v in near]) for part in range(2))
    xa, yb, ya, xb = yield [over_x(a), over_ctx(b), over_ctx(a), over_x(b)]
    a, b = [a, xa, ya], [b, xb, yb]
    da, db, *other = yield [over_ctx(xa), over_x(yb)] + [over_core(v) for v in a + b]
    ca, cb = yield [over_core(da), over_core(db)]
    return a + [da] + other[:3] + [ca] + b + [db] + other[3:] + [cb]


def small_gather_stages(small, start):
    *near, start = yield [pairwise(small, k << 1) for k in range(1, 4)] + [start]
    small = jnp.stack([small] + near)
    (r,) = yield [over_x(small)]
    small = jnp.concatenate([small, r])
    (r,) = yield [over_core(small)]
    return jnp.concatenate([small, r]), start


def reduce_stages(ka, sa, kb, sb):
    ra, rb = yield [over_x(sa), over_ctx(sb)]
    qa, qb = cross_call(ka, ra, kb, rb)
    ca, cb = yield [over_ctx(qa), over_x(qb)]
    total, *low = own_call(ka, ra, ca, kb, rb, cb)
    rest = yield [pairwise(v, k << 1) for k, v in enumerate(low, 1)]
    return total + sum(v.astype(F32) for v in rest)


def small_stages(t):
    ry, rx, rd = yield [over_ctx(t[0]), over_x(t[1]), diagonal(t[1])]
    t = t[0] + ry + (rx + rd)
    rest = yield [pairwise(t[k], k << 1) for k in range(1, 4)]
    return t[0] + sum(rest)


def pair_device(
    tokens,
    cotangent,
    kept_blocks,
    picture_starts,
    qkv_weight,
    score_weight,
    out_weight,
    up_weight,
    down_weight,
    norm_gain,
    norm_bias,
):
    zx = lax.axis_index("zx").astype(jnp.int32)
    y = lax.axis_index("ctx").astype(jnp.int32)
    c = lax.axis_index("core").astype(jnp.int32)
    f = zx * 2 + c
    idx = jnp.stack([f, y, c])
    order = Order(idx)

    def shards(l):
        joined = jnp.concatenate([qkv_weight[l], out_weight[l]], axis=1)
        up = up_weight[l].reshape(ROWS, 2, D).swapaxes(0, 1)
        down = down_weight[l].reshape(2, 2, ROWS, HALF).swapaxes(1, 2).reshape(2, ROWS, D)
        return jnp.stack([joined[:, :D], joined[:, D:]]), up, down

    def gather(v):
        return Chain(gather_stages(order.after(v), zx >> 1))

    w = [shards(l) for l in range(LAYERS)]
    qo0 = gather(w[0][0][:, None])
    kept = jnp.where(c == y, kept_blocks[0], over_core(kept_blocks[0]))
    pics = jnp.where(c == y, picture_starts[0], over_core(picture_starts[0]))
    kept = lax.dynamic_slice_in_dim(kept, c * 6, 6, 0)
    small = jnp.concatenate(
        [jnp.swapaxes(score_weight, 1, 2), norm_gain, norm_bias], axis=1
    ).reshape(LAYERS * 16, ROWS)
    small = jnp.pad(small, ((0, 0), (0, 128 - ROWS)))
    small = Chain(small_gather_stages(small, turn(tokens[0])))
    ffn0 = lax.all_gather(jnp.stack(w[0][1:], axis=1), ("zx", "ctx"), axis=0, tiled=False)
    order.meet(qo0, small)
    order.meet(qo0, small)
    order.meet(qo0, small)
    order.meet(qo0)
    qo0 = qo0.result
    small, residual = small.result
    residual = residual.astype(F32)
    away = jnp.arange(16, dtype=jnp.int32) ^ f
    small = jnp.take(small, (away & 1) * 8 + ((away >> 1) & 1) * 4 + (away >> 2), axis=0)
    small = jnp.moveaxis(small[:, :, :ROWS], 0, 1).reshape(LAYERS, 16, D)
    scale = []
    for l in range(LAYERS):
        gb = jnp.pad(small[l, 12:16].astype(F32), ((0, 4), (0, 0)))
        own_rows = lax.dynamic_slice_in_dim(small[l], c * 6, 6, 0)
        other_rows = lax.dynamic_slice_in_dim(small[l], (1 - c) * 6, 6, 0)
        pad = ((0, 122), (0, 0))
        scale.append((gb, jnp.pad(own_rows, pad), jnp.pad(other_rows, pad)))

    def qkv(l, residual, w):
        own, send, xk, xs = order.passed(qkv_call(order.gate, residual, *scale[l], w))
        return own, over_core(send), xk, over_core(xs)

    def attend(head):
        mixed, send, lse = order.passed(attend_call(order.gate, kept, pics, head[0], head[1]))
        return (mixed, over_core(send)), lse

    def feed(l, residual, mixed, qo, ffn):
        outs = ffn_call(order.gate, residual, *mixed, scale[l][0], qo, ffn)
        after, new, low, mk, ms, hk, hs, slope, ak, as_ = order.passed(outs)
        hr, ar, mr = over_core(hs), over_core(as_), over_core(ms)
        return new, low, (after, slope, (hk, hr), (ak, ar), (mk, mr))

    qo1 = gather(w[1][0][:, None])
    head0 = qkv(0, residual, qo0)
    order.meet(qo1)
    ffn1 = gather(jnp.stack(w[1][1:], axis=1))
    mixed, lse0 = attend(head0)
    order.meet(qo1, ffn1)
    order.meet(qo1)
    ffn0 = order.passed(ffn0)
    ffn0 = order.passed([v.reshape(4, 2, 2, 2, 2, ROWS, D) for v in (ffn0, over_core(ffn0))])
    res1, _, out0 = feed(0, residual, mixed, qo0, ffn0)
    order.meet(qo1, ffn1)
    qo1 = qo1.result
    head1 = qkv(1, res1, qo1)
    order.meet(ffn1)
    mixed, lse1 = attend(head1)
    order.meet(ffn1)
    ffn1 = ffn1.result
    cot = turn(order.after(cotangent[0]))
    _, low, out1 = feed(1, res1, mixed, qo1, ffn1)
    block_output = turn(low).astype(F32)

    weights = ((qo0, ffn0), (qo1, ffn1))

    def down_back(l, low, out):
        gu = order.passed(down_back_call(order.gate, low, out[1], weights[l][1]))
        return gu, over_core(gu)

    def up_back(l, grad, gu, out):
        ga, gat, gmk, gms, nrm = order.passed(
            up_back_call(order.gate, grad, gu, out[0], scale[l][0], *weights[l])
        )
        return ga, nrm, (gmk, over_core(gms)), (gat, over_core(gat))

    def attend_back(head, lse, gm):
        d_own, d_oth = order.passed(
            attend_back_call(order.gate, kept, pics, lse, head[0], head[1], *gm)
        )
        return d_own, over_core(d_oth), d_oth, over_core(d_own)

    def qkv_grads(head, out, d, gat):
        return order.passed(qkv_grad_call(order.gate, head[2], head[3], *out[4], *d, *gat))

    def qkv_back(l, ga, d, res, head):
        return order.passed(qkv_back_call(order.gate, ga, d[0], d[1], res, *scale[l], weights[l][0]))

    scores, norms = [None] * LAYERS, [None] * LAYERS
    low, low_r = cot, over_core(cot)
    gu, gu_r = down_back(1, low, out1)
    ga, nrm2, gm, gat = up_back(1, cot.astype(F32), gu, out1)
    d = attend_back(head1, lse1, gm)
    grad, new_low, nrm1 = qkv_back(1, ga, d, res1, head1)
    ffn = (*out1[2], gu, gu_r, *out1[3], low, low_r)
    qkv_parts = (head1[2], head1[3], *out1[4], *d, *gat)
    grads1, scores[1] = order.passed(layer_grad_call(order.gate, ffn, qkv_parts))
    grads1 = lax.psum_scatter(grads1, ("zx", "ctx"), scatter_dimension=0, tiled=False)
    low, low_r = new_low, over_core(new_low)
    norms[1] = jnp.concatenate([nrm1[0:1], nrm2[0:1], nrm1[1:2], nrm2[1:2]])
    gu, gu_r = down_back(0, low, out0)
    gu_r = order.passed(gu_r)
    grads = ffn_grad_call(order.gate, *out0[2], gu, gu_r, *out0[3], low, low_r)
    ffn0 = Chain(reduce_stages(*order.passed(grads)))
    ga, nrm2, gm, gat = up_back(0, grad, gu, out0)
    d = attend_back(head0, lse0, gm)
    order.meet(ffn0)
    *g, scores[0] = qkv_grads(head0, out0, d, gat)
    qo0 = Chain(reduce_stages(*g))
    grad, low, nrm1 = qkv_back(0, ga, d, residual, head0)
    norms[0] = jnp.concatenate([nrm1[0:1], nrm2[0:1], nrm1[1:2], nrm2[1:2]])
    nrm = jnp.concatenate(norms).reshape(8, 8, 2, ROWS)
    mine, theirs = (lax.dynamic_index_in_dim(nrm, b, 2, keepdims=False) for b in (c, 1 - c))
    nrm = jnp.moveaxis(mine + over_core(theirs), 0, 2)
    nrm = jnp.take(nrm, zx ^ jnp.array([0, 2, 4, 6, 1, 3, 5, 7], jnp.int32), axis=0)
    nrm = nrm.reshape(2, 4, ROWS, 8)
    lanes = [jnp.concatenate([s[..., :6], s[..., 64:70]], -1) for s in scores] + [nrm]
    lanes = jnp.pad(jnp.concatenate(lanes, -1), ((0, 0), (0, 0), (0, 0), (0, 96)))
    lanes = Chain(small_stages(lanes))
    token_grad = turn(low)
    order.meet(ffn0, qo0, lanes)
    order.meet(ffn0, qo0, lanes)
    order.meet(qo0)
    token_grad = order.passed(token_grad).astype(F32)
    lanes = order.after(lanes.result)
    score_grad = jnp.stack([lanes[:, 0:12], lanes[:, 12:24]])
    nrm = lanes[:, 24:32].T.reshape(LAYERS, 2, 2, ROWS)
    grads1 = grads1.astype(F32)
    qo = [qo0.result[:, 0], grads1[:, 0]]
    qkv_grad = jnp.stack([jnp.concatenate([v[0], v[1, :, :HALF]], 1) for v in qo])
    out_grad = jnp.stack([v[1, :, HALF:] for v in qo])
    ffn = [ffn0.result, grads1[:, 1:]]
    up_grad = jnp.stack([jnp.concatenate([v[0, 0], v[1, 0]], 1) for v in ffn])
    down_grad = jnp.stack(
        [v[:, 1].reshape(2, ROWS, 2, HALF).swapaxes(1, 2).reshape(DROWS, HALF) for v in ffn]
    )
    return (
        block_output[None],
        token_grad[None],
        qkv_grad,
        score_grad,
        out_grad,
        up_grad,
        down_grad,
        nrm[:, 0],
        nrm[:, 1],
    )


def solution(mesh):
    in_specs = (
        P("fsdp", "ctx", None),
        P("fsdp", "ctx", None),
        P("fsdp", None, None),
        P("fsdp", None),
        P(None, "fsdp", "ctx"),
        P(None, "fsdp", None),
        P(None, "fsdp", "ctx"),
        P(None, "fsdp", "ctx"),
        P(None, "fsdp", "ctx"),
        P(None, None, "fsdp"),
        P(None, None, "fsdp"),
    )
    out_specs = (
        P("fsdp", "ctx", None),
        P("fsdp", "ctx", None),
        P(None, "fsdp", "ctx"),
        P(None, "fsdp", None),
        P(None, "fsdp", "ctx"),
        P(None, "fsdp", "ctx"),
        P(None, "fsdp", "ctx"),
        P(None, None, "fsdp"),
        P(None, None, "fsdp"),
    )
    step = per_device
    if mesh.shape["fsdp"] == 16 and mesh.shape["ctx"] == 2:
        step = pair_device
        mesh = Mesh(mesh.devices.reshape(8, 2, 2), ("zx", "core", "ctx"))
        in_specs, out_specs = (
            tuple(P(*(("zx", "core") if a == "fsdp" else a for a in spec)) for spec in specs)
            for specs in (in_specs, out_specs)
        )
    return jax.shard_map(
        step, mesh=mesh, in_specs=in_specs, out_specs=out_specs, check_vma=False
    )
```

```python
import math
from functools import partial

import jax
import jax.numpy as jnp
from jax import lax
from jax.experimental import pallas as pl
from jax.experimental.pallas import tpu as pltpu
from jax.sharding import Mesh
from jax.sharding import PartitionSpec as P

HEADS = 12
HEAD_DIM = 64
LAYERS = 2
BLK = 128
WINDOW = 64
PIC_LEN = 256


def normalize(residual, gain, bias):
    mean_value = jnp.mean(residual, axis=-1, keepdims=True)
    centered = residual - mean_value
    variance = jnp.mean(centered * centered, axis=-1, keepdims=True)
    return centered * lax.rsqrt(variance + 1e-05) * gain + bias


def gelu_tanh(value):
    return jax.nn.gelu(value, approximate=True)


def log_sigmoid(value):
    return -(jnp.maximum(-value, 0.0) + jnp.log1p(jnp.exp(-jnp.abs(value))))


def split_heads(tensor):
    return jnp.moveaxis(tensor.reshape(tensor.shape[:-1] + (HEADS, HEAD_DIM)), 2, 0)


def join_heads(tensor):
    moved = jnp.moveaxis(tensor, 0, 2)
    return moved.reshape(moved.shape[:2] + (HEADS * HEAD_DIM,))


def masked_logits(queries, keys, scores, kept, base, causal, key_block):
    logits = jnp.einsum(
        "sqd,skd->sqk", queries, keys, preferred_element_type=jnp.float32
    ) * HEAD_DIM ** (-0.5)
    logits = logits + log_sigmoid(scores.astype(jnp.float32))[:, None, :]
    allowed = base | causal[None] & (key_block[None, None, :] == kept[:, :, None])
    return (logits, allowed)


def attend_head(items, base, causal, key_block):
    queries, keys, values, scores, kept = items
    logits, allowed = masked_logits(queries, keys, scores, kept, base, causal, key_block)
    logits = jnp.where(allowed, logits, -1e30)
    largest = jnp.max(logits, axis=-1, keepdims=True)
    weights = jnp.exp(logits - largest)
    totals = jnp.sum(weights, axis=-1, keepdims=True)
    probs_low = (weights / totals).astype(jnp.bfloat16)
    outputs = jnp.einsum("sqk,skd->sqd", probs_low, values, preferred_element_type=jnp.float32)
    return (outputs, (largest + jnp.log(totals))[..., 0])


def query_side_grads(items, base, causal, key_block):
    queries, keys, values, scores, kept, grad_out, log_totals = items
    logits, allowed = masked_logits(queries, keys, scores, kept, base, causal, key_block)
    probs = jnp.where(allowed, jnp.exp(logits - log_totals[..., None]), 0.0)
    grad_probs = jnp.einsum("sqd,skd->sqk", grad_out, values, preferred_element_type=jnp.float32)
    inner = jnp.sum(probs * grad_probs, axis=-1, keepdims=True)
    grad_logits = (probs * (grad_probs - inner)).astype(jnp.bfloat16)
    grad_queries = jnp.einsum(
        "sqk,skd->sqd", grad_logits, keys, preferred_element_type=jnp.float32
    ) * HEAD_DIM ** (-0.5)
    return (grad_queries, inner[..., 0])


def key_side_grads(items, base, causal, key_block):
    queries, keys, values, scores, kept, grad_out, log_totals, inner = items
    logits, allowed = masked_logits(queries, keys, scores, kept, base, causal, key_block)
    probs = jnp.where(allowed, jnp.exp(logits - log_totals[..., None]), 0.0)
    grad_probs = jnp.einsum("sqd,skd->sqk", grad_out, values, preferred_element_type=jnp.float32)
    grad_logits = (probs * (grad_probs - inner[..., None])).astype(jnp.bfloat16)
    grad_values = jnp.einsum(
        "sqk,sqd->skd", probs.astype(jnp.bfloat16), grad_out, preferred_element_type=jnp.float32
    )
    grad_keys = jnp.einsum(
        "sqk,sqd->skd", grad_logits, queries, preferred_element_type=jnp.float32
    ) * HEAD_DIM ** (-0.5)
    grad_scores = jnp.sum(grad_logits.astype(jnp.float32), axis=1) * jax.nn.sigmoid(
        -scores.astype(jnp.float32)
    )
    return (grad_keys, grad_values, grad_scores)


def build_masks(kept_blocks, picture_starts, query_start, query_len, key_start, key_len):
    query_pos = query_start + jnp.arange(query_len, dtype=jnp.int32)
    key_pos = key_start + jnp.arange(key_len, dtype=jnp.int32)
    causal = key_pos[None, :] <= query_pos[:, None]
    local = causal & (query_pos[:, None] - key_pos[None, :] < WINDOW)
    starts = picture_starts[:, :, None]
    inside_query = (query_pos[None, None, :] >= starts) & (
        query_pos[None, None, :] < starts + PIC_LEN
    )
    inside_key = (key_pos[None, None, :] >= starts) & (key_pos[None, None, :] < starts + PIC_LEN)
    picture = jnp.any(inside_query[:, :, :, None] & inside_key[:, :, None, :], axis=1)
    base = local[None] | picture
    kept_all = jnp.repeat(kept_blocks, BLK, axis=2)
    kept_rows = jnp.moveaxis(lax.dynamic_slice_in_dim(kept_all, query_start, query_len, 2), 1, 0)
    return (base, causal, key_pos // BLK, kept_rows)


def forward_layer(residual, weights, masks):
    qkv_w, score_w, out_w, up_w, down_w, gain, bias = weights
    base, causal, key_block, kept_rows = masks
    gains = gain.astype(jnp.float32)
    biases = bias.astype(jnp.float32)
    hidden = normalize(residual, gains[0], biases[0]).astype(jnp.bfloat16)
    qkv = jnp.dot(hidden, qkv_w, preferred_element_type=jnp.float32).astype(jnp.bfloat16)
    scores = jnp.dot(hidden, score_w, preferred_element_type=jnp.float32).astype(jnp.bfloat16)
    queries, keys, values = jnp.split(qkv, 3, axis=-1)
    all_keys, all_values, all_scores = (
        lax.all_gather(keys, "ctx", axis=1, tiled=True),
        lax.all_gather(values, "ctx", axis=1, tiled=True),
        lax.all_gather(scores, "ctx", axis=1, tiled=True),
    )
    head_items = (
        split_heads(queries),
        split_heads(all_keys),
        split_heads(all_values),
        jnp.moveaxis(all_scores, 2, 0),
        kept_rows,
    )
    heads, log_totals = lax.map(
        partial(attend_head, base=base, causal=causal, key_block=key_block), head_items
    )
    mixed = join_heads(heads).astype(jnp.bfloat16)
    after_attn = residual + jnp.dot(mixed, out_w, preferred_element_type=jnp.float32)
    hidden2 = normalize(after_attn, gains[1], biases[1]).astype(jnp.bfloat16)
    up_part = jnp.dot(hidden2, up_w, preferred_element_type=jnp.float32)
    active = gelu_tanh(up_part).astype(jnp.bfloat16)
    result = after_attn + jnp.dot(active, down_w, preferred_element_type=jnp.float32)
    own_side = (queries, keys, values, scores)
    saved = (
        residual,
        hidden,
        head_items,
        log_totals,
        mixed,
        after_attn,
        hidden2,
        up_part,
        active,
        own_side,
    )
    return (result, saved)


def backward_layer(grad, saved, weights, masks, key_masks):
    qkv_w, score_w, out_w, up_w, down_w, gain, bias = weights
    base, causal, key_block, kept_rows = masks
    (
        residual,
        hidden,
        head_items,
        log_totals,
        mixed,
        after_attn,
        hidden2,
        up_part,
        active,
        own_side,
    ) = saved
    gains = gain.astype(jnp.float32)
    biases = bias.astype(jnp.float32)
    grad_down = grad.astype(jnp.bfloat16)
    grad_active = jnp.einsum("sto,io->sti", grad_down, down_w, preferred_element_type=jnp.float32)
    grad_up = jax.vjp(gelu_tanh, up_part)[1](grad_active)[0].astype(jnp.bfloat16)
    grad_hidden2 = jnp.einsum("stf,df->std", grad_up, up_w, preferred_element_type=jnp.float32)
    late_back = jax.vjp(normalize, after_attn, gains[1], biases[1])[1]
    grad_norm_late, gain_late, bias_late = late_back(grad_hidden2)
    grad_after = grad + grad_norm_late
    grad_attn = grad_after.astype(jnp.bfloat16)
    grad_mixed = jnp.einsum(
        "ste,de->std", grad_attn, out_w, preferred_element_type=jnp.float32
    ).astype(jnp.bfloat16)
    grad_items = head_items + (split_heads(grad_mixed), log_totals)
    grad_queries, inner = lax.map(
        partial(query_side_grads, base=base, causal=causal, key_block=key_block), grad_items
    )
    own_queries, own_keys, own_values, own_scores = own_side
    all_queries, all_grad_mixed = (
        lax.all_gather(own_queries, "ctx", axis=1, tiled=True),
        lax.all_gather(grad_mixed, "ctx", axis=1, tiled=True),
    )
    all_totals, all_inner = (
        lax.all_gather(log_totals, "ctx", axis=2, tiled=True),
        lax.all_gather(inner, "ctx", axis=2, tiled=True),
    )
    key_base, key_causal, key_block_own, kept_all_rows = key_masks
    key_items = (
        split_heads(all_queries),
        split_heads(own_keys),
        split_heads(own_values),
        jnp.moveaxis(own_scores, 2, 0),
        kept_all_rows,
        split_heads(all_grad_mixed),
        all_totals,
        all_inner,
    )
    grad_keys, grad_values, grad_scores = lax.map(
        partial(key_side_grads, base=key_base, causal=key_causal, key_block=key_block_own),
        key_items,
    )
    key_part = join_heads(grad_keys)
    value_part = join_heads(grad_values)
    score_part = jnp.moveaxis(grad_scores, 0, 2)
    grad_qkv = jnp.concatenate([join_heads(grad_queries), key_part, value_part], axis=-1).astype(
        jnp.bfloat16
    )
    grad_score_low = score_part.astype(jnp.bfloat16)
    grad_hidden = jnp.einsum("ste,de->std", grad_qkv, qkv_w, preferred_element_type=jnp.float32)
    grad_hidden = grad_hidden + jnp.einsum(
        "sth,dh->std", grad_score_low, score_w, preferred_element_type=jnp.float32
    )
    early_back = jax.vjp(normalize, residual, gains[0], biases[0])[1]
    grad_norm_early, gain_early, bias_early = early_back(grad_hidden)
    grad_residual = grad_after + grad_norm_early
    inputs = (hidden, mixed, hidden2, active, grad_score_low)
    outputs = (grad_qkv, grad_attn, grad_up, grad_down)
    norms = (jnp.stack([gain_early, gain_late]), jnp.stack([bias_early, bias_late]))
    return (grad_residual, inputs, outputs, norms)


def weight_terms(inputs, outputs, norms):
    all_hidden, all_mixed, all_hidden2, all_active, all_score = (
        lax.all_gather(inputs[0], "ctx", axis=1, tiled=True),
        lax.all_gather(inputs[1], "ctx", axis=1, tiled=True),
        lax.all_gather(inputs[2], "ctx", axis=1, tiled=True),
        lax.all_gather(inputs[3], "ctx", axis=1, tiled=True),
        lax.all_gather(inputs[4], "ctx", axis=1, tiled=True),
    )
    col_qkv, col_attn, col_up, col_down = (
        lax.all_to_all(outputs[0], "ctx", split_axis=2, concat_axis=1, tiled=True),
        lax.all_to_all(outputs[1], "ctx", split_axis=2, concat_axis=1, tiled=True),
        lax.all_to_all(outputs[2], "ctx", split_axis=2, concat_axis=1, tiled=True),
        lax.all_to_all(outputs[3], "ctx", split_axis=2, concat_axis=1, tiled=True),
    )
    gain_total, bias_total = lax.psum((norms[0], norms[1]), "ctx")
    qkv_term = jnp.einsum("std,ste->de", all_hidden, col_qkv, preferred_element_type=jnp.float32)
    score_term = jnp.einsum(
        "std,sth->dh", all_hidden, all_score, preferred_element_type=jnp.float32
    )
    out_term = jnp.einsum("std,ste->de", all_mixed, col_attn, preferred_element_type=jnp.float32)
    up_term = jnp.einsum("std,stf->df", all_hidden2, col_up, preferred_element_type=jnp.float32)
    down_term = jnp.einsum("sti,sto->io", all_active, col_down, preferred_element_type=jnp.float32)
    return (qkv_term, score_term, out_term, up_term, down_term, gain_total, bias_total)


def per_device(
    tokens,
    cotangent,
    kept_blocks,
    picture_starts,
    qkv_weight,
    score_weight,
    out_weight,
    up_weight,
    down_weight,
    norm_gain,
    norm_bias,
):
    local_len = tokens.shape[1]
    whole_len = local_len * lax.axis_size("ctx")
    own_start = lax.axis_index("ctx") * local_len
    masks = build_masks(kept_blocks, picture_starts, own_start, local_len, 0, whole_len)
    key_masks = build_masks(kept_blocks, picture_starts, 0, whole_len, own_start, local_len)
    residual = tokens.astype(jnp.float32)
    kept_weights = []
    saved_all = []
    for layer_index in range(LAYERS):
        rows = (
            lax.all_gather(qkv_weight[layer_index], "fsdp", axis=0, tiled=True),
            lax.all_gather(score_weight[layer_index], "fsdp", axis=0, tiled=True),
            lax.all_gather(out_weight[layer_index], "fsdp", axis=0, tiled=True),
            lax.all_gather(up_weight[layer_index], "fsdp", axis=0, tiled=True),
            lax.all_gather(down_weight[layer_index], "fsdp", axis=0, tiled=True),
            lax.all_gather(norm_gain[layer_index], "fsdp", axis=1, tiled=True),
            lax.all_gather(norm_bias[layer_index], "fsdp", axis=1, tiled=True),
        )
        full_qkv, full_out, full_up, full_down = (
            lax.all_gather(rows[0], "ctx", axis=1, tiled=True),
            lax.all_gather(rows[2], "ctx", axis=1, tiled=True),
            lax.all_gather(rows[3], "ctx", axis=1, tiled=True),
            lax.all_gather(rows[4], "ctx", axis=1, tiled=True),
        )
        weights = (full_qkv, rows[1], full_out, full_up, full_down, rows[5], rows[6])
        kept_weights.append(weights)
        residual, saved = forward_layer(residual, weights, masks)
        saved_all.append(saved)
    grad = cotangent.astype(jnp.float32)
    layer_terms = []
    for layer_index in reversed(range(LAYERS)):
        rows = (
            lax.all_gather(qkv_weight[layer_index], "fsdp", axis=0, tiled=True),
            lax.all_gather(score_weight[layer_index], "fsdp", axis=0, tiled=True),
            lax.all_gather(out_weight[layer_index], "fsdp", axis=0, tiled=True),
            lax.all_gather(up_weight[layer_index], "fsdp", axis=0, tiled=True),
            lax.all_gather(down_weight[layer_index], "fsdp", axis=0, tiled=True),
            lax.all_gather(norm_gain[layer_index], "fsdp", axis=1, tiled=True),
            lax.all_gather(norm_bias[layer_index], "fsdp", axis=1, tiled=True),
        )
        full_qkv, full_out, full_up, full_down = (
            lax.all_gather(rows[0], "ctx", axis=1, tiled=True),
            lax.all_gather(rows[2], "ctx", axis=1, tiled=True),
            lax.all_gather(rows[3], "ctx", axis=1, tiled=True),
            lax.all_gather(rows[4], "ctx", axis=1, tiled=True),
        )
        weights = (full_qkv, rows[1], full_out, full_up, full_down, rows[5], rows[6])
        grad, inputs, outputs, norms = backward_layer(
            grad, saved_all[layer_index], weights, masks, key_masks
        )
        terms = weight_terms(inputs, outputs, norms)
        layer_terms.insert(0, terms)
    stacked = [jnp.stack([entry[number] for entry in layer_terms]) for number in range(7)]
    summed = (
        lax.psum_scatter(
            stacked[0].astype(jnp.bfloat16), "fsdp", scatter_dimension=1, tiled=True
        ).astype(jnp.float32),
        lax.psum_scatter(
            stacked[1].astype(jnp.bfloat16), "fsdp", scatter_dimension=1, tiled=True
        ).astype(jnp.float32),
        lax.psum_scatter(
            stacked[2].astype(jnp.bfloat16), "fsdp", scatter_dimension=1, tiled=True
        ).astype(jnp.float32),
        lax.psum_scatter(
            stacked[3].astype(jnp.bfloat16), "fsdp", scatter_dimension=1, tiled=True
        ).astype(jnp.float32),
        lax.psum_scatter(
            stacked[4].astype(jnp.bfloat16), "fsdp", scatter_dimension=1, tiled=True
        ).astype(jnp.float32),
        lax.psum_scatter(
            stacked[5].astype(jnp.bfloat16), "fsdp", scatter_dimension=2, tiled=True
        ).astype(jnp.float32),
        lax.psum_scatter(
            stacked[6].astype(jnp.bfloat16), "fsdp", scatter_dimension=2, tiled=True
        ).astype(jnp.float32),
    )
    return (
        residual,
        grad,
        summed[0],
        summed[1],
        summed[2],
        summed[3],
        summed[4],
        summed[5],
        summed[6],
    )


D = 768
FF = 3072
HALF = 384
TOK = 512
SEQ = 1024
ROWS = 48
DROWS = 192
NEG = -1e30
FULL = 58 << 20
F32 = jnp.float32
BF16 = jnp.bfloat16
VM = pl.BlockSpec(memory_space=pltpu.VMEM)
HB = pl.BlockSpec(memory_space=pltpu.HBM)
SM = pl.BlockSpec(memory_space=pltpu.SMEM)


def nn(a, b):
    return lax.dot_general(a, b, (((1,), (0,)), ((), ())), preferred_element_type=F32)


def nt(a, b):
    return lax.dot_general(a, b, (((1,), (1,)), ((), ())), preferred_element_type=F32)


def tn(a, b):
    return lax.dot_general(a, b, (((0,), (0,)), ((), ())), preferred_element_type=F32)


def sds(shape, dtype):
    return jax.ShapeDtypeStruct(shape, dtype)


COST = dict(layer_grad=20, qkv=7, attend=12, ffn=20, down_back=6, up_back=10, ffn_grad=11)
COST |= dict(attend_back=16, qkv_grad=8, qkv_back=9, cross=4, own=4)


def duration(us):
    flops = int(us * 0.4e9)
    return pl.CostEstimate(flops=flops, bytes_accessed=1 << 20, transcendentals=0)


def kernel_call(body, ins, in_specs, outs, out_specs, scratch, name, limit=None):
    held = [v for v, spec in zip((*ins, *outs), (*in_specs, *out_specs)) if spec is VM]
    held += [b for b in scratch if getattr(b, "memory_space", None) == pltpu.VMEM]
    held = sum(math.prod(v.shape) * jnp.dtype(v.dtype).itemsize for v in held)
    return pl.pallas_call(
        body,
        out_shape=tuple(outs),
        in_specs=in_specs,
        out_specs=tuple(out_specs),
        scratch_shapes=scratch,
        compiler_params=pltpu.CompilerParams(vmem_limit_bytes=FULL),
        cost_estimate=duration(COST[name]),
        name=name,
    )(*ins)


def aligned(v, m):
    return pl.multiple_of(v, m)


def layer_norm_parts(x):
    centered = x - jnp.mean(x, axis=-1, keepdims=True)
    variance = jnp.mean(centered * centered, axis=-1, keepdims=True)
    scale = lax.rsqrt(variance + 1e-05)
    return centered * scale, scale


def split_blocks(src, keep, send, c, rows):
    for b in range(8):
        keep[b] = src[pl.ds(aligned((2 * b + c) * rows, 16), rows), :]
        send[b] = src[pl.ds(aligned((2 * b + 1 - c) * rows, 16), rows), :]


def visit(f, y, arrays, n, fns):
    if len(arrays) == 16:
        for q in range(8):
            device = (f & 3) ^ ((q & 1) * 2 + (q >> 2))
            for part, fn in enumerate(fns):
                fn(arrays[part * 8 + q].at[:, n], device, y ^ ((q >> 1) & 1))
        return
    for pxx in range(2):
        for pc in range(2):
            for y2 in range(2):
                for part, fn in enumerate(fns):
                    device = pxx * 2 + ((f & 1) ^ pc)
                    fn(arrays[pc].at[:, pxx, y2, part, n], device, y2)


QKV_W = pltpu.VMEM((6, 4, 4, ROWS, HALF), BF16)
OUT_W = pltpu.VMEM((2, 4, 4, ROWS, HALF), BF16)
UP_W = pltpu.VMEM((4, 4, 4, ROWS, D), BF16)
DOWN_W = pltpu.VMEM((2, 4, 4, 4, ROWS, HALF), BF16)


def fetch_qkv(f, y, parts, w, sem):
    def put(src, cols, group, device, y2):
        dst = w.at[y2 * 3 + group, :, device]
        pltpu.make_async_copy(src.at[:, :, cols], dst, sem).start()

    def fetch_a(src, device, y2):
        put(src, pl.ds(0, HALF), 0, device, y2)
        put(src, pl.ds(HALF, HALF), 1, device, y2)

    def fetch_b(src, device, y2):
        put(src, pl.ds(0, HALF), 2, device, y2)

    visit(f, y, parts, 0, (fetch_a, fetch_b))


def fetch_out(f, y, parts, wo, sem):
    def fetch(src, device, y2):
        dst = wo.at[y2, :, device]
        pltpu.make_async_copy(src.at[:, :, pl.ds(HALF, HALF)], dst, sem).start()

    visit(f, y, parts, 0, (lambda *_: None, fetch))


def fetch_up(f, y, parts, wu, sem):
    def fetch(part):
        def copy(src, device, y2):
            pltpu.make_async_copy(src, wu.at[y2 * 2 + part, :, device], sem).start()

        return copy

    visit(f, y, parts, 0, (fetch(0), fetch(1)))


def fetch_down(f, y, parts, wd, sem):
    def fetch(part):
        def copy(src, device, y2):
            for k in range(2):
                dst = wd.at[y2, :, device, part * 2 + k]
                pltpu.make_async_copy(src.at[:, :, pl.ds(k * HALF, HALF)], dst, sem).start()

        return copy

    visit(f, y, parts, 1, (fetch(0), fetch(1)))


def arrived(w, sem):
    pltpu.make_async_copy(w, w, sem).wait()


def load(pairs, sem):
    copies = [pltpu.make_async_copy(a, b, sem.at[k]) for k, (a, b) in enumerate(pairs)]
    for copy in copies:
        copy.start()
    return copies


def qkv_kernel(idx, res, gb, sw0, sw1, *refs):
    parts, refs = refs[:-8], refs[-8:]
    keep, send, htk, hts, w, h, ht, sem = refs
    f, y, c = idx[0], idx[1], idx[2]

    fetch_qkv(f, y, parts, w, sem)
    gain, bias = gb[0:1, :], gb[2:3, :]
    for t in range(4):
        rows = pl.ds(t * 128, 128)
        n, _ = layer_norm_parts(res[rows, :])
        v = n * gain + bias
        h[rows, :] = v.astype(BF16)
        ht[:, rows] = v.T.astype(BF16)
    split_blocks(ht, htk, hts, c, ROWS)
    pltpu.make_async_copy(w, w, sem).wait()

    def tile(t, carry):
        rows = pl.ds(aligned(t * 256, 256), 256)
        hv = h[rows, :]
        for j in range(3):
            cols = pl.ds(j * HALF, HALF)
            keep[rows, cols] = nn(hv, w[2 * j + c].reshape(D, HALF)).astype(BF16)
            send[rows, cols] = nn(hv, w[2 * j + 1 - c].reshape(D, HALF)).astype(BF16)
        keep[rows, pl.ds(1152, 128)] = nt(hv, sw0[...]).astype(BF16)
        send[rows, pl.ds(1152, 128)] = nt(hv, sw1[...]).astype(BF16)
        return carry

    lax.fori_loop(0, 2, tile, 0)


def qkv_call(idx, res, gb, sw0, sw1, w):
    return kernel_call(
        qkv_kernel,
        [idx, res, gb, sw0, sw1, *w],
        [SM, VM, VM, VM, VM] + [HB] * len(w),
        [
            sds((TOK, 1280), BF16),
            sds((TOK, 1280), BF16),
            sds((8, ROWS, TOK), BF16),
            sds((8, ROWS, TOK), BF16),
        ],
        [VM, VM, VM, VM],
        [
            QKV_W,
            pltpu.VMEM((TOK, D), BF16),
            pltpu.VMEM((D, TOK), BF16),
            pltpu.SemaphoreType.DMA,
        ],
        "qkv",
        FULL,
    )


def load_halves(pairs, c, pad, sem):
    copies = []
    for number, (own, other, dst) in enumerate(pairs):
        for k, (src, half) in enumerate(((own, c), (other, 1 - c))):
            rows = pl.ds(aligned(pad + half * TOK, 128), TOK)
            copy = pltpu.make_async_copy(src, dst.at[rows, :], sem.at[2 * number + k])
            copy.start()
            copies.append(copy)
    return copies


def mask_tiles(tab):
    key = lax.broadcasted_iota(jnp.int32, (BLK, BLK), 0)
    query = lax.broadcasted_iota(jnp.int32, (BLK, BLK), 1)
    gap = query - key
    tab[0] = jnp.where((gap >= 0) & (gap < WINDOW), 0.0, NEG)
    tab[1] = jnp.where(gap >= 0, 0.0, NEG)
    tab[2] = jnp.zeros((BLK, BLK), F32)
    tab[3] = jnp.where(gap + BLK < WINDOW, 0.0, NEG)
    tab[4] = jnp.full((BLK, BLK), NEG, F32)


def log_sigmoid_of(v):
    return -(jnp.maximum(-v, 0.0) + jnp.log1p(jnp.exp(-jnp.abs(v))))


def picture_flags(pics, i):
    p0, p1 = pics[0] // BLK, pics[1] // BLK
    starts = (p0 == i) | (p1 == i)
    follows = (p0 == i - 1) | (p1 == i - 1)
    return starts, follows


def split_log_sigmoid(s, la):
    value = log_sigmoid_of(s[:, 1152:1280].astype(F32))
    lane = lax.broadcasted_iota(jnp.int32, value.shape, 1)
    value = jnp.where(lane < 6, value, 0.0)
    high = value.astype(BF16).astype(F32)
    middle = (value - high).astype(BF16).astype(F32)
    low = value - high - middle
    la[...] = (high + pltpu.roll(middle, 8, 1) + pltpu.roll(low, 16, 1)).astype(BF16)


def pair_logits(s, la, tab, kept, i, pair, blocks, starts, follows):
    lane = lax.broadcasted_iota(jnp.int32, (BLK, BLK), 1)
    first = lane < 64
    base = aligned(i * BLK, BLK)
    cols = pair * BLK
    q = s[pl.ds(base + BLK, BLK), pl.ds(cols, BLK)] * jnp.asarray(HEAD_DIM**-0.5, BF16)
    zero = jnp.zeros_like(q)
    q = jnp.concatenate([jnp.where(first, q, zero), jnp.where(first, zero, q)], axis=0)
    terms = [((lane & 7) == 2 * pair + odd) & (lane < 24) for odd in range(2)]
    ones = jnp.concatenate([jnp.where(t, 1.0, 0.0) for t in terms], axis=0).astype(BF16)
    near = pl.ds(base, blocks * BLK)
    chosen = [kept[2 * pair + odd, i] for odd in range(2)]
    far = [pl.ds(aligned((b + 1) * BLK, BLK), BLK) for b in chosen]

    def rows_of(cols):
        far_rows = jnp.where(first, s[far[0], cols], s[far[1], cols])
        return jnp.concatenate([s[near, cols], far_rows], axis=0)

    k = rows_of(pl.ds(HALF + cols, BLK))
    v = rows_of(pl.ds(2 * HALF + cols, BLK))
    bias = jnp.where(terms[0], la[far[0], :], la[far[1], :])
    bias = jnp.concatenate([la[near, :], bias], axis=0)
    logits = nt(jnp.concatenate([k, bias], axis=1), jnp.concatenate([q, ones], axis=1))
    before, here, beyond = [], [], []
    for block in chosen:
        before.append(tab[jnp.where(i == 0, 4, jnp.where(follows | (block == i - 1), 2, 3))])
        here.append(tab[jnp.where(starts | follows, 2, jnp.where(block == i, 1, 0))])
        beyond.append(jnp.full((1, BLK), jnp.where(block < i - 1, 0.0, NEG), F32))
    parts = [
        logits[0:BLK] + jnp.concatenate(before, axis=1),
        logits[BLK : 2 * BLK] + jnp.concatenate(here, axis=1),
    ]
    if blocks == 3:
        parts.append(logits[2 * BLK : 3 * BLK])
    parts.append(logits[blocks * BLK :] + jnp.concatenate(beyond, axis=1))
    return jnp.concatenate(parts, axis=0), q, k, v, near, far, first


def block_probs(s, ls, tab, kept, i, h, blocks, starts, follows):
    pair, odd = h // 2, h % 2
    lane = lax.broadcasted_iota(jnp.int32, (BLK, BLK), 1)
    mine = (lane >= 64) if odd else (lane < 64)
    base = aligned(i * BLK, BLK)
    cols = pair * BLK
    q = s[pl.ds(base + BLK, BLK), pl.ds(cols, BLK)] * jnp.asarray(HEAD_DIM**-0.5, BF16)
    q = jnp.where(mine, q, jnp.zeros_like(q))
    near, chosen = pl.ds(base, blocks * BLK), kept[h, i]
    far = pl.ds(aligned((chosen + 1) * BLK, BLK), BLK)
    kcols, vcols = pl.ds(HALF + cols, BLK), pl.ds(2 * HALF + cols, BLK)
    k = jnp.concatenate([s[near, kcols], s[far, kcols]], axis=0)
    v = jnp.concatenate([s[near, vcols], s[far, vcols]], axis=0)
    before = jnp.where(i == 0, 4, jnp.where(follows | (chosen == i - 1), 2, 3))
    here = jnp.where(starts | follows, 2, jnp.where(chosen == i, 1, 0))
    beyond = jnp.where(chosen < i - 1, 0.0, NEG).astype(F32)
    logits = nt(k, q)
    parts = [
        logits[0:BLK] + (tab[before] + ls[pl.ds(base, BLK), h : h + 1]),
        logits[BLK : 2 * BLK] + (tab[here] + ls[pl.ds(base + BLK, BLK), h : h + 1]),
    ]
    if blocks == 3:
        parts.append(logits[2 * BLK : 3 * BLK] + ls[pl.ds(base + 2 * BLK, BLK), h : h + 1])
    parts.append(logits[blocks * BLK :] + (ls[far, h : h + 1] + beyond))
    logits = jnp.concatenate(parts, axis=0)
    largest = jnp.max(logits, axis=0, keepdims=True)
    weights = jnp.exp(logits - largest)
    total = jnp.sum(weights, axis=0, keepdims=True)
    probs = weights * (1.0 / total)
    return probs, v, mine, largest + jnp.log(total)


def attend_kernel(idx, kept, pics, own, other, okeep, osend, lse, s, ls, o, tab, sem):
    c = idx[2]
    copies = load_halves([(own, other, s)], c, BLK, sem)
    s[0:BLK, :] = jnp.zeros((BLK, 1280), BF16)
    mask_tiles(tab)
    for copy in copies:
        copy.wait()
    ls[...] = log_sigmoid_of(s[:, 1152:1280].astype(F32))
    lse[...] = jnp.zeros_like(lse)

    def step(i, carry):
        starts, follows = picture_flags(pics, i)

        def run(blocks):
            rows = pl.ds(aligned(i * BLK, BLK), BLK)
            for pair in range(3):
                halves = []
                for odd in range(2):
                    h = 2 * pair + odd
                    probs, v, mine, logs = block_probs(
                        s, ls, tab, kept, i, h, blocks, starts, follows
                    )
                    halves.append(tn(probs.astype(BF16), v))
                    lse[h : h + 1, rows] = logs
                o[rows, pl.ds(pair * BLK, BLK)] = jnp.where(mine, halves[1], halves[0]).astype(BF16)

        @pl.when(starts)
        def _():
            run(3)

        @pl.when(jnp.logical_not(starts))
        def _():
            run(2)

        return carry

    lax.fori_loop(0, 8, step, 0)
    okeep[...] = o[pl.ds(aligned(c * TOK, TOK), TOK), :]
    osend[...] = o[pl.ds(aligned((1 - c) * TOK, TOK), TOK), :]


def attend_call(idx, kept, pics, own, other):
    return kernel_call(
        attend_kernel,
        [idx, kept, pics, own, other],
        [SM, SM, SM, HB, HB],
        [sds((TOK, HALF), BF16), sds((TOK, HALF), BF16), sds((8, SEQ), F32)],
        [VM, VM, VM],
        [
            pltpu.VMEM((SEQ + BLK, 1280), BF16),
            pltpu.VMEM((SEQ + BLK, BLK), F32),
            pltpu.VMEM((SEQ, HALF), BF16),
            pltpu.VMEM((5, BLK, BLK), F32),
            pltpu.SemaphoreType.DMA((2,)),
        ],
        "attend",
        FULL,
    )


def ffn_kernel(idx, res_in, mk, mr, gb, *refs):
    qo, ffn, refs = refs[:16], refs[16:-23], refs[-23:]
    aa, new, low, mtk, mts, htk, hts, slope_o, atk, ats = refs[:10]
    wo, wu, wd, res, h, ht, act, slope, at, sem, isem, osem, asem = refs[10:]
    f, y, c = idx[0], idx[1], idx[2]
    (res_copy,) = load([(res_in, res)], isem)
    fetch_out(f, y, qo, wo, sem.at[0])
    fetch_up(f, y, ffn, wu, sem.at[1])
    fetch_down(f, y, ffn, wd, sem.at[2])
    ht[pl.ds(aligned(c * HALF, HALF), HALF), :] = mk[...].T
    ht[pl.ds(aligned((1 - c) * HALF, HALF), HALF), :] = mr[...].T
    split_blocks(ht, mtk, mts, c, ROWS)
    arrived(wo, sem.at[0])
    res_copy.wait()
    gain, bias = gb[1:2, :], gb[3:4, :]
    mine, theirs = pl.ds(c * 2, 2), pl.ds((1 - c) * 2, 2)
    for half in range(2):
        cols = pl.ds(half * HALF, HALF)
        part = nn(mk[...], wo[half, mine].reshape(HALF, HALF))
        part += nn(mr[...], wo[half, theirs].reshape(HALF, HALF))
        aa[:, cols] = res[:, cols] + part
    for t in range(4):
        rows = pl.ds(t * 128, 128)
        n, _ = layer_norm_parts(aa[rows, :])
        v = (n * gain + bias).astype(BF16)
        h[rows, :] = v
        ht[:, rows] = v.T
    split_blocks(ht, htk, hts, c, ROWS)
    arrived(wu, sem.at[1])
    outs = []
    for g in range(4):

        def tile(t, carry):
            rows = pl.ds(0, TOK)
            u = nn(h[rows, :], wu[g].reshape(D, D))
            square = u * u
            th = jnp.tanh(u * (0.7978845608 + (0.7978845608 * 0.044715) * square))
            share = 0.5 + 0.5 * th
            a = u * share
            bend = 2 * 0.7978845608 + (6 * 0.7978845608 * 0.044715) * square
            d = share + a * (1.0 - share) * bend
            cols = pl.ds(g * D, D)
            a = a.astype(BF16)
            act[rows, cols] = a
            slope[rows, cols] = d.astype(BF16)
            at[cols, rows] = a.T
            return carry

        tile(0, 0)
        cols = pl.ds(g * D, D)
        outs.append(pltpu.make_async_copy(slope.at[:, cols], slope_o.at[:, cols], osem.at[g]))
        outs[-1].start()
        for b in (2 * g, 2 * g + 1):
            for k, (dst, row) in enumerate(((atk, 2 * b + c), (ats, 2 * b + 1 - c))):
                src = at.at[pl.ds(aligned(row * DROWS, 16), DROWS), :]
                outs.append(pltpu.make_async_copy(src, dst.at[b], asem.at[2 * b + k]))
                outs[-1].start()
    arrived(wd, sem.at[2])

    def tile(t, carry):
        rows = pl.ds(0, TOK)
        for half in range(2):
            cols = pl.ds(half * HALF, HALF)
            total = aa[rows, cols] + nn(act[rows, :], wd[half].reshape(FF, HALF))
            new[rows, cols] = total
            low[rows, cols] = total.astype(BF16)
        return carry

    tile(0, 0)
    for copy in outs:
        copy.wait()


def ffn_call(idx, res, mk, mr, gb, qo, ffn):
    return kernel_call(
        ffn_kernel,
        [idx, res, mk, mr, gb, *qo, *ffn],
        [SM, HB, VM, VM, VM] + [HB] * (len(qo) + len(ffn)),
        [
            sds((TOK, D), F32),
            sds((TOK, D), F32),
            sds((TOK, D), BF16),
            sds((8, ROWS, TOK), BF16),
            sds((8, ROWS, TOK), BF16),
            sds((8, ROWS, TOK), BF16),
            sds((8, ROWS, TOK), BF16),
            sds((TOK, FF), BF16),
            sds((8, DROWS, TOK), BF16),
            sds((8, DROWS, TOK), BF16),
        ],
        [VM] * 7 + [HB] * 3,
        [
            OUT_W,
            UP_W,
            DOWN_W,
            pltpu.VMEM((TOK, D), F32),
            pltpu.VMEM((TOK, D), BF16),
            pltpu.VMEM((D, TOK), BF16),
            pltpu.VMEM((TOK, FF), BF16),
            pltpu.VMEM((TOK, FF), BF16),
            pltpu.VMEM((FF, TOK), BF16),
            pltpu.SemaphoreType.DMA((3,)),
            pltpu.SemaphoreType.DMA((1,)),
            pltpu.SemaphoreType.DMA((4,)),
            pltpu.SemaphoreType.DMA((16,)),
        ],
        "ffn",
        FULL,
    )


def down_back_kernel(idx, grad, slope_in, *refs):
    parts, refs = refs[:-5], refs[-5:]
    gu, wd, slope, sem, isem = refs
    copies = load([(slope_in.at[:, pl.ds(g * D, D)], slope.at[g]) for g in range(4)], isem)
    fetch_down(idx[0], idx[1], parts, wd, sem)
    arrived(wd, sem)
    for g in range(4):
        copies[g].wait()
        left = wd[0, g].reshape(D, HALF)
        right = wd[1, g].reshape(D, HALF)

        def tile(t, carry):
            rows = pl.ds(aligned(t * 256, 256), 256)
            part = nt(grad[rows, 0:HALF], left) + nt(grad[rows, HALF:D], right)
            gu[rows, pl.ds(g * D, D)] = (part * slope[g, rows, :].astype(F32)).astype(BF16)
            return carry

        lax.fori_loop(0, 2, tile, 0)


def down_back_call(idx, grad, slope, w):
    return kernel_call(
        down_back_kernel,
        [idx, grad, slope, *w],
        [SM, VM, HB] + [HB] * len(w),
        [sds((TOK, FF), BF16)],
        [VM],
        [
            DOWN_W,
            pltpu.VMEM((4, TOK, D), BF16),
            pltpu.SemaphoreType.DMA,
            pltpu.SemaphoreType.DMA((4,)),
        ],
        "down_back",
    )[0]


def norm_back(x, grad_out, gain):
    n, scale = layer_norm_parts(x)
    e = grad_out * gain
    back = scale * (
        e - jnp.mean(e, axis=-1, keepdims=True) - n * jnp.mean(e * n, axis=-1, keepdims=True)
    )
    gain_part = jnp.sum(grad_out * n, axis=0, keepdims=True)
    bias_part = jnp.sum(grad_out, axis=0, keepdims=True)
    return back, gain_part, bias_part


def up_back_kernel(idx, grad_in, gu, aa_in, gb, *refs):
    qo, ffn, refs = refs[:16], refs[16:-12], refs[-12:]
    ga, gat, gmk, gms, nrm, wu, wo, grad, aa, gh, sem, isem = refs
    f, y, c = idx[0], idx[1], idx[2]
    fetch_up(f, y, ffn, wu, sem.at[0])
    copies = load([(aa_in, aa), (grad_in, grad)], isem)
    fetch_out(f, y, qo, wo, sem.at[1])
    nrm[...] = jnp.zeros_like(nrm)
    gain = gb[1:2, :]
    mine, theirs = pl.ds(c * 2, 2), pl.ds((1 - c) * 2, 2)
    arrived(wu, sem.at[0])

    def wide(t, carry):
        rows = pl.ds(aligned(t * 256, 256), 256)
        total = nt(gu[rows, 0:D], wu[0].reshape(D, D))
        for g in range(1, 4):
            total += nt(gu[rows, pl.ds(g * D, D)], wu[g].reshape(D, D))
        gh[rows, :] = total
        return carry

    lax.fori_loop(0, 2, wide, 0)
    for copy in copies:
        copy.wait()

    def tile(t, carry):
        rows = pl.ds(aligned(t * 128, 128), 128)
        back, gain_part, bias_part = norm_back(aa[rows, :], gh[rows, :], gain)
        total = grad[rows, :] + back
        ga[rows, :] = total
        gat[rows, :] = total.astype(BF16)
        nrm[0:1, :] += gain_part
        nrm[1:2, :] += bias_part
        return carry

    lax.fori_loop(0, 4, tile, 0)
    arrived(wo, sem.at[1])
    for dst, part in ((gmk, mine), (gms, theirs)):
        dst[...] = (
            nt(gat[:, 0:HALF], wo[0, part].reshape(HALF, HALF))
            + nt(gat[:, HALF:D], wo[1, part].reshape(HALF, HALF))
        ).astype(BF16)


def up_back_call(idx, grad, gu, aa, gb, qo, ffn):
    return kernel_call(
        up_back_kernel,
        [idx, grad, gu, aa, gb, *qo, *ffn],
        [SM, HB, VM, HB, VM] + [HB] * (len(qo) + len(ffn)),
        [
            sds((TOK, D), F32),
            sds((TOK, D), BF16),
            sds((TOK, HALF), BF16),
            sds((TOK, HALF), BF16),
            sds((8, D), F32),
        ],
        [VM] * 5,
        [
            UP_W,
            OUT_W,
            pltpu.VMEM((TOK, D), F32),
            pltpu.VMEM((TOK, D), F32),
            pltpu.VMEM((TOK, D), F32),
            pltpu.SemaphoreType.DMA((2,)),
            pltpu.SemaphoreType.DMA((2,)),
        ],
        "up_back",
    )


def attend_back_kernel(
    idx, kept, pics, lse, own, other, gown, gother, down_, doth, s, g, la, d, dk, dv, ds, tab, sem
):
    c = idx[2]
    copies = load_halves([(own, other, s)], c, BLK, sem)
    copies += load_halves([(gown, gother, g)], c, 0, sem.at[pl.ds(2, 2)])
    s[0:BLK, :] = jnp.zeros((BLK, 1280), BF16)
    mask_tiles(tab)
    dk[...] = jnp.zeros_like(dk)
    dv[...] = jnp.zeros_like(dv)
    ds[...] = jnp.zeros_like(ds)
    for copy in copies:
        copy.wait()
    split_log_sigmoid(s, la)
    lane = lax.broadcasted_iota(jnp.int32, (BLK, BLK), 1)

    def step(i, carry):
        starts, follows = picture_flags(pics, i)

        def run(blocks):
            rows = pl.ds(aligned(i * BLK, BLK), BLK)
            cut = blocks * BLK
            for pair in range(3):
                cols = pl.ds(pair * BLK, BLK)
                logits, q, k, v, near, far, first = pair_logits(
                    s, la, tab, kept, i, pair, blocks, starts, follows
                )
                logs = [lse[2 * pair + odd : 2 * pair + odd + 1, rows] for odd in range(2)]
                probs = jnp.exp(logits - jnp.concatenate(logs, axis=1))
                gm = g[rows, cols]
                zero = jnp.zeros_like(gm)
                gm = jnp.concatenate([jnp.where(first, gm, zero), jnp.where(first, zero, gm)], axis=0)
                gprob = nt(v, gm)
                inner = jnp.sum(probs * gprob, axis=0, keepdims=True)
                gl = (probs * (gprob - inner)).astype(BF16)
                gv = nn(probs.astype(BF16), gm)
                heads = [jnp.where(lane == 2 * pair + odd, 1.0, 0.0) for odd in range(2)]
                heads = jnp.concatenate(heads, axis=0).astype(BF16)
                gk = nn(gl, jnp.concatenate([q, heads], axis=1))
                dv[near, cols] += gv[:cut]
                dk[near, cols] += gk[:cut, :BLK]
                ds[near, :] += gk[:cut, BLK:]
                for odd in range(2):
                    mine = jnp.logical_not(first) if odd else first
                    dv[far[odd], cols] += jnp.where(mine, gv[cut:], 0.0)
                    dk[far[odd], cols] += jnp.where(mine, gk[cut:, :BLK], 0.0)
                    ds[far[odd], :] += jnp.where(lane == 2 * pair + odd, gk[cut:, BLK:], 0.0)
                dq = tn(gl, k)
                dq = jnp.where(first, dq[:BLK], dq[BLK:]) * (HEAD_DIM**-0.5)
                d[rows, cols] = dq.astype(BF16)

        @pl.when(starts)
        def _():
            run(3)

        @pl.when(jnp.logical_not(starts))
        def _():
            run(2)

        return carry

    lax.fori_loop(0, 8, step, 0)
    keys = pl.ds(BLK, SEQ)
    d[:, HALF : 2 * HALF] = dk[keys, :].astype(BF16)
    d[:, 2 * HALF : 3 * HALF] = dv[keys, :].astype(BF16)
    back = ds[keys, :] * jax.nn.sigmoid(-s[keys, 1152:1280].astype(F32))
    d[:, 1152:1280] = back.astype(BF16)
    down_[...] = d[pl.ds(aligned(c * TOK, TOK), TOK), :]
    doth[...] = d[pl.ds(aligned((1 - c) * TOK, TOK), TOK), :]


def attend_back_call(idx, kept, pics, lse, own, other, gown, gother):
    return kernel_call(
        attend_back_kernel,
        [idx, kept, pics, lse, own, other, gown, gother],
        [SM, SM, SM, VM, HB, HB, HB, HB],
        [sds((TOK, 1280), BF16), sds((TOK, 1280), BF16)],
        [VM, VM],
        [
            pltpu.VMEM((SEQ + BLK, 1280), BF16),
            pltpu.VMEM((SEQ, HALF), BF16),
            pltpu.VMEM((SEQ + BLK, BLK), BF16),
            pltpu.VMEM((SEQ, 1280), BF16),
            pltpu.VMEM((SEQ + BLK, HALF), F32),
            pltpu.VMEM((SEQ + BLK, HALF), F32),
            pltpu.VMEM((SEQ + BLK, BLK), F32),
            pltpu.VMEM((5, BLK, BLK), F32),
            pltpu.SemaphoreType.DMA((4,)),
        ],
        "attend_back",
    )


def qkv_back_kernel(idx, ga_in, down_, dr, res_in, gb, sw0, sw1, *refs):
    parts, refs = refs[:-9], refs[-9:]
    gout, glow, nrm, w, ga, res, gh, sem, isem = refs
    c = idx[2]
    fetch_qkv(idx[0], idx[1], parts, w, sem)
    copies = load([(res_in, res), (ga_in, ga)], isem)
    nrm[...] = jnp.zeros_like(nrm)
    gain = gb[0:1, :]
    arrived(w, sem)

    def wide(t, carry):
        rows = pl.ds(aligned(t * 256, 256), 256)
        total = nn(down_[rows, 1152:1280], sw0[...]) + nn(dr[rows, 1152:1280], sw1[...])
        for j in range(3):
            cols = pl.ds(j * HALF, HALF)
            total += nt(down_[rows, cols], w[2 * j + c].reshape(D, HALF))
            total += nt(dr[rows, cols], w[2 * j + 1 - c].reshape(D, HALF))
        gh[rows, :] = total
        return carry

    lax.fori_loop(0, 2, wide, 0)
    for copy in copies:
        copy.wait()

    def tile(t, carry):
        rows = pl.ds(aligned(t * 128, 128), 128)
        back, gain_part, bias_part = norm_back(res[rows, :], gh[rows, :], gain)
        total = ga[rows, :] + back
        gout[rows, :] = total
        glow[rows, :] = total.astype(BF16)
        nrm[0:1, :] += gain_part
        nrm[1:2, :] += bias_part
        return carry

    lax.fori_loop(0, 4, tile, 0)


def qkv_back_call(idx, ga, down_, dr, res, gb, sw0, sw1, w):
    return kernel_call(
        qkv_back_kernel,
        [idx, ga, down_, dr, res, gb, sw0, sw1, *w],
        [SM, HB, VM, VM, HB, VM, VM, VM] + [HB] * len(w),
        [sds((TOK, D), F32), sds((TOK, D), BF16), sds((8, D), F32)],
        [VM, VM, VM],
        [
            QKV_W,
            pltpu.VMEM((TOK, D), F32),
            pltpu.VMEM((TOK, D), F32),
            pltpu.VMEM((TOK, D), F32),
            pltpu.SemaphoreType.DMA,
            pltpu.SemaphoreType.DMA((2,)),
        ],
        "qkv_back",
    )


def scatter_rows(src, f, rows, offset, pyy, portion, outs, n, cols):
    if len(outs) == 1:
        for block in range(8):
            value = src[pl.ds(block * rows + offset, ROWS), :]
            outs[0][2 * block + pyy, portion, n, :, cols] = value
        return
    ka, sa, kb, sb = outs
    for pxx in range(2):
        for pz in range(4):
            block = (f >> 1) ^ (pz * 2 + pxx)
            value = src[pl.ds(aligned(block * rows + offset, 16), ROWS), :]
            if portion == 0:
                (sa if pxx else ka)[pyy, pz, n, :, cols] = value
            else:
                (sb if pyy else kb)[pxx, pz, n, :, cols] = value


def up_grads_into(f, y, xk, xr, gk, gr, outs, tmp, n):
    for portion in range(2):
        for pyy in range(2):
            cols = pl.ds(aligned((y ^ pyy) * 1536 + portion * D, 128), D)
            slot = portion * 2 + pyy
            tmp[slot] = (nn(xk[...], gk[:, cols]) + nn(xr[...], gr[:, cols])).astype(BF16)
            scatter_rows(tmp.at[slot], f, ROWS, 0, pyy, portion, outs, n, pl.ds(0, D))


def down_grads_into(f, y, ak, ar, dk, dr, outs, tmp, n):
    for pyy in range(2):
        cols = pl.ds(aligned((y ^ pyy) * HALF, 128), HALF)

        def tile(t, carry):
            rows = pl.ds(aligned(t * HALF, HALF), HALF)
            value = nn(ak[rows, :], dk[:, cols]) + nn(ar[rows, :], dr[:, cols])
            tmp[pyy, rows, :] = value.astype(BF16)
            return carry

        lax.fori_loop(0, 4, tile, 0)
        for portion in range(2):
            for k in range(2):
                offset, half = (portion * 2 + k) * ROWS, pl.ds(k * HALF, HALF)
                scatter_rows(tmp.at[pyy], f, DROWS, offset, pyy, portion, outs, n, half)


def qkv_grads_into(y, xk, xr, mk, mr, dy, gk, gr, outs, tmp, f):
    for pyy in range(2):
        y2 = y ^ pyy
        for part in range(4):
            portion, side = part // 2, part % 2
            if part < 3:
                g = y2 * 3 + part
                value = nn(xk[...], dy[0, g]) + nn(xr[...], dy[1, g])
            else:
                oc = pl.ds(aligned(y2 * HALF, 128), HALF)
                value = nn(mk[...], gk[:, oc]) + nn(mr[...], gr[:, oc])
            tmp[portion * 2 + pyy, :, pl.ds(side * HALF, HALF)] = value.astype(BF16)
        for portion in range(2):
            slot = portion * 2 + pyy
            scatter_rows(tmp.at[slot], f, ROWS, 0, pyy, portion, outs, 0, pl.ds(0, D))


def score_grads_into(f, c, xk, xr, tsc, sc):
    own = nn(xk[...], tsc[0]) + nn(xr[...], tsc[2])
    theirs = nn(xk[...], tsc[1]) + nn(xr[...], tsc[3])
    first = jnp.where(c == 0, own, theirs)
    second = jnp.where(c == 0, theirs, own)
    both = first + pltpu.roll(second, 64, 1)
    for pxx in range(2):
        for pz in range(4):
            target = (f >> 1) ^ (pz * 2 + pxx)
            for b in range(8):

                @pl.when(target == b)
                def _():
                    sc[pxx, pz] = both[b * ROWS : (b + 1) * ROWS, :]


def start_outputs_grads(c, grads, dy, tsc, sem):
    copies = []
    for tok in range(2):
        for k in range(2):
            src = grads[tok * 2 + k]
            for j in range(3):
                part = src.at[:, pl.ds(j * HALF, HALF)]
                at = sem.at[tok * 8 + k * 4 + j]
                copies.append(pltpu.make_async_copy(part, dy.at[tok, 2 * j + (c ^ k)], at))
            part = src.at[:, pl.ds(1152, 128)]
            at = sem.at[tok * 8 + k * 4 + 3]
            copies.append(pltpu.make_async_copy(part, tsc.at[tok * 2 + k], at))
    for copy in copies:
        copy.start()
    return copies


def wait_all(copies):
    for copy in copies:
        copy.wait()


FFN_SHAPES = [(4 * HALF, TOK)] * 2 + [(TOK, D)] * 2 + [(HALF, TOK)] * 2 + [(TOK, FF)] * 2
QKV_SHAPES = [(HALF, TOK)] * 4 + [(TOK, D)] * 2
DY_SCRATCH = [pltpu.VMEM((2, 6, TOK, HALF), BF16), pltpu.VMEM((4, TOK, 128), BF16)]


def ffn_grad_kernel(idx, *refs):
    ins, outs, refs = refs[:8], refs[8:12], refs[12:]
    held, (tmp, tmp2, sem) = refs[:8], refs[8:]
    copies = load(list(zip(ins, held)), sem)
    ak, ar, dk, dr, xk, xr, gk, gr = held
    wait_all(copies[:4])
    down_grads_into(idx[0], idx[1], ak, ar, dk, dr, outs, tmp2, 1)
    wait_all(copies[4:])
    up_grads_into(idx[0], idx[1], xk, xr, gk, gr, outs, tmp, 0)


def ffn_grad_call(idx, xk, xr, gk, gr, ak, ar, dk, dr):
    ins = [v.reshape(4 * HALF, TOK) for v in (ak, ar)] + [dk, dr]
    ins += [v.reshape(HALF, TOK) for v in (xk, xr)] + [gk, gr]
    return kernel_call(
        ffn_grad_kernel,
        [idx, *ins],
        [SM] + [HB] * 8,
        [sds((2, 4, 2, ROWS, D), BF16)] * 4,
        [VM] * 4,
        [pltpu.VMEM(shape, BF16) for shape in FFN_SHAPES]
        + [pltpu.VMEM((4, HALF, D), BF16), pltpu.VMEM((2, 4 * HALF, HALF), BF16)]
        + [pltpu.SemaphoreType.DMA((8,))],
        "ffn_grad",
    )


def qkv_grad_kernel(idx, *refs):
    ins, grads, outs, sc, refs = refs[:6], refs[6:10], refs[10:14], refs[14], refs[15:]
    held, (dy, tsc, tmp, sem, isem) = refs[:6], refs[6:]
    f, y, c = idx[0], idx[1], idx[2]
    copies = start_outputs_grads(c, grads, dy, tsc, sem) + load(list(zip(ins, held)), isem)
    xk, xr, mk, mr, gk, gr = held
    wait_all(copies)
    qkv_grads_into(y, xk, xr, mk, mr, dy, gk, gr, outs, tmp, f)
    score_grads_into(f, c, xk, xr, tsc, sc)


def qkv_grad_call(idx, xk, xr, mk, mr, d00, d01, d10, d11, gk, gr):
    ins = [v.reshape(HALF, TOK) for v in (xk, xr, mk, mr)] + [gk, gr, d00, d01, d10, d11]
    return kernel_call(
        qkv_grad_kernel,
        [idx, *ins],
        [SM] + [HB] * 10,
        [sds((2, 4, 1, ROWS, D), BF16)] * 4 + [sds((2, 4, ROWS, 128), F32)],
        [VM] * 5,
        [pltpu.VMEM(shape, BF16) for shape in QKV_SHAPES]
        + DY_SCRATCH
        + [pltpu.VMEM((4, HALF, D), BF16)]
        + [pltpu.SemaphoreType.DMA((16,)), pltpu.SemaphoreType.DMA((6,))],
        "qkv_grad",
    )


def layer_grad_kernel(idx, *refs):
    ins, grads, out, sc, refs = refs[:14], refs[14:18], refs[18], refs[19], refs[20:]
    held, (dy, tsc, tmp, tmp2, sem, isem) = refs[:14], refs[14:]
    f, c = idx[0], idx[2]
    copies = load(list(zip(ins, held)), isem)
    more = start_outputs_grads(c, grads, dy, tsc, sem)
    ak, ar, dk, dr, xk, xr, gk, gr = held[:8]
    wait_all(copies[:4])
    down_grads_into(0, 0, ak, ar, dk, dr, [out], tmp2, 2)
    wait_all(copies[4:8])
    up_grads_into(0, 0, xk, xr, gk, gr, [out], tmp, 1)
    wait_all(copies[8:] + more)
    xk, xr, mk, mr, gk, gr = held[8:]
    qkv_grads_into(0, xk, xr, mk, mr, dy, gk, gr, [out], tmp, 0)
    score_grads_into(f, c, xk, xr, tsc, sc)


def layer_grad_call(idx, ffn, qkv):
    xk, xr, gk, gr, ak, ar, dk, dr = ffn
    ins = [v.reshape(4 * HALF, TOK) for v in (ak, ar)] + [dk, dr]
    ins += [v.reshape(HALF, TOK) for v in (xk, xr)] + [gk, gr]
    xk, xr, mk, mr, d00, d01, d10, d11, gk, gr = qkv
    ins += [v.reshape(HALF, TOK) for v in (xk, xr, mk, mr)] + [gk, gr, d00, d01, d10, d11]
    return kernel_call(
        layer_grad_kernel,
        [idx, *ins],
        [SM] + [HB] * 18,
        [sds((16, 2, 3, ROWS, D), BF16), sds((2, 4, ROWS, 128), F32)],
        [VM] * 2,
        [pltpu.VMEM(shape, BF16) for shape in FFN_SHAPES + QKV_SHAPES]
        + DY_SCRATCH
        + [pltpu.VMEM((4, HALF, D), BF16), pltpu.VMEM((2, 4 * HALF, HALF), BF16)]
        + [pltpu.SemaphoreType.DMA((16,)), pltpu.SemaphoreType.DMA((14,))],
        "layer_grad",
    )


def cross_kernel(ka, ra, kb, rb, qa, qb):
    for k, r, q in ((ka, ra, qa), (kb, rb, qb)):
        q[...] = (k[...].astype(F32) + r[...].astype(F32)).astype(BF16)[0]


def cross_call(ka, ra, kb, rb):
    n = ka.shape[2]
    block = pl.BlockSpec((1, 1, n, ROWS, D), lambda z: (1, z, 0, 0, 0))
    out = pl.BlockSpec((1, n, ROWS, D), lambda z: (z, 0, 0, 0))
    return pl.pallas_call(
        cross_kernel,
        out_shape=(sds((4, n, ROWS, D), BF16),) * 2,
        grid=(4,),
        in_specs=[block] * 4,
        out_specs=(out,) * 2,
        cost_estimate=duration(COST["cross"]),
        name="cross",
    )(ka, ra, kb, rb)


def own_kernel(ka, ra, ca, kb, rb, cb, *outs):
    z = pl.program_id(0)
    for part, (k, r, q) in enumerate(((ka, ra, ca), (kb, rb, cb))):
        total = k[0, 0].astype(F32) + r[0, 0].astype(F32) + q[0].astype(F32)
        for t in range(4):

            @pl.when(z == t)
            def _():
                outs[t][part] = total.astype(outs[t].dtype)


def own_call(ka, ra, ca, kb, rb, cb):
    n = ka.shape[2]
    block = pl.BlockSpec((1, 1, n, ROWS, D), lambda z: (0, z, 0, 0, 0))
    quarter = pl.BlockSpec((1, n, ROWS, D), lambda z: (z, 0, 0, 0))
    out = pl.BlockSpec((2, n, ROWS, D), lambda z: (0, 0, 0, 0))
    return pl.pallas_call(
        own_kernel,
        out_shape=tuple(sds((2, n, ROWS, D), F32 if t == 0 else BF16) for t in range(4)),
        grid=(4,),
        in_specs=[block, block, quarter] * 2,
        out_specs=(out,) * 4,
        cost_estimate=duration(COST["own"]),
        name="own",
    )(ka, ra, ca, kb, rb, cb)


def pairwise(v, bits):
    return lax.ppermute(v, "zx", [(i, i ^ bits) for i in range(8)])


def over_ctx(v):
    return lax.ppermute(v, "ctx", [(0, 1), (1, 0)])


def over_core(v):
    return lax.ppermute(v, "core", [(0, 1), (1, 0)])


def over_x(v):
    return pairwise(v, 1)


def diagonal(v):
    return lax.ppermute(v, ("zx", "ctx"), [(i, i ^ 3) for i in range(16)])


def turn(v):
    return lax.ppermute(v, ("core", "ctx"), [(0, 0), (1, 2), (2, 1), (3, 3)])


class Chain:
    def __init__(self, stages):
        self.stages, self.result = stages, None
        self.flying = next(stages)

    def advance(self, arrived):
        try:
            self.flying = self.stages.send(arrived)
        except StopIteration as stop:
            self.flying, self.result = None, stop.value


class Order:
    def __init__(self, idx):
        self.gate = idx

    def after(self, value):
        return lax.optimization_barrier((value, self.gate))[0]

    def passed(self, value):
        self.gate, value = lax.optimization_barrier((self.gate, value))
        return value

    def meet(self, *chains):
        for chain, items in zip(chains, self.passed([c.flying for c in chains])):
            chain.advance(items)


def gather_stages(both, z):
    near = yield [pairwise(both, k << 1) for k in range(1, 4)]
    near = [both] + near
    near = [lax.select_n(z, *(near[k ^ t] for t in range(4))) for k in range(4)]
    a, b = (jnp.stack([v[part] for v in near]) for part in range(2))
    xa, yb, ya, xb = yield [over_x(a), over_ctx(b), over_ctx(a), over_x(b)]
    a, b = [a, xa, ya], [b, xb, yb]
    da, db, *other = yield [over_ctx(xa), over_x(yb)] + [over_core(v) for v in a + b]
    ca, cb = yield [over_core(da), over_core(db)]
    return a + [da] + other[:3] + [ca] + b + [db] + other[3:] + [cb]


def small_gather_stages(small, start):
    *near, start = yield [pairwise(small, k << 1) for k in range(1, 4)] + [start]
    small = jnp.stack([small] + near)
    (r,) = yield [over_x(small)]
    small = jnp.concatenate([small, r])
    (r,) = yield [over_core(small)]
    return jnp.concatenate([small, r]), start


def reduce_stages(ka, sa, kb, sb):
    ra, rb = yield [over_x(sa), over_ctx(sb)]
    qa, qb = cross_call(ka, ra, kb, rb)
    ca, cb = yield [over_ctx(qa), over_x(qb)]
    total, *low = own_call(ka, ra, ca, kb, rb, cb)
    rest = yield [pairwise(v, k << 1) for k, v in enumerate(low, 1)]
    return total + sum(v.astype(F32) for v in rest)


def small_stages(t):
    ry, rx, rd = yield [over_ctx(t[0]), over_x(t[1]), diagonal(t[1])]
    t = t[0] + ry + (rx + rd)
    rest = yield [pairwise(t[k], k << 1) for k in range(1, 4)]
    return t[0] + sum(rest)


def pair_device(
    tokens,
    cotangent,
    kept_blocks,
    picture_starts,
    qkv_weight,
    score_weight,
    out_weight,
    up_weight,
    down_weight,
    norm_gain,
    norm_bias,
):
    zx = lax.axis_index("zx").astype(jnp.int32)
    y = lax.axis_index("ctx").astype(jnp.int32)
    c = lax.axis_index("core").astype(jnp.int32)
    f = zx * 2 + c
    idx = jnp.stack([f, y, c])
    order = Order(idx)

    def shards(l):
        joined = jnp.concatenate([qkv_weight[l], out_weight[l]], axis=1)
        up = up_weight[l].reshape(ROWS, 2, D).swapaxes(0, 1)
        down = down_weight[l].reshape(2, 2, ROWS, HALF).swapaxes(1, 2).reshape(2, ROWS, D)
        return jnp.stack([joined[:, :D], joined[:, D:]]), up, down

    def gather(v):
        return Chain(gather_stages(order.after(v), zx >> 1))

    w = [shards(l) for l in range(LAYERS)]
    qo0 = gather(w[0][0][:, None])
    kept = jnp.where(c == y, kept_blocks[0], over_core(kept_blocks[0]))
    pics = jnp.where(c == y, picture_starts[0], over_core(picture_starts[0]))
    kept = lax.dynamic_slice_in_dim(kept, c * 6, 6, 0)
    small = jnp.concatenate(
        [jnp.swapaxes(score_weight, 1, 2), norm_gain, norm_bias], axis=1
    ).reshape(LAYERS * 16, ROWS)
    small = jnp.pad(small, ((0, 0), (0, 128 - ROWS)))
    small = Chain(small_gather_stages(small, turn(tokens[0])))
    ffn0 = lax.all_gather(jnp.stack(w[0][1:], axis=1), ("zx", "ctx"), axis=0, tiled=False)
    order.meet(qo0, small)
    order.meet(qo0, small)
    order.meet(qo0, small)
    order.meet(qo0)
    qo0 = qo0.result
    small, residual = small.result
    residual = residual.astype(F32)
    away = jnp.arange(16, dtype=jnp.int32) ^ f
    small = jnp.take(small, (away & 1) * 8 + ((away >> 1) & 1) * 4 + (away >> 2), axis=0)
    small = jnp.moveaxis(small[:, :, :ROWS], 0, 1).reshape(LAYERS, 16, D)
    scale = []
    for l in range(LAYERS):
        gb = jnp.pad(small[l, 12:16].astype(F32), ((0, 4), (0, 0)))
        own_rows = lax.dynamic_slice_in_dim(small[l], c * 6, 6, 0)
        other_rows = lax.dynamic_slice_in_dim(small[l], (1 - c) * 6, 6, 0)
        pad = ((0, 122), (0, 0))
        scale.append((gb, jnp.pad(own_rows, pad), jnp.pad(other_rows, pad)))

    def qkv(l, residual, w):
        own, send, xk, xs = order.passed(qkv_call(order.gate, residual, *scale[l], w))
        return own, over_core(send), xk, over_core(xs)

    def attend(head):
        mixed, send, lse = order.passed(attend_call(order.gate, kept, pics, head[0], head[1]))
        return (mixed, over_core(send)), lse

    def feed(l, residual, mixed, qo, ffn):
        outs = ffn_call(order.gate, residual, *mixed, scale[l][0], qo, ffn)
        after, new, low, mk, ms, hk, hs, slope, ak, as_ = order.passed(outs)
        hr, ar, mr = over_core(hs), over_core(as_), over_core(ms)
        return new, low, (after, slope, (hk, hr), (ak, ar), (mk, mr))

    qo1 = gather(w[1][0][:, None])
    head0 = qkv(0, residual, qo0)
    order.meet(qo1)
    ffn1 = gather(jnp.stack(w[1][1:], axis=1))
    mixed, lse0 = attend(head0)
    order.meet(qo1, ffn1)
    order.meet(qo1)
    ffn0 = order.passed(ffn0)
    ffn0 = order.passed([v.reshape(4, 2, 2, 2, 2, ROWS, D) for v in (ffn0, over_core(ffn0))])
    res1, _, out0 = feed(0, residual, mixed, qo0, ffn0)
    order.meet(qo1, ffn1)
    qo1 = qo1.result
    head1 = qkv(1, res1, qo1)
    order.meet(ffn1)
    mixed, lse1 = attend(head1)
    order.meet(ffn1)
    ffn1 = ffn1.result
    cot = turn(order.after(cotangent[0]))
    _, low, out1 = feed(1, res1, mixed, qo1, ffn1)
    block_output = turn(low).astype(F32)

    weights = ((qo0, ffn0), (qo1, ffn1))

    def down_back(l, low, out):
        gu = order.passed(down_back_call(order.gate, low, out[1], weights[l][1]))
        return gu, over_core(gu)

    def up_back(l, grad, gu, out):
        ga, gat, gmk, gms, nrm = order.passed(
            up_back_call(order.gate, grad, gu, out[0], scale[l][0], *weights[l])
        )
        return ga, nrm, (gmk, over_core(gms)), (gat, over_core(gat))

    def attend_back(head, lse, gm):
        d_own, d_oth = order.passed(
            attend_back_call(order.gate, kept, pics, lse, head[0], head[1], *gm)
        )
        return d_own, over_core(d_oth), d_oth, over_core(d_own)

    def qkv_grads(head, out, d, gat):
        return order.passed(qkv_grad_call(order.gate, head[2], head[3], *out[4], *d, *gat))

    def qkv_back(l, ga, d, res, head):
        return order.passed(qkv_back_call(order.gate, ga, d[0], d[1], res, *scale[l], weights[l][0]))

    scores, norms = [None] * LAYERS, [None] * LAYERS
    low, low_r = cot, over_core(cot)
    gu, gu_r = down_back(1, low, out1)
    ga, nrm2, gm, gat = up_back(1, cot.astype(F32), gu, out1)
    d = attend_back(head1, lse1, gm)
    grad, new_low, nrm1 = qkv_back(1, ga, d, res1, head1)
    ffn = (*out1[2], gu, gu_r, *out1[3], low, low_r)
    qkv_parts = (head1[2], head1[3], *out1[4], *d, *gat)
    grads1, scores[1] = order.passed(layer_grad_call(order.gate, ffn, qkv_parts))
    grads1 = lax.psum_scatter(grads1, ("zx", "ctx"), scatter_dimension=0, tiled=False)
    low, low_r = new_low, over_core(new_low)
    norms[1] = jnp.concatenate([nrm1[0:1], nrm2[0:1], nrm1[1:2], nrm2[1:2]])
    gu, gu_r = down_back(0, low, out0)
    gu_r = order.passed(gu_r)
    grads = ffn_grad_call(order.gate, *out0[2], gu, gu_r, *out0[3], low, low_r)
    ffn0 = Chain(reduce_stages(*order.passed(grads)))
    ga, nrm2, gm, gat = up_back(0, grad, gu, out0)
    d = attend_back(head0, lse0, gm)
    order.meet(ffn0)
    *g, scores[0] = qkv_grads(head0, out0, d, gat)
    qo0 = Chain(reduce_stages(*g))
    grad, low, nrm1 = qkv_back(0, ga, d, residual, head0)
    norms[0] = jnp.concatenate([nrm1[0:1], nrm2[0:1], nrm1[1:2], nrm2[1:2]])
    nrm = jnp.concatenate(norms).reshape(8, 8, 2, ROWS)
    mine, theirs = (lax.dynamic_index_in_dim(nrm, b, 2, keepdims=False) for b in (c, 1 - c))
    nrm = jnp.moveaxis(mine + over_core(theirs), 0, 2)
    nrm = jnp.take(nrm, zx ^ jnp.array([0, 2, 4, 6, 1, 3, 5, 7], jnp.int32), axis=0)
    nrm = nrm.reshape(2, 4, ROWS, 8)
    lanes = [jnp.concatenate([s[..., :6], s[..., 64:70]], -1) for s in scores] + [nrm]
    lanes = jnp.pad(jnp.concatenate(lanes, -1), ((0, 0), (0, 0), (0, 0), (0, 96)))
    lanes = Chain(small_stages(lanes))
    token_grad = turn(low)
    order.meet(ffn0, qo0, lanes)
    order.meet(ffn0, qo0, lanes)
    order.meet(qo0)
    token_grad = order.passed(token_grad).astype(F32)
    lanes = order.after(lanes.result)
    score_grad = jnp.stack([lanes[:, 0:12], lanes[:, 12:24]])
    nrm = lanes[:, 24:32].T.reshape(LAYERS, 2, 2, ROWS)
    grads1 = grads1.astype(F32)
    qo = [qo0.result[:, 0], grads1[:, 0]]
    qkv_grad = jnp.stack([jnp.concatenate([v[0], v[1, :, :HALF]], 1) for v in qo])
    out_grad = jnp.stack([v[1, :, HALF:] for v in qo])
    ffn = [ffn0.result, grads1[:, 1:]]
    up_grad = jnp.stack([jnp.concatenate([v[0, 0], v[1, 0]], 1) for v in ffn])
    down_grad = jnp.stack(
        [v[:, 1].reshape(2, ROWS, 2, HALF).swapaxes(1, 2).reshape(DROWS, HALF) for v in ffn]
    )
    return (
        block_output[None],
        token_grad[None],
        qkv_grad,
        score_grad,
        out_grad,
        up_grad,
        down_grad,
        nrm[:, 0],
        nrm[:, 1],
    )


def solution(mesh):
    in_specs = (
        P("fsdp", "ctx", None),
        P("fsdp", "ctx", None),
        P("fsdp", None, None),
        P("fsdp", None),
        P(None, "fsdp", "ctx"),
        P(None, "fsdp", None),
        P(None, "fsdp", "ctx"),
        P(None, "fsdp", "ctx"),
        P(None, "fsdp", "ctx"),
        P(None, None, "fsdp"),
        P(None, None, "fsdp"),
    )
    out_specs = (
        P("fsdp", "ctx", None),
        P("fsdp", "ctx", None),
        P(None, "fsdp", "ctx"),
        P(None, "fsdp", None),
        P(None, "fsdp", "ctx"),
        P(None, "fsdp", "ctx"),
        P(None, "fsdp", "ctx"),
        P(None, None, "fsdp"),
        P(None, None, "fsdp"),
    )
    step = per_device
    if mesh.shape["fsdp"] == 16 and mesh.shape["ctx"] == 2:
        step = pair_device
        mesh = Mesh(mesh.devices.reshape(8, 2, 2), ("zx", "core", "ctx"))
        in_specs, out_specs = (
            tuple(P(*(("zx", "core") if a == "fsdp" else a for a in spec)) for spec in specs)
            for specs in (in_specs, out_specs)
        )
    return jax.shard_map(
        step, mesh=mesh, in_specs=in_specs, out_specs=out_specs, check_vma=False
    )
```
